32 devices in a mesh: section: 2 (over x), dp: 4 (over y, core), tensor: 4 (over z).
Axes of the slice: x: 2, y: 2, z: 4, core: 2. Of those that a mesh axis runs over, the one named last changes fastest.
Arguments:
- block_input: bfloat16 [2, 4, 256, 1024], P(None, 'dp', 'tensor'), may hold values from -6 to 6
- seq_ids: int32 [2, 4, 256], P(None, 'dp'), may hold values from 0 to 7, never falling along the last dimension, each value on 1 to 192 neighbouring positions
- out_cotangent: bfloat16 [2, 4, 256, 1024], P(None, 'dp', 'tensor'), may hold values from -6 to 6
- qkv_weight: bfloat16 [2, 1024, 3, 1024], P('section', 'dp', None, 'tensor'), may hold values from -0.1875 to 0.1875
- qv_bias: bfloat16 [2, 2, 16, 64], P('section', None, 'tensor', 'dp'), may hold values from -3 to 3
- out_weight: bfloat16 [2, 1024, 1024], P('section', 'tensor', 'dp'), may hold values from -0.5 to 0.5
- out_bias: bfloat16 [2, 1024], P('section', 'dp'), may hold values from -3 to 3
- norm1_gain: bfloat16 [2, 1024], P('section', 'dp'), may hold values from 0.25 to 1.75
- norm1_bias: bfloat16 [2, 1024], P('section', 'dp'), may hold values from -3 to 3
- up_weight: bfloat16 [2, 1024, 4096], P('section', 'dp', 'tensor'), may hold values from -0.1875 to 0.1875
- up_bias: bfloat16 [2, 16, 256], P('section', 'tensor', 'dp'), may hold values from -3 to 3
- down_weight: bfloat16 [2, 4096, 1024], P('section', 'tensor', 'dp'), may hold values from -0.09375 to 0.09375
- down_bias: bfloat16 [2, 1024], P('section', 'dp'), may hold values from -3 to 3
- norm2_gain: bfloat16 [2, 1024], P('section', 'dp'), may hold values from 0.25 to 1.75
- norm2_bias: bfloat16 [2, 1024], P('section', 'dp'), may hold values from -3 to 3
Outputs:
- section_outputs: bfloat16 [2, 2, 4, 256, 1024], P('section', None, 'dp', 'tensor')
- input_grads: float32 [2, 2, 4, 256, 1024], P('section', None, 'dp', 'tensor')
- qkv_weight_grad: float32 [2, 1024, 3, 1024], P('section', 'dp', None, 'tensor')
- qv_bias_grad: float32 [2, 2, 16, 64], P('section', None, 'tensor', 'dp')
- out_weight_grad: float32 [2, 1024, 1024], P('section', 'tensor', 'dp')
- out_bias_grad: float32 [2, 1024], P('section', ('dp', 'tensor'))
- norm1_gain_grad: float32 [2, 1024], P('section', ('dp', 'tensor'))
- norm1_bias_grad: float32 [2, 1024], P('section', ('dp', 'tensor'))
- up_weight_grad: float32 [2, 1024, 4096], P('section', 'dp', 'tensor')
- up_bias_grad: float32 [2, 16, 256], P('section', 'tensor', 'dp')
- down_weight_grad: float32 [2, 4096, 1024], P('section', 'tensor', 'dp')
- down_bias_grad: float32 [2, 1024], P('section', ('dp', 'tensor'))
- norm2_gain_grad: float32 [2, 1024], P('section', ('dp', 'tensor'))
- norm2_bias_grad: float32 [2, 1024], P('section', ('dp', 'tensor'))
The draws below stay inside these ranges and needn't reach their ends.
Inputs may be any that keep to these rules, and one draw needn't show every extreme that they name: `seq_ids`: along each pack of 256 tokens the ids never fall; every sequence has 1 to 192 tokens and one of each pack has exactly 192.
All inputs are finite; a program needn't handle non-finite values.
Results may differ from the reference program's by a relative error of at most 0.029.
Values may be sent and summed in bfloat16 or wider, within the bound.
A program may use at most 128 MiB of HBM per device.

```python
import math
import jax
import jax.numpy as jnp
import numpy as np
from jax import lax

D = 1024
FF = 4096
H = 16
HD = 64
MB = 2
TOK_MB = 256
PACKS = 4
SEQ_MAX = 192
SEQS = 8


def level_of(key, shape, shards, smallest, high):
    factor_of = 1.0
    for axis_at, parts in shards:
        steps = jax.random.uniform(jax.random.fold_in(jax.random.fold_in(key, 6), axis_at), (parts,), jnp.float32, smallest / len(shards), high / len(shards))
        factor_of = factor_of * jnp.repeat(jnp.exp(steps), shape[axis_at] // parts).reshape((-1,) + (1,) * (len(shape) - 1 - axis_at))
    return factor_of


def length_profile(amount, total, limit, lean):
    weights = [(1 << 20) // math.isqrt(grade ** lean) + 1 for grade in range(2, amount + 1)]
    spare, given = total - limit - (amount - 1), [1] * (amount - 1)
    while spare > 0:
        movable = [i for i in range(amount - 1) if given[i] < limit]
        pool, budget = sum([weights[i] for i in movable]), spare
        for i in movable:
            more = min(limit - given[i], max(1, budget * weights[i] // pool), spare)
            given[i] = given[i] + more
            spare = spare - more
    return np.array([limit] + given)


def ragged(own_key, amount, total, bound, skew):
    if amount == 2:
        one = jax.random.randint(own_key, (), max(1, total - bound), min(bound, total - 1) + 1)
        return jnp.stack([one, total - one])
    sizes = jnp.asarray(length_profile(amount, total, bound, skew), jnp.int32)
    twos = (amount - 1) // 2
    giver, sink = sizes[1:1 + 2 * twos:2], sizes[2:2 + 2 * twos:2]
    room = jnp.minimum(giver - 1, bound - sink)
    moved = jax.random.randint(jax.random.fold_in(own_key, 1), (twos,), 0, 1 << 20) % (room + 1)
    sizes = sizes.at[1:1 + 2 * twos:2].set(giver - moved).at[2:2 + 2 * twos:2].set(sink + moved)
    return sizes[jax.random.permutation(jax.random.fold_in(own_key, 2), amount)]


def noise(own_key, dims, scale, limit, split=(), kind=jnp.bfloat16):
    entries = scale * jax.random.normal(own_key, dims, jnp.float32)
    if split:
        entries = entries * level_of(own_key, dims, split, -0.22, 0.18)
    return jnp.clip(entries, -limit, limit).astype(kind)


def setup_inputs(seed: int = 0) -> dict:
    key_of = jax.random.split(jax.random.key(seed), 16)
    block_input = noise(key_of[0], (MB, PACKS, TOK_MB, D), 1.0, 6.0, ((1, 4), (2, 4)))
    seq_ids = jax.vmap(lambda own: jnp.searchsorted(jnp.cumsum(ragged(own, SEQS, TOK_MB, SEQ_MAX, 2)), jnp.arange(TOK_MB), side="right"))(jax.random.split(key_of[1], MB * PACKS)).reshape((MB, PACKS, TOK_MB)).astype(jnp.int32)
    out_cotangent = noise(key_of[2], (MB, PACKS, TOK_MB, D), 1.0, 6.0, ((1, 4), (2, 4)))
    qkv_weight = noise(key_of[3], (2, D, 3, D), D ** -0.5, 0.1875, ((0, 2), (1, 4), (3, 4)))
    qv_bias = noise(key_of[4], (2, 2, H, HD), 0.5, 3.0, ((0, 2), (2, 4), (3, 4)))
    out_weight = noise(key_of[5], (2, D, D), (D // 8) ** -0.5, 0.5, ((0, 2), (1, 4), (2, 4)))
    out_bias = noise(key_of[6], (2, D), 0.5, 3.0, ((0, 2), (1, 4)))
    norm1_gain = jnp.clip(1.0 + 0.15 * jax.random.normal(key_of[7], (2, D), jnp.float32), 0.25, 1.75).astype(jnp.bfloat16)
    norm1_bias = noise(key_of[8], (2, D), 0.5, 3.0, ((0, 2), (1, 4)))
    up_weight = noise(key_of[9], (2, D, FF), D ** -0.5, 0.1875, ((0, 2), (1, 4), (2, 4)))
    up_bias = noise(key_of[10], (2, 16, FF // 16), 0.5, 3.0, ((0, 2), (1, 4), (2, 4)))
    down_weight = noise(key_of[11], (2, FF, D), FF ** -0.5, 0.09375, ((0, 2), (1, 4), (2, 4)))
    down_bias = noise(key_of[12], (2, D), 0.5, 3.0, ((0, 2), (1, 4)))
    norm2_gain = jnp.clip(1.0 + 0.15 * jax.random.normal(key_of[13], (2, D), jnp.float32), 0.25, 1.75).astype(jnp.bfloat16)
    norm2_bias = noise(key_of[14], (2, D), 0.5, 3.0, ((0, 2), (1, 4)))
    return dict(block_input=block_input, seq_ids=seq_ids, out_cotangent=out_cotangent, qkv_weight=qkv_weight, qv_bias=qv_bias, out_weight=out_weight, out_bias=out_bias, norm1_gain=norm1_gain, norm1_bias=norm1_bias, up_weight=up_weight, up_bias=up_bias, down_weight=down_weight, down_bias=down_bias, norm2_gain=norm2_gain, norm2_bias=norm2_bias)


def gelu_exact(values):
    return 0.5 * values * (1.0 + jax.scipy.special.erf(values * 0.7071067811865476))

def gelu_slope(values):
    return 0.5 * (1.0 + jax.scipy.special.erf(values * 0.7071067811865476)) + values * jnp.exp(-0.5 * values * values) * 0.3989422804014327

def to_wide(values):
    return lax.optimization_barrier(values.astype(jnp.bfloat16)).astype(jnp.float32)

def normalize(summed):
    center = summed - lax.optimization_barrier(jnp.mean(summed, axis=-1, keepdims=True))
    scaled = lax.rsqrt(lax.optimization_barrier(jnp.mean(center * center, axis=-1, keepdims=True)) + 1e-12)
    return (center * scaled, scaled)

def norm_back(upstream, normed, scaled):
    return scaled * (upstream - lax.optimization_barrier(jnp.mean(upstream, axis=-1, keepdims=True)) - normed * lax.optimization_barrier(jnp.mean(upstream * normed, axis=-1, keepdims=True)))

def masked_probs(queries, keys, same_seq):
    scores = jnp.einsum('qhd,khd->hqk', queries, keys) * HD ** (-0.5)
    scores = jnp.where(same_seq[None], scores, -jnp.inf)
    largest = lax.optimization_barrier(jnp.max(scores, axis=-1, keepdims=True))
    shifted = jnp.exp(scores - largest)
    return shifted / lax.optimization_barrier(jnp.sum(shifted, axis=-1, keepdims=True))

def layer_forward(inputs, same_seq, params):
    qkv_mat, qv_shift, out_mat, out_shift, gain_one, shift_one, up_mat, up_shift, down_mat, down_shift, gain_two, shift_two = params
    tokens = inputs.shape[0]
    inputs_wide = inputs.astype(jnp.float32)
    projected = jnp.einsum('tc,cjn->tjn', inputs_wide, qkv_mat.astype(jnp.float32))
    qv_wide = qv_shift.astype(jnp.float32).reshape(2, D)
    bias_rows = jnp.concatenate([qv_wide[0:1], jnp.zeros((1, D), jnp.float32), qv_wide[1:2]], axis=0)
    qkv_held = (projected + bias_rows[None]).astype(jnp.bfloat16)
    queries = qkv_held[:, 0].reshape(tokens, H, HD).astype(jnp.float32)
    keys = qkv_held[:, 1].reshape(tokens, H, HD).astype(jnp.float32)
    values = qkv_held[:, 2].reshape(tokens, H, HD).astype(jnp.float32)
    attn_prob = masked_probs(queries, keys, same_seq)
    context = jnp.einsum('hqk,khd->qhd', to_wide(attn_prob), values).reshape(tokens, D).astype(jnp.bfloat16)
    resid_one = inputs_wide + jnp.dot(context, out_mat, preferred_element_type=jnp.float32) + out_shift.astype(jnp.float32)
    normed_one, scaled_one = normalize(resid_one)
    hidden_one = normed_one * gain_one.astype(jnp.float32) + shift_one.astype(jnp.float32)
    hidden_held = hidden_one.astype(jnp.bfloat16)
    pre_act = jnp.dot(hidden_held, up_mat, preferred_element_type=jnp.float32) + up_shift.astype(jnp.float32).reshape(FF)
    activated = gelu_exact(pre_act).astype(jnp.bfloat16)
    resid_two = hidden_one + jnp.dot(activated, down_mat, preferred_element_type=jnp.float32) + down_shift.astype(jnp.float32)
    normed_two, scaled_two = normalize(resid_two)
    layer_out = (normed_two * gain_two.astype(jnp.float32) + shift_two.astype(jnp.float32)).astype(jnp.bfloat16)
    return (layer_out, (qkv_held, context, normed_one, scaled_one, hidden_held, pre_act, activated, normed_two, scaled_two))

def layer_backward(inputs, same_seq, params, saved, upstream):
    qkv_mat, qv_shift, out_mat, out_shift, gain_one, shift_one, up_mat, up_shift, down_mat, down_shift, gain_two, shift_two = params
    qkv_held, context, normed_one, scaled_one, hidden_held, pre_act, activated, normed_two, scaled_two = saved
    tokens = inputs.shape[0]
    queries = qkv_held[:, 0].reshape(tokens, H, HD).astype(jnp.float32)
    keys = qkv_held[:, 1].reshape(tokens, H, HD).astype(jnp.float32)
    values = qkv_held[:, 2].reshape(tokens, H, HD).astype(jnp.float32)
    grad_two = norm_back(upstream * gain_two.astype(jnp.float32), normed_two, scaled_two)
    grad_two_held = grad_two.astype(jnp.bfloat16)
    down_grad = jnp.dot(activated.T, grad_two_held, preferred_element_type=jnp.float32)
    grad_pre = jnp.dot(grad_two_held, down_mat.T, preferred_element_type=jnp.float32) * gelu_slope(pre_act)
    grad_pre_held = grad_pre.astype(jnp.bfloat16)
    up_grad = jnp.dot(hidden_held.T, grad_pre_held, preferred_element_type=jnp.float32)
    grad_hidden = grad_two + jnp.dot(grad_pre_held, up_mat.T, preferred_element_type=jnp.float32)
    grad_one = norm_back(grad_hidden * gain_one.astype(jnp.float32), normed_one, scaled_one)
    grad_one_held = grad_one.astype(jnp.bfloat16)
    out_grad = jnp.dot(context.T, grad_one_held, preferred_element_type=jnp.float32)
    grad_context = jnp.dot(grad_one_held, out_mat.T, preferred_element_type=jnp.float32).astype(jnp.bfloat16).reshape(tokens, H, HD).astype(jnp.float32)
    attn_prob = masked_probs(queries, keys, same_seq)
    grad_prob = jnp.einsum('qhd,khd->hqk', grad_context, values)
    row_dots = lax.optimization_barrier(jnp.sum(attn_prob * grad_prob, axis=-1, keepdims=True))
    grad_scores = to_wide(attn_prob * (grad_prob - row_dots) * HD ** (-0.5))
    grad_queries = jnp.einsum('hqk,khd->qhd', grad_scores, keys)
    grad_keys = jnp.einsum('hqk,qhd->khd', grad_scores, queries)
    grad_values = jnp.einsum('hqk,qhd->khd', to_wide(attn_prob), grad_context)
    qv_grad = jnp.stack([lax.optimization_barrier(jnp.sum(grad_queries, axis=0)), lax.optimization_barrier(jnp.sum(grad_values, axis=0))])
    grad_qkv = jnp.stack([grad_queries, grad_keys, grad_values], axis=1).reshape(tokens, 3, D).astype(jnp.bfloat16)
    qkv_grad = jnp.einsum('tc,tjn->cjn', inputs.astype(jnp.float32), grad_qkv.astype(jnp.float32))
    grad_inputs = grad_one + jnp.einsum('tjn,cjn->tc', grad_qkv.astype(jnp.float32), qkv_mat.astype(jnp.float32))
    row_grads = jnp.stack([lax.optimization_barrier(jnp.sum(grad_one, axis=0)), lax.optimization_barrier(jnp.sum(grad_hidden * normed_one, axis=0)), lax.optimization_barrier(jnp.sum(grad_hidden, axis=0)), lax.optimization_barrier(jnp.sum(grad_two, axis=0)), lax.optimization_barrier(jnp.sum(upstream * normed_two, axis=0)), lax.optimization_barrier(jnp.sum(upstream, axis=0))])
    up_shift_grad = lax.optimization_barrier(jnp.sum(grad_pre, axis=0)).reshape(16, FF // 16)
    return (grad_inputs, (qkv_grad, qv_grad, out_grad, up_grad, up_shift_grad, down_grad, row_grads))

def reference(block_input, seq_ids, out_cotangent, qkv_weight, qv_bias, out_weight, out_bias, norm1_gain, norm1_bias, up_weight, up_bias, down_weight, down_bias, norm2_gain, norm2_bias):

    def section_params(which):
        return (qkv_weight[which], qv_bias[which], out_weight[which], out_bias[which], norm1_gain[which], norm1_bias[which], up_weight[which], up_bias[which], down_weight[which], down_bias[which], norm2_gain[which], norm2_bias[which])
    first_params = section_params(0)
    second_params = section_params(1)
    pack_count = MB * PACKS
    inputs_all = block_input.reshape(pack_count, TOK_MB, D)
    ids_all = seq_ids.reshape(pack_count, TOK_MB)
    upstream_all = out_cotangent.reshape(pack_count, TOK_MB, D)
    grad_shapes = [(D, 3, D), (2, H, HD), (D, D), (D, FF), (16, FF // 16), (FF, D), (6, D)]
    initial = tuple((jnp.zeros((2,) + grad_shape, jnp.float32) for grad_shape in grad_shapes))

    def advance(totals, pack_item):
        inputs, pack_ids, upstream = pack_item
        same_seq = pack_ids[:, None] == pack_ids[None, :]
        middle, saved_first = layer_forward(inputs, same_seq, first_params)
        final_out, saved_second = layer_forward(middle, same_seq, second_params)
        grad_middle, from_second = layer_backward(middle, same_seq, second_params, saved_second, upstream.astype(jnp.float32))
        grad_inputs, from_first = layer_backward(inputs, same_seq, first_params, saved_first, grad_middle)
        totals = tuple((running + jnp.stack([early, later]) for running, early, later in zip(totals, from_first, from_second)))
        return (totals, (middle, final_out, grad_inputs, grad_middle))
    totals, (middles, finals, grad_firsts, grad_seconds) = lax.scan(advance, initial, (inputs_all, ids_all, upstream_all))
    section_outputs = jnp.stack([middles, finals]).reshape(2, MB, PACKS, TOK_MB, D)
    input_grads = jnp.stack([grad_firsts, grad_seconds]).reshape(2, MB, PACKS, TOK_MB, D)
    row_grads = totals[6]
    return (section_outputs, input_grads, totals[0], totals[1], totals[2], row_grads[:, 0], row_grads[:, 1], row_grads[:, 2], totals[3], totals[4], totals[5], row_grads[:, 3], row_grads[:, 4], row_grads[:, 5])
```

```python
import functools

import jax
import jax.numpy as jnp
from jax import lax
from jax.experimental import pallas as pl
from jax.experimental.pallas import tpu as pltpu
from jax.sharding import PartitionSpec as P

MESH = pl.DeviceIdType.MESH
F32 = jnp.float32
BF16 = jnp.bfloat16
VMEM_SPEC = pl.BlockSpec(memory_space=pltpu.VMEM)
ANY_SPEC = pl.BlockSpec(memory_space=pl.ANY)
VMEM_LIMIT = 63 * 1024 * 1024
CHUNK = 32
QUARTERS = 4
SLABS = 3
PIECES = SLABS * QUARTERS
STATS = 8
BLOCK = 256

ERF_TOP = (
    0.00022905065861350646,
    0.0034082910107109506,
    0.050955695062380861,
    0.18520832239976145,
    1.128379143519084,
)
ERF_BELOW = (
    -1.1791602954361697e-7,
    0.000023547966471313185,
    0.0010179625278914885,
    0.014070470171167667,
    0.11098505178285362,
    0.49746925110067538,
    1.0,
)


def erf(values):
    x = jnp.clip(values, -3.832506856900711, 3.832506856900711)
    square = x * x
    top = jnp.full_like(square, ERF_TOP[0])
    for term in ERF_TOP[1:]:
        top = top * square + term
    below = jnp.full_like(square, ERF_BELOW[0])
    for term in ERF_BELOW[1:]:
        below = below * square + term
    return x * top / below


def nn(a, b):
    return lax.dot_general(a, b, (((1,), (0,)), ((), ())), preferred_element_type=F32)


def nt(a, b):
    return lax.dot_general(a, b, (((1,), (1,)), ((), ())), preferred_element_type=F32)


def tn(a, b):
    return lax.dot_general(a, b, (((0,), (0,)), ((), ())), preferred_element_type=F32)


def loop(count, body):
    def one(index, carry):
        body(index)
        return carry

    lax.fori_loop(0, count, one, 0)


def span(index, size):
    return pl.ds(pl.multiple_of(index * size, size), size)


def mean(values):
    return jnp.mean(values, axis=-1, keepdims=True)


def normalize(summed):
    center = summed - mean(summed)
    scaled = lax.rsqrt(mean(center * center) + 1e-12)
    return center * scaled, scaled


def norm_back(upstream, normed, scaled):
    return scaled * (upstream - mean(upstream) - normed * mean(upstream * normed))


def low_bit(mask):
    return (mask & -mask).bit_length() - 1


class Layers:
    def __init__(self, sizes, refs):
        for name, ref in zip(sizes["names"], refs):
            setattr(self, name, ref)
        self.line = sizes["line"]
        self.dp_count = sizes["dp_count"]
        self.bits = self.dp_count.bit_length() - 1
        self.part = sizes["part"]
        self.width = sizes["width"]
        self.rows = sizes["rows"]
        self.tokens = self.line * self.rows
        self.model = sizes["model"]
        self.units = sizes["units"]
        self.heads = sizes["heads"]
        self.head_size = sizes["head_size"]
        self.chunks = self.tokens // CHUNK
        self.quarter = self.part // QUARTERS
        self.section = lax.axis_index("section")
        self.dp = lax.axis_index("dp")
        self.me = lax.axis_index("tensor")
        self.nears = self.me // (self.line // 2)
        self.fars = 1 - self.nears
        self.middle = jnp.logical_and(self.me > 0, self.me < self.line - 1)
        self.own_rows = span(self.me, self.rows)
        self.passes = 0


    def place(self, mask):
        dp = self.dp
        for bit in range(self.bits):
            if mask & (1 << bit):
                dp = dp + (1 << bit) * (1 - 2 * ((self.dp // (1 << bit)) % 2))
        return dp

    def neighbour(self, bit):
        return {"dp": self.place(1 << bit)}

    def across(self):
        return {"section": 1 - self.section}

    def line_peer(self, step):
        return lax.rem(self.me + step, self.line)

    def remote(self, src, dst, send_sem, recv_sem, device):
        return pltpu.make_async_remote_copy(
            src_ref=src,
            dst_ref=dst,
            send_sem=send_sem,
            recv_sem=recv_sem,
            device_id=device,
            device_id_type=MESH,
        )

    def greet(self):
        barrier = pltpu.get_barrier_semaphore()
        targets = [{"tensor": self.line_peer(step)} for step in range(1, self.line)]
        targets += [self.neighbour(bit) for bit in range(self.bits)] + [self.across()]
        for target in targets:
            pl.semaphore_signal(barrier, inc=1, device_id=target, device_id_type=MESH)
        pl.semaphore_wait(barrier, len(targets))


    def rows_copy(self, which, source, target, step):
        return self.remote(
            source.at[self.section],
            target.at[self.own_rows],
            self.rows_send.at[which, step - 1],
            self.rows_recv.at[which, step - 1],
            {"tensor": self.line_peer(step)},
        )

    def rows_local(self, which, source, target):
        return pltpu.make_async_copy(
            source.at[self.section], target.at[self.own_rows], self.rows_own.at[which]
        )

    def rows_start(self, which, source, target):
        for step in range(1, self.line):
            self.rows_copy(which, source, target, step).start()
        self.rows_local(which, source, target).start()

    def rows_wait(self, which, source, target):
        self.rows_local(which, source, target).wait()
        for step in range(1, self.line):
            self.rows_copy(which, source, target, step).wait_recv()


    def weight_slot(self, s, p, mask):
        if p is None:
            return self.small_all.at[s, self.place(mask)]
        return self.weights.at[s, p // QUARTERS, self.piece_rows(p, mask)]

    def piece_rows(self, p, mask):
        at = self.place(mask) * self.part + (p % QUARTERS) * self.quarter
        return pl.ds(pl.multiple_of(at, self.quarter), self.quarter)

    def weight_own(self, p):
        if p is None:
            return self.small
        return self.own.at[p // QUARTERS, span(p % QUARTERS, self.quarter)]

    def weight_copy(self, s, p, held, bit, own=False):
        number = PIECES if p is None else p
        mask = held | (1 << bit)
        return self.remote(
            self.weight_own(p) if own else self.weight_slot(s, p, held),
            self.weight_slot(s, p, held),
            self.weight_send.at[s, number, mask],
            self.weight_recv.at[s, number, mask],
            self.neighbour(bit),
        )

    def weight_arrival(self, s, p, mask):
        number = PIECES if p is None else p
        return self.remote(
            self.weight_slot(s, p, mask),
            self.weight_slot(s, p, mask),
            self.weight_send.at[s, number, mask],
            self.weight_recv.at[s, number, mask],
            self.neighbour(low_bit(mask)),
        )

    def weight_across(self, s, p):
        number = PIECES if p is None else p
        return self.remote(
            self.weight_own(p),
            self.weight_slot(s, p, 0),
            self.weight_send.at[s, number, 0],
            self.weight_recv.at[s, number, 0],
            self.across(),
        )

    def weight_forward(self, s, p, held, own=False):
        top = self.bits if held == 0 else low_bit(held)
        for bit in reversed(range(top)):
            self.weight_copy(s, p, held, bit, own).start()

    def weights_offer(self, s):
        @pl.when(self.section == s)
        def _():
            def offer(p):
                self.weight_across(s, p).start()
                self.weight_forward(s, p, 0, True)

            offer(None)
            loop(PIECES, offer)

    def weights_cross(self, s, p):
        @pl.when(self.section != s)
        def _():
            self.weight_across(s, p).wait_recv()
            self.weight_forward(s, p, 0)

    def weights_relay(self, s, p):
        masks = [mask for mask in range(2, self.dp_count, 2)]
        masks.sort(key=lambda mask: (-low_bit(mask & -mask), mask))
        for bit in reversed(range(1, self.bits)):
            for mask in range(self.dp_count):
                if mask and low_bit(mask) == bit:
                    self.weight_arrival(s, p, mask).wait_recv()
                    self.weight_forward(s, p, mask)

    def weights_land(self, s, p):
        for mask in range(1, self.dp_count, 2):
            self.weight_arrival(s, p, mask).wait_recv()

    def weights_sent(self, s, p):
        for mask in range(1, self.dp_count):
            held = mask & (mask - 1)
            self.weight_copy(s, p, held, low_bit(mask)).wait_send()

        @pl.when(self.section == s)
        def _():
            self.weight_across(s, p).wait_send()


    def grad_slot(self, s, p, mask):
        return self.grads.at[s, p // QUARTERS, self.piece_rows(p, mask)]

    def grad_landed(self, s, p, mask):
        at = mask * self.part + (p % QUARTERS) * self.quarter
        rows = pl.ds(pl.multiple_of(at, self.quarter), self.quarter)
        return self.landed.at[s, p // QUARTERS, rows]

    def grad_copy(self, s, p, mask):
        device = self.neighbour(low_bit(mask)) if mask else self.across()
        return self.remote(
            self.grad_slot(s, p, mask),
            self.grad_landed(s, p, mask),
            self.grad_send.at[s, p, mask],
            self.grad_recv.at[s, p, mask],
            device,
        )

    def grad_total(self, s, p, mask, last=False):
        total = self.grad_slot(s, p, mask)[...].astype(F32)
        for bit in range(low_bit(mask) if mask else self.bits):
            self.grad_copy(s, p, mask | (1 << bit)).wait_recv()
            total = total + self.grad_landed(s, p, mask | (1 << bit))[...].astype(F32)
        return total

    def grads_offer(self, s, p):
        for mask in range(1, self.dp_count, 2):
            self.grad_copy(s, p, mask).start()

    def grads_fold(self, s, p):
        for bit in range(1, self.bits):
            for mask in range(self.dp_count):
                if mask and low_bit(mask) == bit:
                    self.grad_slot(s, p, mask)[...] = self.grad_total(s, p, mask).astype(BF16)
                    self.grad_copy(s, p, mask).start()

    def grads_cross(self, s, p):
        @pl.when(self.section != s)
        def _():
            self.grad_slot(s, p, 0)[...] = self.grad_total(s, p, 0).astype(BF16)
            self.grad_copy(s, p, 0).start()

    def grads_end(self, s, p):
        @pl.when(self.section == s)
        def _():
            total = self.grad_total(s, p, 0)
            self.grad_copy(s, p, 0).wait_recv()
            total = total + self.grad_landed(s, p, 0)[...].astype(F32)
            self.grad_sums[p // QUARTERS, span(p % QUARTERS, self.quarter)] = total

    def grads_sent(self, s, p):
        for mask in range(1, self.dp_count):
            self.grad_copy(s, p, mask).wait_send()

        @pl.when(self.section != s)
        def _():
            self.grad_copy(s, p, 0).wait_send()


    def line_copy(self, half, side, chunk, target):
        rows = span(chunk, CHUNK)
        return self.remote(
            self.staged.at[side, rows],
            self.sums.at[half, side, rows],
            self.line_send.at[side, chunk],
            self.line_recv.at[half, side, chunk],
            {"tensor": target},
        )

    def line_sum(self, finish, tick):
        number = self.passes
        half = number % 2
        self.passes += 1
        near_target = self.me + 1 - 2 * self.nears
        far_target = self.me - 1 + 2 * self.nears

        def send(side, chunk, target):
            rows = span(chunk, CHUNK)
            if number > 0:
                self.line_copy(half, side, chunk, target).wait_send()
            total = self.partial[rows] + self.sums[half, side, rows].astype(F32)
            self.staged[side, rows] = total.astype(BF16)
            self.line_copy(half, side, chunk, target).start()

        def near(chunk):
            @pl.when(self.middle)
            def _():
                self.line_copy(half, self.nears, chunk, near_target).wait_recv()

            send(self.nears, chunk, near_target)

        ahead = jnp.where(self.middle, 2, self.chunks)
        loop(ahead, near)

        def body(chunk):
            @pl.when(chunk + ahead < self.chunks)
            def _():
                near(chunk + ahead)

            self.line_copy(half, self.fars, chunk, near_target).wait_recv()

            @pl.when(self.middle)
            def _():
                send(self.fars, chunk, far_target)

            rows = span(chunk, CHUNK)
            total = (
                self.partial[rows]
                + self.sums[half, 0, rows].astype(F32)
                + self.sums[half, 1, rows].astype(F32)
            )
            finish(rows, total)
            tick(chunk)

        loop(self.chunks, body)

    def line_sent(self):
        def one(chunk):
            self.line_copy(0, self.nears, chunk, self.me + 1 - 2 * self.nears).wait_send()

            @pl.when(self.middle)
            def _():
                self.line_copy(0, self.fars, chunk, self.me - 1 + 2 * self.nears).wait_send()

        loop(self.chunks, one)

    def clear(self):
        for half in range(2):
            for side, end in ((0, 0), (1, self.line - 1)):

                @pl.when(self.me == end)
                def _():
                    self.sums[half, side] = jnp.zeros(self.sums.shape[2:], BF16)

        self.stats[...] = jnp.zeros(self.stats.shape, F32)
        row = jnp.broadcast_to(self.ids[self.section], (self.tokens, self.tokens))
        self.hidden_pairs[...] = jnp.where(row == row.T, 0.0, -1e30)


    def param(self, s, row):
        return self.params[s, row : row + 1]

    def count_stat(self, s, row, values):
        folded = values.reshape(values.shape[0] // 8, 8, values.shape[1])
        self.stats[s, row] += jnp.sum(folded, axis=0)

    def attention(self, s):
        width = self.width
        for block in range(3):
            at = slice(block * width, (block + 1) * width)
            made = nn(self.inputs[s], self.weights[s, 0, :, at])
            if block != 1:
                low = 0 if block == 0 else width
                made = made + self.params[s, 6:7, low : low + width]
            self.qkv[s, :, at] = made.astype(BF16)
        contexts = []
        for head in range(self.heads):
            query, key, value = self.head_parts(s, head)
            scores = nt(query, key) * self.head_size ** (-0.5) + self.hidden_pairs[...]
            shifted = jnp.exp(scores - jnp.max(scores, axis=-1, keepdims=True))
            prob = shifted / jnp.sum(shifted, axis=-1, keepdims=True)
            prob = prob.astype(BF16)
            self.probs[s, head] = prob
            contexts.append(nn(prob, value).astype(BF16))
        self.context[s] = jnp.concatenate(contexts, axis=1)

        def project(block):
            at = span(block, BLOCK)
            self.partial[:, at] = nt(self.context[s], self.weights[s, 0, at, 3 * width :])

        loop(self.model // BLOCK, project)

    def head_parts(self, s, head):
        size = self.head_size
        low = head * size
        return [
            self.qkv[s, :, which * self.width + low : which * self.width + low + size]
            for which in range(3)
        ]

    def feed_up(self, s):
        def block_of(block):
            at = span(block, BLOCK)
            self.partial[:, at] = nn(self.hidden[s], self.weights[s, 1, :, at])

        loop(self.units // BLOCK, block_of)

        def gelu(step):
            rows = span(step, 16)
            pre = self.partial[rows] + self.param(s, 7)
            half = 0.5 * (1.0 + erf(pre * 0.7071067811865476))
            self.active[s, rows] = (pre * half).astype(BF16)
            bell = pre * jnp.exp(-0.5 * pre * pre) * 0.3989422804014327
            self.slope[s, rows] = (half + bell).astype(BF16)

        loop(self.tokens // 16, gelu)

    def feed_down(self, s):
        def block_of(block):
            at = span(block, BLOCK)
            self.partial[:, at] = nt(self.active[s], self.weights[s, 2, at])

        loop(self.model // BLOCK, block_of)

    def after_attention(self, s):
        def finish(rows, total):
            summed = self.inputs[s, rows].astype(F32) + total + self.param(s, 0)
            normed, scaled = normalize(summed)
            self.normed_one[s, rows] = normed.astype(BF16)
            self.scaled_one[s, rows] = jnp.broadcast_to(scaled, (CHUNK, 128))
            hidden = normed * self.param(s, 1) + self.param(s, 2)
            self.wide[rows] = hidden
            self.hidden[s, rows] = hidden.astype(BF16)

        return finish

    def after_feed(self, s):
        def finish(rows, total):
            summed = self.wide[rows] + total + self.param(s, 3)
            normed, scaled = normalize(summed)
            out = normed * self.param(s, 4) + self.param(s, 5)
            self.inputs[s + 1, rows] = out.astype(BF16)
            if s == 0:
                self.normed_two[rows] = normed.astype(BF16)
                self.scaled_two[rows] = jnp.broadcast_to(scaled, (CHUNK, 128))
            else:
                self.start_back(s, rows, self.grad_one_held[rows].astype(F32), normed, scaled)

        return finish

    def start_back(self, s, rows, upstream, normed, scaled):
        grad_two = norm_back(upstream * self.param(s, 4), normed, scaled)
        self.wide[rows] = grad_two
        self.grad_two_held[rows] = grad_two.astype(BF16)
        self.count_stat(s, 3, grad_two)
        self.count_stat(s, 4, upstream * normed)
        self.count_stat(s, 5, upstream)

    def feed_back(self, s):
        def block_of(block):
            at = span(block, BLOCK)
            self.partial[:, at] = nn(self.grad_two_held[...], self.weights[s, 2, :, at])

        loop(self.units // BLOCK, block_of)

        def slopes(step):
            rows = span(step, 16)
            grad_pre = self.partial[rows] * self.slope[s, rows].astype(F32)
            self.grad_pre[rows] = grad_pre.astype(BF16)
            self.count_stat(s, 7, grad_pre)

        loop(self.tokens // 16, slopes)

        def up_of(block):
            at = span(block, BLOCK)
            self.partial[:, at] = nt(self.grad_pre[...], self.weights[s, 1, at])

        loop(self.model // BLOCK, up_of)

    def after_feed_back(self, s):
        def finish(rows, total):
            grad_hidden = self.wide[rows] + total
            normed = self.normed_one[s, rows].astype(F32)
            scaled = self.scaled_one[s, rows][:, :1]
            grad_one = norm_back(grad_hidden * self.param(s, 1), normed, scaled)
            self.grad_wide[rows] = grad_one
            self.grad_one_held[rows] = grad_one.astype(BF16)
            self.count_stat(s, 0, grad_one)
            self.count_stat(s, 1, grad_hidden * normed)
            self.count_stat(s, 2, grad_hidden)

        return finish

    def feed_grads(self, s, step):
        cuts = self.chunks // 2
        block = step // 2
        size = self.model // cuts
        at = span(block, size)

        @pl.when(step % 2 == 0)
        def _():
            made = tn(self.grad_two_held[:, at], self.active[s])
            self.grads[s, 2, at] = made.astype(BF16)

        @pl.when(step % 2 == 1)
        def _():
            made = tn(self.hidden[s, :, at], self.grad_pre[...])
            self.grads[s, 1, at] = made.astype(BF16)

    def attention_grads(self, s, step):
        cuts = self.chunks // 2
        block = step // 2
        size = self.model // cuts
        at = span(block, size)

        @pl.when(step % 2 == 0)
        def _():
            made = tn(self.inputs[s, :, at], self.grad_qkv[...])
            self.grads[s, 0, at, : 3 * self.width] = made.astype(BF16)

        @pl.when(step % 2 == 1)
        def _():
            made = tn(self.grad_one_held[:, at], self.context[s])
            self.grads[s, 0, at, 3 * self.width :] = made.astype(BF16)

    def attention_back(self, s):
        width, size = self.width, self.head_size
        grad_context = nn(self.grad_one_held[...], self.weights[s, 0, :, 3 * width :])
        self.grad_context[...] = grad_context.astype(BF16)
        parts = [[], [], []]
        for head in range(self.heads):
            query, key, value = self.head_parts(s, head)
            above = self.grad_context[:, head * size : (head + 1) * size]
            held = self.probs[s, head]
            prob = held.astype(F32)
            grad_prob = nt(above, value)
            dots = jnp.sum(prob * grad_prob, axis=-1, keepdims=True)
            grad_scores = (prob * (grad_prob - dots) * size ** (-0.5)).astype(BF16)
            parts[0].append(nn(grad_scores, key))
            parts[1].append(tn(grad_scores, query))
            parts[2].append(tn(held, above))
        for which in range(3):
            made = jnp.concatenate(parts[which], axis=1)
            self.grad_qkv[:, which * width : (which + 1) * width] = made.astype(BF16)
            if which != 1:
                folded = jnp.sum(made.reshape(self.tokens // 8, 8, width), axis=0)
                low = 0 if which == 0 else width
                self.stats[s, 6, :, low : low + width] = folded

        def block_of(block):
            at = span(block, BLOCK)
            self.partial[:, at] = nt(self.grad_qkv[...], self.weights[s, 0, at, : 3 * width])

        loop(self.model // BLOCK, block_of)

    def after_attention_back(self, s):
        def finish(rows, total):
            upstream = self.grad_wide[rows] + total
            self.grad_wide[rows] = upstream
            if s == 1:
                normed = self.normed_two[rows].astype(F32)
                self.start_back(0, rows, upstream, normed, self.scaled_two[rows][:, :1])

        return finish


    def output_copy(self, s, local):
        source = self.inputs.at[s + 1, self.own_rows]
        target = self.outputs.at[self.section]
        if local:
            return pltpu.make_async_copy(source, target, self.out_sem.at[0])
        return self.remote(source, target, self.out_sem.at[1], self.out_sem.at[2], self.across())

    def output_start(self, s):
        for local in (True, False):

            @pl.when((self.section == s) if local else (self.section != s))
            def _():
                self.output_copy(s, local).start()

    def input_grad_copy(self):
        return self.remote(
            self.input_grad_staged,
            self.input_grad_landed,
            self.out_sem.at[3],
            self.out_sem.at[4],
            self.across(),
        )

    def input_grad_start(self, s):
        @pl.when(self.section == s)
        def _():
            self.input_grads[self.section] = self.grad_wide[self.own_rows]

        @pl.when(self.section != s)
        def _():
            self.input_grad_staged[...] = self.grad_wide[self.own_rows].astype(BF16)
            self.input_grad_copy().start()

    def outputs_end(self):
        self.output_copy(0, True).wait()
        self.output_copy(0, False).wait()
        self.input_grad_copy().wait()
        self.input_grads[1 - self.section] = self.input_grad_landed[...].astype(F32)


    def stat_copy(self, step):
        return self.remote(
            self.stat_sums.at[step],
            self.stat_landed.at[step],
            self.stat_sem.at[0, step],
            self.stat_sem.at[1, step],
            self.neighbour(step) if step < self.bits else self.across(),
        )

    def run(self):
        nothing = lambda step: None
        self.greet()
        self.rows_start(0, self.block_rows, self.inputs.at[0])
        mine = pl.ds(pl.multiple_of(self.dp * self.part, self.part), self.part)
        own_copies = [
            pltpu.make_async_copy(
                self.small, self.small_all.at[self.section, self.dp], self.own_sem.at[0]
            ),
            pltpu.make_async_copy(
                self.own,
                self.weights.at[self.section, pl.ds(0, SLABS), mine],
                self.own_sem.at[1],
            ),
        ]
        self.weights_offer(0)
        for copy in own_copies:
            copy.start()
        self.clear()
        for copy in own_copies:
            copy.wait()
        self.weights_cross(0, None)
        self.weights_relay(0, None)
        for p in range(QUARTERS + 1):
            if p < QUARTERS:
                self.weights_cross(0, p)
            if p > 0:
                self.weights_relay(0, p - 1)
        self.weights_land(0, None)
        loop(QUARTERS, functools.partial(self.weights_land, 0))
        self.params[0] = jnp.sum(self.small_all[0], axis=0)
        self.rows_wait(0, self.block_rows, self.inputs.at[0])
        self.rows_start(1, self.upstream_rows, self.grad_one_held)

        self.attention(0)

        def first_tick(step):
            self.weights_cross(0, QUARTERS + step)

            @pl.when(step > 0)
            def _():
                self.weights_relay(0, QUARTERS + step - 1)

        self.line_sum(self.after_attention(0), first_tick)
        self.weights_relay(0, PIECES - 1)
        self.weights_offer(1)
        loop(QUARTERS, lambda p: self.weights_land(0, QUARTERS + p))
        self.feed_up(0)
        loop(QUARTERS, lambda p: self.weights_land(0, 2 * QUARTERS + p))
        self.feed_down(0)

        def second_tick(step):
            @pl.when(step == 0)
            def _():
                self.weights_cross(1, None)

            @pl.when(step == 1)
            def _():
                self.weights_relay(1, None)

            self.weights_cross(1, step)

            @pl.when(step > 0)
            def _():
                self.weights_relay(1, step - 1)

        self.line_sum(self.after_feed(0), second_tick)
        self.output_start(0)
        self.weights_land(1, None)
        loop(QUARTERS, functools.partial(self.weights_land, 1))
        self.params[1] = jnp.sum(self.small_all[1], axis=0)

        self.attention(1)

        def third_tick(step):
            @pl.when(step < QUARTERS)
            def _():
                self.weights_cross(1, 2 * QUARTERS + step)

            @pl.when(step <= QUARTERS)
            def _():
                self.weights_relay(1, 2 * QUARTERS + step - 1)

        self.line_sum(self.after_attention(1), third_tick)
        loop(QUARTERS, lambda p: self.weights_land(1, QUARTERS + p))
        self.feed_up(1)
        loop(QUARTERS, lambda p: self.weights_land(1, 2 * QUARTERS + p))
        self.feed_down(1)
        self.rows_wait(1, self.upstream_rows, self.grad_one_held)
        self.line_sum(self.after_feed(1), nothing)
        self.output_start(1)

        def turn(order):
            return (SLABS - 1 - order // QUARTERS) * QUARTERS + order % QUARTERS

        def service(s, action, order):
            @pl.when(jnp.logical_and(order >= 0, order < PIECES))
            def _():
                action(s, turn(order))

        self.feed_back(1)
        self.line_sum(self.after_feed_back(1), functools.partial(self.feed_grads, 1))
        loop(2 * QUARTERS, lambda order: self.grads_offer(1, turn(order)))
        self.attention_back(1)

        def fourth_tick(step):
            self.attention_grads(1, step)
            service(1, self.grads_fold, step)
            service(1, self.grads_cross, step - 2)
            service(1, self.grads_end, step - 4)

        self.line_sum(self.after_attention_back(1), fourth_tick)
        loop(QUARTERS, lambda q: self.grads_offer(1, q))
        self.input_grad_start(1)
        self.feed_back(0)

        def fifth_tick(step):
            self.feed_grads(0, step)
            service(1, self.grads_fold, step + 8)
            service(1, self.grads_cross, step + 6)
            service(1, self.grads_end, step + 4)

        self.line_sum(self.after_feed_back(0), fifth_tick)
        loop(2 * QUARTERS, lambda order: self.grads_offer(0, turn(order)))
        self.attention_back(0)

        def sixth_tick(step):
            self.attention_grads(0, step)
            service(0, self.grads_fold, step)
            service(0, self.grads_cross, step - 2)
            service(0, self.grads_end, step - 4)

        self.line_sum(self.after_attention_back(0), sixth_tick)
        loop(QUARTERS, lambda q: self.grads_offer(0, q))
        self.input_grad_start(0)
        self.stat_sums[0] = jnp.sum(self.stats[...], axis=2)
        self.stat_copy(0).start()

        def last_tick(step):
            service(0, self.grads_fold, step + 8)
            service(0, self.grads_cross, step + 6)
            service(0, self.grads_end, step + 4)

        loop(8, last_tick)
        for step in range(self.bits + 1):
            self.stat_copy(step).wait_recv()
            self.stat_sums[step + 1] = self.stat_sums[step] + self.stat_landed[step]
            if step < self.bits:
                self.stat_copy(step + 1).start()
        self.small_sums[...] = self.stat_sums[self.bits + 1, self.section]
        self.outputs_end()

        for which, source, target in (
            (0, self.block_rows, self.inputs.at[0]),
            (1, self.upstream_rows, self.grad_one_held),
        ):
            for step in range(1, self.line):
                self.rows_copy(which, source, target, step).wait_send()
        self.line_sent()
        for s in range(2):
            self.weights_sent(s, None)
            loop(PIECES, functools.partial(self.weights_sent, s))
            loop(PIECES, functools.partial(self.grads_sent, s))
        for step in range(self.bits + 1):
            self.stat_copy(step).wait_send()


def layers_kernel(sizes, *refs):
    Layers(sizes, refs).run()


def both_layers(block_rows, upstream_rows, ids, own, small, sizes):
    line, dp_count, part = sizes["line"], sizes["dp_count"], sizes["part"]
    rows, width, model, units = sizes["rows"], sizes["width"], sizes["model"], sizes["units"]
    heads = sizes["heads"]
    tokens = line * rows
    chunks = tokens // CHUNK
    bits = dp_count.bit_length() - 1
    dma = pltpu.SemaphoreType.DMA
    vmem = pltpu.VMEM
    scratch = dict(
        inputs=vmem((3, tokens, model), BF16),
        weights=vmem((2, SLABS, model, units), BF16),
        grads=vmem((2, SLABS, model, units), BF16),
        landed=vmem((2, SLABS, model, units), BF16),
        small_all=vmem((2, dp_count, STATS, model), F32),
        params=vmem((2, STATS, model), F32),
        sums=vmem((2, 2, tokens, model), BF16),
        staged=vmem((2, tokens, model), BF16),
        partial=vmem((tokens, model), F32),
        wide=vmem((tokens, model), F32),
        grad_wide=vmem((tokens, model), F32),
        normed_one=vmem((2, tokens, model), BF16),
        normed_two=vmem((tokens, model), BF16),
        scaled_one=vmem((2, tokens, 128), F32),
        scaled_two=vmem((tokens, 128), F32),
        hidden=vmem((2, tokens, model), BF16),
        active=vmem((2, tokens, units), BF16),
        slope=vmem((2, tokens, units), BF16),
        qkv=vmem((2, tokens, 3 * width), BF16),
        probs=vmem((2, heads, tokens, tokens), BF16),
        context=vmem((2, tokens, width), BF16),
        grad_two_held=vmem((tokens, model), BF16),
        grad_one_held=vmem((tokens, model), BF16),
        grad_pre=vmem((tokens, units), BF16),
        grad_context=vmem((tokens, width), BF16),
        grad_qkv=vmem((tokens, 3 * width), BF16),
        hidden_pairs=vmem((tokens, tokens), F32),
        stats=vmem((2, STATS, 8, model), F32),
        stat_sums=vmem((bits + 2, 2, STATS, model), F32),
        stat_landed=vmem((bits + 1, 2, STATS, model), F32),
        input_grad_staged=vmem((rows, model), BF16),
        input_grad_landed=vmem((rows, model), BF16),
        rows_send=dma((2, line - 1)),
        rows_recv=dma((2, line - 1)),
        rows_own=dma((2,)),
        own_sem=dma((2,)),
        weight_send=dma((2, PIECES + 1, dp_count)),
        weight_recv=dma((2, PIECES + 1, dp_count)),
        grad_send=dma((2, PIECES, dp_count)),
        grad_recv=dma((2, PIECES, dp_count)),
        line_send=dma((2, chunks)),
        line_recv=dma((2, 2, chunks)),
        out_sem=dma((5,)),
        stat_sem=dma((2, bits + 1)),
    )
    names = ["block_rows", "upstream_rows", "ids", "own", "small"]
    names += ["outputs", "input_grads", "grad_sums", "small_sums"] + list(scratch)
    return pl.pallas_call(
        functools.partial(layers_kernel, dict(sizes, names=names)),
        out_shape=[
            jax.ShapeDtypeStruct((2, rows, model), BF16),
            jax.ShapeDtypeStruct((2, rows, model), F32),
            jax.ShapeDtypeStruct((SLABS, part, units), F32),
            jax.ShapeDtypeStruct((STATS, model), F32),
        ],
        in_specs=[ANY_SPEC, ANY_SPEC, VMEM_SPEC, ANY_SPEC, ANY_SPEC],
        out_specs=[VMEM_SPEC] * 4,
        scratch_shapes=list(scratch.values()),
        compiler_params=pltpu.CompilerParams(
            collective_id=1, has_side_effects=True, vmem_limit_bytes=VMEM_LIMIT
        ),
        name="both_layers",
    )(block_rows, upstream_rows, ids, own, small)


def shards(
    block_input,
    seq_ids,
    out_cotangent,
    qkv_weight,
    qv_bias,
    out_weight,
    out_bias,
    norm1_gain,
    norm1_bias,
    up_weight,
    up_bias,
    down_weight,
    down_bias,
    norm2_gain,
    norm2_bias,
):
    dp_count = lax.axis_size("dp")
    line = lax.axis_size("tensor")
    dp = lax.axis_index("dp")
    heads, head_part = qv_bias.shape[2], qv_bias.shape[3]
    groups, unit_part = up_bias.shape[1], up_bias.shape[2]
    part = out_bias.shape[1]
    width = qkv_weight.shape[3]
    model = block_input.shape[3]
    units = up_weight.shape[2]
    sizes = dict(
        line=line,
        dp_count=dp_count,
        part=part,
        width=width,
        rows=block_input.shape[2],
        model=model,
        units=units,
        heads=heads,
        head_size=head_part * dp_count,
    )
    first_slab = jnp.concatenate([qkv_weight[0].reshape(part, 3 * width), out_weight[0].T], axis=1)
    own = jnp.stack([first_slab, up_weight[0], down_weight[0].T])

    def spread(values, axis):
        wide = jnp.expand_dims(values.astype(F32), axis)
        here = lax.broadcasted_iota(jnp.int32, (dp_count,) + (1,) * (wide.ndim - 1 - axis), 0) == dp
        return jnp.where(here, wide, 0.0)

    small = jnp.concatenate(
        [
            spread(values[0], 0).reshape(1, model)
            for values in (out_bias, norm1_gain, norm1_bias, down_bias, norm2_gain, norm2_bias)
        ]
        + [
            jnp.pad(spread(qv_bias[0], 2).reshape(1, 2 * width), ((0, 0), (0, model - 2 * width))),
            spread(up_bias[0], 1).reshape(1, units),
        ],
        axis=0,
    )
    outputs, input_grads, grad_sums, small_sums = both_layers(
        block_input[:, 0], out_cotangent[:, 0], seq_ids, own, small, sizes
    )
    qkv_sum = grad_sums[0][:, : 3 * width].reshape(1, part, 3, width)
    out_sum = grad_sums[0][:, 3 * width :].T
    down_sum = grad_sums[2].T
    share = part // line
    at = dp * part + lax.axis_index("tensor") * share
    rows = lax.dynamic_slice(small_sums, (0, at), (6, share))
    qv_sum = small_sums[6, : 2 * width].reshape(2, heads, dp_count, head_part)
    qv_sum = lax.dynamic_index_in_dim(qv_sum, dp, 2, keepdims=False)
    up_shift = small_sums[7].reshape(groups, dp_count, unit_part)
    up_shift = lax.dynamic_index_in_dim(up_shift, dp, 1, keepdims=False)
    return (
        outputs[None, :, None],
        input_grads[None, :, None],
        qkv_sum,
        qv_sum[None],
        out_sum[None],
        rows[0][None],
        rows[1][None],
        rows[2][None],
        grad_sums[1][None],
        up_shift[None],
        down_sum[None],
        rows[3][None],
        rows[4][None],
        rows[5][None],
    )


def solution(mesh):
    return jax.shard_map(
        shards,
        mesh=mesh,
        in_specs=(
            P(None, "dp", "tensor", None),
            P(None, "dp", None),
            P(None, "dp", "tensor", None),
            P("section", "dp", None, "tensor"),
            P("section", None, "tensor", "dp"),
            P("section", "tensor", "dp"),
            P("section", "dp"),
            P("section", "dp"),
            P("section", "dp"),
            P("section", "dp", "tensor"),
            P("section", "tensor", "dp"),
            P("section", "tensor", "dp"),
            P("section", "dp"),
            P("section", "dp"),
            P("section", "dp"),
        ),
        out_specs=(
            P("section", None, "dp", "tensor", None),
            P("section", None, "dp", "tensor", None),
            P("section", "dp", None, "tensor"),
            P("section", None, "tensor", "dp"),
            P("section", "tensor", "dp"),
            P("section", ("dp", "tensor")),
            P("section", ("dp", "tensor")),
            P("section", ("dp", "tensor")),
            P("section", "dp", "tensor"),
            P("section", "tensor", "dp"),
            P("section", "tensor", "dp"),
            P("section", ("dp", "tensor")),
            P("section", ("dp", "tensor")),
            P("section", ("dp", "tensor")),
        ),
        check_vma=False,
    )
```

```python
import functools

import jax
import jax.numpy as jnp
from jax import lax
from jax.experimental import pallas as pl
from jax.experimental.pallas import tpu as pltpu
from jax.sharding import PartitionSpec as P

MESH = pl.DeviceIdType.MESH
F32 = jnp.float32
BF16 = jnp.bfloat16
VMEM_SPEC = pl.BlockSpec(memory_space=pltpu.VMEM)
ANY_SPEC = pl.BlockSpec(memory_space=pl.ANY)
VMEM_LIMIT = 63 * 1024 * 1024
CHUNK = 32
AHEAD = 5
QUARTERS = 4
SLABS = 3
PIECES = SLABS * QUARTERS
STATS = 8
BLOCK = 256
VECTORS = ("out_bias", "gain_one", "bias_one", "down_bias", "gain_two", "bias_two")

ERF_TOP = (
    0.00022905065861350646,
    0.0034082910107109506,
    0.050955695062380861,
    0.18520832239976145,
    1.128379143519084,
)
ERF_BELOW = (
    -1.1791602954361697e-7,
    0.000023547966471313185,
    0.0010179625278914885,
    0.014070470171167667,
    0.11098505178285362,
    0.49746925110067538,
    1.0,
)


def erf(values):
    x = jnp.clip(values, -3.832506856900711, 3.832506856900711)
    square = x * x
    top = jnp.full_like(square, ERF_TOP[0])
    for term in ERF_TOP[1:]:
        top = top * square + term
    below = jnp.full_like(square, ERF_BELOW[0])
    for term in ERF_BELOW[1:]:
        below = below * square + term
    return x * top / below


def nn(a, b):
    return lax.dot_general(a, b, (((1,), (0,)), ((), ())), preferred_element_type=F32)


def nt(a, b):
    return lax.dot_general(a, b, (((1,), (1,)), ((), ())), preferred_element_type=F32)


def tn(a, b):
    return lax.dot_general(a, b, (((0,), (0,)), ((), ())), preferred_element_type=F32)


def loop(count, body):
    def one(index, carry):
        body(index)
        return carry

    lax.fori_loop(0, count, one, 0)


def span(index, size):
    return pl.ds(pl.multiple_of(index * size, size), size)


def mean(values):
    return jnp.mean(values, axis=-1, keepdims=True)


def normalize(summed):
    center = summed - mean(summed)
    scaled = lax.rsqrt(mean(center * center) + 1e-12)
    return center * scaled, scaled


def norm_back(upstream, normed, scaled):
    return scaled * (upstream - mean(upstream) - normed * mean(upstream * normed))


def low_bit(mask):
    return (mask & -mask).bit_length() - 1


class Layers:
    def __init__(self, sizes, refs):
        for name, ref in zip(sizes["names"], refs):
            setattr(self, name, ref)
        self.vectors = [getattr(self, name) for name in VECTORS]
        self.line = sizes["line"]
        self.dp_count = sizes["dp_count"]
        self.bits = self.dp_count.bit_length() - 1
        self.part = sizes["part"]
        self.width = sizes["width"]
        self.rows = sizes["rows"]
        self.tokens = self.line * self.rows
        self.model = sizes["model"]
        self.units = sizes["units"]
        self.heads = sizes["heads"]
        self.head_size = sizes["head_size"]
        self.chunks = self.tokens // CHUNK
        self.quarter = self.part // QUARTERS
        self.section = lax.axis_index("section")
        self.dp = lax.axis_index("dp")
        self.me = lax.axis_index("tensor")
        self.nears = self.me // (self.line // 2)
        self.fars = 1 - self.nears
        self.middle = jnp.logical_and(self.me > 0, self.me < self.line - 1)
        self.own_rows = span(self.me, self.rows)
        self.passes = 0


    def place(self, mask):
        dp = self.dp
        for bit in range(self.bits):
            if mask & (1 << bit):
                dp = dp + (1 << bit) * (1 - 2 * ((self.dp // (1 << bit)) % 2))
        return dp

    def neighbour(self, bit):
        return {"dp": self.place(1 << bit)}

    def across(self):
        return {"section": 1 - self.section}

    def line_peer(self, step):
        return lax.rem(self.me + step, self.line)

    def remote(self, src, dst, send_sem, recv_sem, device):
        return pltpu.make_async_remote_copy(
            src_ref=src,
            dst_ref=dst,
            send_sem=send_sem,
            recv_sem=recv_sem,
            device_id=device,
            device_id_type=MESH,
        )

    def greet(self):
        barrier = pltpu.get_barrier_semaphore()
        targets = [{"tensor": self.line_peer(step)} for step in range(1, self.line)]
        targets += [self.neighbour(bit) for bit in range(self.bits)] + [self.across()]
        for target in targets:
            pl.semaphore_signal(barrier, inc=1, device_id=target, device_id_type=MESH)
        pl.semaphore_wait(barrier, len(targets))


    def rows_copy(self, which, source, target, step):
        return self.remote(
            source.at[self.section],
            target.at[self.own_rows],
            self.rows_send.at[which, step - 1],
            self.rows_recv.at[which, step - 1],
            {"tensor": self.line_peer(step)},
        )

    def rows_local(self, which, source, target):
        return pltpu.make_async_copy(
            source.at[self.section], target.at[self.own_rows], self.rows_own.at[which]
        )

    def rows_start(self, which, source, target):
        for step in range(1, self.line):
            self.rows_copy(which, source, target, step).start()
        self.rows_local(which, source, target).start()

    def rows_wait(self, which, source, target):
        self.rows_local(which, source, target).wait()
        for step in range(1, self.line):
            self.rows_copy(which, source, target, step).wait_recv()


    def weight_slot(self, s, p, mask):
        if p is None:
            return self.small_all.at[s, self.place(mask)]
        return self.weights.at[s, p // QUARTERS, self.piece_rows(p, mask)]

    def piece_rows(self, p, mask):
        at = self.place(mask) * self.part + (p % QUARTERS) * self.quarter
        return pl.ds(pl.multiple_of(at, self.quarter), self.quarter)

    def weight_copy(self, s, p, held, bit):
        number = PIECES if p is None else p
        mask = held | (1 << bit)
        return self.remote(
            self.weight_slot(s, p, held),
            self.weight_slot(s, p, held),
            self.weight_send.at[s, number, mask],
            self.weight_recv.at[s, number, mask],
            self.neighbour(bit),
        )

    def weight_arrival(self, s, p, mask):
        number = PIECES if p is None else p
        return self.remote(
            self.weight_slot(s, p, mask),
            self.weight_slot(s, p, mask),
            self.weight_send.at[s, number, mask],
            self.weight_recv.at[s, number, mask],
            self.neighbour(low_bit(mask)),
        )

    def weight_across(self, s, p):
        number = PIECES if p is None else p
        return self.remote(
            self.weight_slot(s, p, 0),
            self.weight_slot(s, p, 0),
            self.weight_send.at[s, number, 0],
            self.weight_recv.at[s, number, 0],
            self.across(),
        )

    def weight_forward(self, s, p, held):
        top = self.bits if held == 0 else low_bit(held)
        for bit in reversed(range(top)):
            self.weight_copy(s, p, held, bit).start()

    def weight_offer(self, s, p):
        self.weight_across(s, p).start()
        self.weight_forward(s, p, 0)

    def weights_offer(self, s, first, last):
        @pl.when(self.section == s)
        def _():
            loop(last - first, lambda p: self.weight_offer(s, first + p))

    def small_offer(self, s):
        @pl.when(self.section == s)
        def _():
            self.weight_offer(s, None)

    def weights_cross(self, s, p):
        @pl.when(self.section != s)
        def _():
            self.weight_across(s, p).wait_recv()
            self.weight_forward(s, p, 0)

    def weights_relay(self, s, p):
        for bit in reversed(range(1, self.bits)):
            for mask in range(self.dp_count):
                if mask and low_bit(mask) == bit:
                    self.weight_arrival(s, p, mask).wait_recv()
                    self.weight_forward(s, p, mask)

    def weights_land(self, s, p):
        for mask in range(1, self.dp_count, 2):
            self.weight_arrival(s, p, mask).wait_recv()

    def weights_sent(self, s, p):
        for mask in range(1, self.dp_count):
            held = mask & (mask - 1)
            self.weight_copy(s, p, held, low_bit(mask)).wait_send()

        @pl.when(self.section == s)
        def _():
            self.weight_across(s, p).wait_send()


    def grad_slot(self, s, p, mask):
        return self.grads.at[s, p // QUARTERS, self.piece_rows(p, mask)]

    def grad_landed(self, s, p, mask):
        at = mask * self.part + (p % QUARTERS) * self.quarter
        rows = pl.ds(pl.multiple_of(at, self.quarter), self.quarter)
        return self.landed.at[s, p // QUARTERS, rows]

    def grad_copy(self, s, p, mask):
        device = self.neighbour(low_bit(mask)) if mask else self.across()
        return self.remote(
            self.grad_slot(s, p, mask),
            self.grad_landed(s, p, mask),
            self.grad_send.at[s, p, mask],
            self.grad_recv.at[s, p, mask],
            device,
        )

    def grad_total(self, s, p, mask, last=False):
        total = self.grad_slot(s, p, mask)[...].astype(F32)
        for bit in range(low_bit(mask) if mask else self.bits):
            self.grad_copy(s, p, mask | (1 << bit)).wait_recv()
            total = total + self.grad_landed(s, p, mask | (1 << bit))[...].astype(F32)
        return total

    def grads_offer(self, s, p):
        for mask in range(1, self.dp_count, 2):
            self.grad_copy(s, p, mask).start()

    def grads_fold(self, s, p):
        for bit in range(1, self.bits):
            for mask in range(self.dp_count):
                if mask and low_bit(mask) == bit:
                    self.grad_slot(s, p, mask)[...] = self.grad_total(s, p, mask).astype(BF16)
                    self.grad_copy(s, p, mask).start()

    def grads_cross(self, s, p):
        @pl.when(self.section != s)
        def _():
            self.grad_slot(s, p, 0)[...] = self.grad_total(s, p, 0).astype(BF16)
            self.grad_copy(s, p, 0).start()

    def grads_end(self, s, p):
        @pl.when(self.section == s)
        def _():
            total = self.grad_total(s, p, 0)
            self.grad_copy(s, p, 0).wait_recv()
            total = total + self.grad_landed(s, p, 0)[...].astype(F32)
            rows = span(p % QUARTERS, self.quarter)
            slab = p // QUARTERS

            @pl.when(slab == 0)
            def _():
                for which in range(3):
                    at = slice(which * self.width, (which + 1) * self.width)
                    self.qkv_sums[which, rows] = total[:, at]
                self.out_turned[rows] = total[:, 3 * self.width :]

            @pl.when(slab == 1)
            def _():
                self.up_sums[rows] = total

            @pl.when(slab == 2)
            def _():
                self.down_turned[rows] = total

    def grads_sent(self, s, p):
        for mask in range(1, self.dp_count):
            self.grad_copy(s, p, mask).wait_send()

        @pl.when(self.section != s)
        def _():
            self.grad_copy(s, p, 0).wait_send()


    def line_copy(self, half, side, chunk, target):
        rows = span(chunk, CHUNK)
        return self.remote(
            self.staged.at[side, rows],
            self.sums.at[half, side, rows],
            self.line_send.at[side, chunk],
            self.line_recv.at[half, side, chunk],
            {"tensor": target},
        )

    def line_sum(self, finish, tick, early):
        number = self.passes
        half = number % 2
        self.passes += 1
        near_target = self.me + 1 - 2 * self.nears
        far_target = self.me - 1 + 2 * self.nears

        def send(side, chunk, target):
            rows = span(chunk, CHUNK)
            if number > 0:
                self.line_copy(half, side, chunk, target).wait_send()
            total = self.partial[rows] + self.sums[half, side, rows].astype(F32)
            self.staged[side, rows] = total.astype(BF16)
            self.line_copy(half, side, chunk, target).start()

        def near(chunk):
            @pl.when(self.middle)
            def _():
                self.line_copy(half, self.nears, chunk, near_target).wait_recv()

            send(self.nears, chunk, near_target)

        @pl.when(jnp.logical_not(self.middle))
        def _():
            loop(self.chunks, near)

        def ahead(chunk):
            @pl.when(self.middle)
            def _():
                near(chunk)

            early(chunk)

        loop(AHEAD, ahead)

        def body(chunk):
            @pl.when(jnp.logical_and(self.middle, chunk + AHEAD < self.chunks))
            def _():
                near(chunk + AHEAD)

            self.line_copy(half, self.fars, chunk, near_target).wait_recv()

            @pl.when(self.middle)
            def _():
                send(self.fars, chunk, far_target)

            rows = span(chunk, CHUNK)
            total = (
                self.partial[rows]
                + self.sums[half, 0, rows].astype(F32)
                + self.sums[half, 1, rows].astype(F32)
            )
            finish(rows, total)
            tick(chunk)

        loop(self.chunks, body)

    def line_sent(self):
        def one(chunk):
            self.line_copy(0, self.nears, chunk, self.me + 1 - 2 * self.nears).wait_send()

            @pl.when(self.middle)
            def _():
                self.line_copy(0, self.fars, chunk, self.me - 1 + 2 * self.nears).wait_send()

        loop(self.chunks, one)

    def clear(self):
        for half in range(2):
            for side, end in ((0, 0), (1, self.line - 1)):

                @pl.when(self.me == end)
                def _():
                    self.sums[half, side] = jnp.zeros(self.sums.shape[2:], BF16)

        self.stats[...] = jnp.zeros(self.stats.shape, F32)
        row = jnp.broadcast_to(self.ids[self.section], (self.tokens, self.tokens))
        self.hidden_pairs[...] = jnp.where(row == row.T, 0.0, -1e30)


    def param(self, s, row):
        return self.params[s, row : row + 1]

    def count_stat(self, s, row, values):
        folded = values.reshape(values.shape[0] // 8, 8, values.shape[1])
        self.stats[s, row] += jnp.sum(folded, axis=0)

    def attention(self, s):
        width = self.width
        for block in range(3):
            at = slice(block * width, (block + 1) * width)
            made = nn(self.inputs[s], self.weights[s, 0, :, at])
            if block != 1:
                low = 0 if block == 0 else width
                made = made + self.params[s, 6:7, low : low + width]
            self.qkv[s, :, at] = made.astype(BF16)
        contexts = []
        for head in range(self.heads):
            query, key, value = self.head_parts(s, head)
            scores = nt(query, key) * self.head_size ** (-0.5) + self.hidden_pairs[...]
            shifted = jnp.exp(scores - jnp.max(scores, axis=-1, keepdims=True))
            prob = shifted / jnp.sum(shifted, axis=-1, keepdims=True)
            prob = prob.astype(BF16)
            self.probs[s, head] = prob
            contexts.append(nn(prob, value).astype(BF16))
        self.context[s] = jnp.concatenate(contexts, axis=1)

        def project(block):
            at = span(block, BLOCK)
            self.partial[:, at] = nt(self.context[s], self.weights[s, 0, at, 3 * width :])

        loop(self.model // BLOCK, project)

    def head_parts(self, s, head):
        size = self.head_size
        low = head * size
        return [
            self.qkv[s, :, which * self.width + low : which * self.width + low + size]
            for which in range(3)
        ]

    def feed_up(self, s):
        def block_of(block):
            at = span(block, BLOCK)
            self.partial[:, at] = nn(self.hidden[s], self.weights[s, 1, :, at])

        loop(self.units // BLOCK, block_of)

        def gelu(step):
            rows = span(step, 16)
            pre = self.partial[rows] + self.param(s, 7)
            half = 0.5 * (1.0 + erf(pre * 0.7071067811865476))
            self.active[s, rows] = (pre * half).astype(BF16)
            bell = pre * jnp.exp(-0.5 * pre * pre) * 0.3989422804014327
            self.slope[s, rows] = (half + bell).astype(BF16)

        loop(self.tokens // 16, gelu)

    def feed_down(self, s):
        def block_of(block):
            at = span(block, BLOCK)
            self.partial[:, at] = nt(self.active[s], self.weights[s, 2, at])

        loop(self.model // BLOCK, block_of)

    def after_attention(self, s):
        def finish(rows, total):
            summed = self.inputs[s, rows].astype(F32) + total + self.param(s, 0)
            normed, scaled = normalize(summed)
            self.normed_one[s, rows] = normed.astype(BF16)
            self.scaled_one[s, rows] = jnp.broadcast_to(scaled, (CHUNK, 128))
            hidden = normed * self.param(s, 1) + self.param(s, 2)
            self.wide[rows] = hidden
            self.hidden[s, rows] = hidden.astype(BF16)

        return finish

    def after_feed(self, s):
        def finish(rows, total):
            summed = self.wide[rows] + total + self.param(s, 3)
            normed, scaled = normalize(summed)
            out = normed * self.param(s, 4) + self.param(s, 5)
            self.inputs[s + 1, rows] = out.astype(BF16)
            if s == 0:
                self.normed_two[rows] = normed.astype(BF16)
                self.scaled_two[rows] = jnp.broadcast_to(scaled, (CHUNK, 128))
            else:
                self.start_back(s, rows, self.grad_one_held[rows].astype(F32), normed, scaled)

        return finish

    def start_back(self, s, rows, upstream, normed, scaled):
        grad_two = norm_back(upstream * self.param(s, 4), normed, scaled)
        self.wide[rows] = grad_two
        self.grad_two_held[rows] = grad_two.astype(BF16)
        self.count_stat(s, 3, grad_two)
        self.count_stat(s, 4, upstream * normed)
        self.count_stat(s, 5, upstream)

    def feed_back(self, s):
        def block_of(block):
            at = span(block, BLOCK)
            self.partial[:, at] = nn(self.grad_two_held[...], self.weights[s, 2, :, at])

        loop(self.units // BLOCK, block_of)

        def slopes(step):
            rows = span(step, 16)
            grad_pre = self.partial[rows] * self.slope[s, rows].astype(F32)
            self.grad_pre[rows] = grad_pre.astype(BF16)
            self.count_stat(s, 7, grad_pre)

        loop(self.tokens // 16, slopes)

        def up_of(block):
            at = span(block, BLOCK)
            self.partial[:, at] = nt(self.grad_pre[...], self.weights[s, 1, at])

        loop(self.model // BLOCK, up_of)

    def after_feed_back(self, s):
        def finish(rows, total):
            grad_hidden = self.wide[rows] + total
            normed = self.normed_one[s, rows].astype(F32)
            scaled = self.scaled_one[s, rows][:, :1]
            grad_one = norm_back(grad_hidden * self.param(s, 1), normed, scaled)
            self.grad_wide[rows] = grad_one
            self.grad_one_held[rows] = grad_one.astype(BF16)
            self.count_stat(s, 0, grad_one)
            self.count_stat(s, 1, grad_hidden * normed)
            self.count_stat(s, 2, grad_hidden)

        return finish

    def feed_grads(self, s, block):
        at = span(block, BLOCK)
        made = tn(self.grad_two_held[:, at], self.active[s])
        self.grads[s, 2, at] = made.astype(BF16)
        made = tn(self.hidden[s, :, at], self.grad_pre[...])
        self.grads[s, 1, at] = made.astype(BF16)

    def attention_grads(self, s, block):
        at = span(block, BLOCK)
        made = tn(self.inputs[s, :, at], self.grad_qkv[...])
        self.grads[s, 0, at, : 3 * self.width] = made.astype(BF16)
        made = tn(self.grad_one_held[:, at], self.context[s])
        self.grads[s, 0, at, 3 * self.width :] = made.astype(BF16)

    def attention_back(self, s):
        width, size = self.width, self.head_size
        grad_context = nn(self.grad_one_held[...], self.weights[s, 0, :, 3 * width :])
        self.grad_context[...] = grad_context.astype(BF16)
        parts = [[], [], []]
        for head in range(self.heads):
            query, key, value = self.head_parts(s, head)
            above = self.grad_context[:, head * size : (head + 1) * size]
            held = self.probs[s, head]
            prob = held.astype(F32)
            grad_prob = nt(above, value)
            dots = jnp.sum(prob * grad_prob, axis=-1, keepdims=True)
            grad_scores = (prob * (grad_prob - dots) * size ** (-0.5)).astype(BF16)
            parts[0].append(nn(grad_scores, key))
            parts[1].append(tn(grad_scores, query))
            parts[2].append(tn(held, above))
        for which in range(3):
            made = jnp.concatenate(parts[which], axis=1)
            self.grad_qkv[:, which * width : (which + 1) * width] = made.astype(BF16)
            if which != 1:
                folded = jnp.sum(made.reshape(self.tokens // 8, 8, width), axis=0)
                low = 0 if which == 0 else width
                self.stats[s, 6, :, low : low + width] = folded

        def block_of(block):
            at = span(block, BLOCK)
            self.partial[:, at] = nt(self.grad_qkv[...], self.weights[s, 0, at, : 3 * width])

        loop(self.model // BLOCK, block_of)

    def after_attention_back(self, s):
        def finish(rows, total):
            upstream = self.grad_wide[rows] + total
            self.grad_wide[rows] = upstream
            if s == 1:
                normed = self.normed_two[rows].astype(F32)
                self.start_back(0, rows, upstream, normed, self.scaled_two[rows][:, :1])

        return finish


    def output_copy(self, s, local):
        source = self.inputs.at[s + 1, self.own_rows]
        target = self.outputs.at[self.section]
        if local:
            return pltpu.make_async_copy(source, target, self.out_sem.at[0])
        return self.remote(source, target, self.out_sem.at[1], self.out_sem.at[2], self.across())

    def output_start(self, s):
        for local in (True, False):

            @pl.when((self.section == s) if local else (self.section != s))
            def _():
                self.output_copy(s, local).start()

    def input_grad_copy(self):
        return self.remote(
            self.input_grad_staged,
            self.input_grad_landed,
            self.out_sem.at[3],
            self.out_sem.at[4],
            self.across(),
        )

    def input_grad_start(self, s):
        @pl.when(self.section == s)
        def _():
            self.input_grads[self.section] = self.grad_wide[self.own_rows]

        @pl.when(self.section != s)
        def _():
            self.input_grad_staged[...] = self.grad_wide[self.own_rows].astype(BF16)
            self.input_grad_copy().start()

    def outputs_end(self):
        self.output_copy(0, True).wait()
        self.output_copy(0, False).wait()
        self.input_grad_copy().wait()
        self.input_grads[1 - self.section] = self.input_grad_landed[...].astype(F32)


    def stat_copy(self, step):
        return self.remote(
            self.stat_sums.at[step],
            self.stat_landed.at[step],
            self.stat_sem.at[0, step],
            self.stat_sem.at[1, step],
            self.neighbour(step) if step < self.bits else self.across(),
        )

    def stat_step(self, step):
        self.stat_copy(step).wait_recv()
        self.stat_sums[step + 1] = self.stat_sums[step] + self.stat_landed[step]
        if step < self.bits:
            self.stat_copy(step + 1).start()


    def spread_small(self):
        model, dp_count = self.model, self.dp_count
        place = lax.broadcasted_iota(jnp.int32, (1, model), 1) // self.part
        rows = []
        for ref in self.vectors:
            tiled = jnp.concatenate([ref[...].astype(F32)] * dp_count, axis=1)
            rows.append(jnp.where(place == self.dp, tiled, 0.0))

        def spread(values):
            size = values.shape[1]
            shape = (size, size * dp_count)
            low = lax.broadcasted_iota(jnp.int32, shape, 0) + self.dp * size
            chosen = jnp.where(lax.broadcasted_iota(jnp.int32, shape, 1) == low, 1.0, 0.0)
            return nn(values.astype(BF16), chosen.astype(BF16))

        query, value = spread(self.qv_bias[0]), spread(self.qv_bias[1])
        pieces = [query[head : head + 1] for head in range(self.heads)]
        pieces += [value[head : head + 1] for head in range(self.heads)]
        pieces.append(jnp.zeros((1, model - 2 * self.width), F32))
        rows.append(jnp.concatenate(pieces, axis=1))
        above = spread(self.up_bias[...])
        rows.append(
            jnp.concatenate([above[group : group + 1] for group in range(above.shape[0])], axis=1)
        )
        self.small_all[self.section, self.dp] = jnp.concatenate(rows, axis=0)

    def small_outputs(self):
        total = self.stat_sums[self.bits + 1, self.section]
        model = self.model

        def turned(offset):
            return pltpu.roll(total, lax.rem(model - offset, model), 1)

        share = self.part // self.line
        self.row_sums[...] = turned(self.dp * self.part + self.me * share)[:6, :share]
        size = self.head_size // self.dp_count
        moved = turned(self.dp * size)
        for which in range(2):
            for head in range(self.heads):
                low = which * self.width + head * self.head_size
                self.qv_sums[which, head : head + 1] = moved[6:7, low : low + size]
        groups, size = self.shift_sums.shape
        moved = turned(self.dp * size)
        for group in range(groups):
            low = group * size * self.dp_count
            self.shift_sums[group : group + 1] = moved[7:8, low : low + size]

    def own_copies(self):
        mine = pl.ds(pl.multiple_of(self.dp * self.part, self.part), self.part)
        here = self.weights.at[self.section]
        pairs = [
            (self.qkv_own, here.at[0, mine, pl.ds(0, 3 * self.width)]),
            (self.out_own, self.out_raw),
            (self.up_own, here.at[1, mine]),
            (self.down_own, self.down_raw),
        ]
        return [
            pltpu.make_async_copy(source, target, self.own_sem.at[number])
            for number, (source, target) in enumerate(pairs)
        ]

    def run(self):
        def nothing(step):
            pass

        copies = self.own_copies()
        for copy in copies:
            copy.start()
        self.greet()
        self.rows_start(0, self.block_rows, self.inputs.at[0])
        mine = pl.ds(pl.multiple_of(self.dp * self.part, self.part), self.part)
        copies[0].wait()
        copies[1].wait()
        self.weights[self.section, 0, mine, 3 * self.width :] = self.out_raw[...].T
        self.weights_offer(0, 0, QUARTERS)
        self.spread_small()
        self.small_offer(0)
        copies[2].wait()
        copies[3].wait()
        self.weights[self.section, 2, mine] = self.down_raw[...].T
        self.weights_offer(0, QUARTERS, PIECES)
        self.clear()
        for p in range(QUARTERS + 1):
            if p < QUARTERS:
                self.weights_cross(0, p)
            if p == 1:
                self.weights_cross(0, None)
            if p == 2:
                self.weights_relay(0, None)
            if p > 0:
                self.weights_relay(0, p - 1)
        self.weights_land(0, None)
        loop(QUARTERS, functools.partial(self.weights_land, 0))
        self.params[0] = jnp.sum(self.small_all[0], axis=0)
        self.rows_wait(0, self.block_rows, self.inputs.at[0])
        self.rows_start(1, self.upstream_rows, self.grad_one_held)

        def weights_early(s, base):
            def early(step):
                @pl.when(step < QUARTERS)
                def _():
                    self.weights_cross(s, base + step)

                @pl.when(step > 0)
                def _():
                    self.weights_relay(s, base + step - 1)

            return early

        def weights_tick(s, base):
            def tick(step):
                @pl.when(step % 2 == 0)
                def _():
                    self.weights_cross(s, base + step // 2)

                @pl.when(step % 2 == 1)
                def _():
                    self.weights_relay(s, base + step // 2)

            return tick

        self.attention(0)
        self.line_sum(
            self.after_attention(0),
            weights_tick(0, 2 * QUARTERS),
            weights_early(0, QUARTERS),
        )
        self.small_offer(1)
        self.weights_offer(1, 0, PIECES)
        loop(QUARTERS, lambda p: self.weights_land(0, QUARTERS + p))
        self.feed_up(0)
        loop(QUARTERS, lambda p: self.weights_land(0, 2 * QUARTERS + p))
        self.feed_down(0)
        self.weights_cross(1, None)
        self.weights_relay(1, None)
        self.line_sum(
            self.after_feed(0), weights_tick(1, QUARTERS), weights_early(1, 0)
        )
        self.output_start(0)
        self.weights_land(1, None)
        loop(QUARTERS, functools.partial(self.weights_land, 1))
        self.params[1] = jnp.sum(self.small_all[1], axis=0)

        self.attention(1)
        self.line_sum(
            self.after_attention(1), nothing, weights_early(1, 2 * QUARTERS)
        )
        loop(QUARTERS, lambda p: self.weights_land(1, QUARTERS + p))
        self.feed_up(1)
        loop(QUARTERS, lambda p: self.weights_land(1, 2 * QUARTERS + p))
        self.feed_down(1)
        self.rows_wait(1, self.upstream_rows, self.grad_one_held)
        self.line_sum(self.after_feed(1), nothing, nothing)
        self.output_start(1)

        def turn(order):
            return (SLABS - 1 - order // QUARTERS) * QUARTERS + order % QUARTERS

        half = 2 * QUARTERS
        blocks = self.model // BLOCK

        def feed_early(s):
            def early(step):
                @pl.when(step < blocks)
                def _():
                    self.feed_grads(s, step)

                @pl.when(step == blocks)
                def _():
                    loop(half, lambda order: self.grads_offer(s, turn(order)))

            return early

        def feed_tick(s):
            def tick(step):
                self.grads_fold(s, turn(step))

                @pl.when(step >= 4)
                def _():
                    self.grads_cross(s, turn(step - 4))

                if s == 0:

                    @pl.when(step < QUARTERS)
                    def _():
                        self.grads_end(1, step)

            return tick

        def attention_early(s):
            def early(step):
                @pl.when(step < blocks)
                def _():
                    self.attention_grads(s, step)

                @pl.when(step == blocks)
                def _():
                    loop(QUARTERS, lambda order: self.grads_offer(s, order))
                    if s == 0:
                        self.stat_sums[0] = jnp.sum(self.stats[...], axis=2)
                        self.stat_copy(0).start()

            return early

        def attention_tick(s):
            def tick(step):
                @pl.when(step < QUARTERS)
                def _():
                    self.grads_fold(s, step)

                self.grads_cross(s, turn(step + 4))
                self.grads_end(s, turn(step))
                if s == 0:
                    for number in range(self.bits + 1):

                        @pl.when(step == min(2 * number + 1, self.chunks - 1))
                        def _():
                            self.stat_step(number)

            return tick

        for s in (1, 0):
            self.feed_back(s)
            self.line_sum(self.after_feed_back(s), feed_tick(s), feed_early(s))
            self.attention_back(s)
            self.line_sum(self.after_attention_back(s), attention_tick(s), attention_early(s))
            self.input_grad_start(s)

        self.small_outputs()

        @pl.when(self.section == 1)
        def _():
            self.out_sums[...] = self.out_turned[...].T

        self.down_sums[...] = self.down_turned[...].T
        loop(QUARTERS, functools.partial(self.grads_end, 0))

        @pl.when(self.section == 0)
        def _():
            self.out_sums[...] = self.out_turned[...].T

        self.outputs_end()

        for which, source, target in (
            (0, self.block_rows, self.inputs.at[0]),
            (1, self.upstream_rows, self.grad_one_held),
        ):
            for step in range(1, self.line):
                self.rows_copy(which, source, target, step).wait_send()
        self.line_sent()
        for s in range(2):
            self.weights_sent(s, None)
            loop(PIECES, functools.partial(self.weights_sent, s))
            loop(PIECES, functools.partial(self.grads_sent, s))
        for step in range(self.bits + 1):
            self.stat_copy(step).wait_send()


def layers_kernel(sizes, *refs):
    Layers(sizes, refs).run()


def both_layers(arrays, sizes):
    line, dp_count, part = sizes["line"], sizes["dp_count"], sizes["part"]
    rows, width, model, units = sizes["rows"], sizes["width"], sizes["model"], sizes["units"]
    heads = sizes["heads"]
    tokens = line * rows
    chunks = tokens // CHUNK
    bits = dp_count.bit_length() - 1
    dma = pltpu.SemaphoreType.DMA
    vmem = pltpu.VMEM
    scratch = dict(
        inputs=vmem((3, tokens, model), BF16),
        weights=vmem((2, SLABS, model, units), BF16),
        grads=vmem((2, SLABS, model, units), BF16),
        landed=vmem((2, SLABS, model, units), BF16),
        small_all=vmem((2, dp_count, STATS, model), F32),
        params=vmem((2, STATS, model), F32),
        sums=vmem((2, 2, tokens, model), BF16),
        staged=vmem((2, tokens, model), BF16),
        partial=vmem((tokens, model), F32),
        wide=vmem((tokens, model), F32),
        grad_wide=vmem((tokens, model), F32),
        normed_one=vmem((2, tokens, model), BF16),
        normed_two=vmem((tokens, model), BF16),
        scaled_one=vmem((2, tokens, 128), F32),
        scaled_two=vmem((tokens, 128), F32),
        hidden=vmem((2, tokens, model), BF16),
        active=vmem((2, tokens, units), BF16),
        slope=vmem((2, tokens, units), BF16),
        qkv=vmem((2, tokens, 3 * width), BF16),
        probs=vmem((2, heads, tokens, tokens), BF16),
        context=vmem((2, tokens, width), BF16),
        grad_two_held=vmem((tokens, model), BF16),
        grad_one_held=vmem((tokens, model), BF16),
        grad_pre=vmem((tokens, units), BF16),
        grad_context=vmem((tokens, width), BF16),
        grad_qkv=vmem((tokens, 3 * width), BF16),
        hidden_pairs=vmem((tokens, tokens), F32),
        stats=vmem((2, STATS, 8, model), F32),
        stat_sums=vmem((bits + 2, 2, STATS, model), F32),
        stat_landed=vmem((bits + 1, 2, STATS, model), F32),
        input_grad_staged=vmem((rows, model), BF16),
        input_grad_landed=vmem((rows, model), BF16),
        out_raw=vmem((width, part), BF16),
        down_raw=vmem((units, part), BF16),
        out_turned=vmem((part, width), F32),
        down_turned=vmem((part, units), F32),
        rows_send=dma((2, line - 1)),
        rows_recv=dma((2, line - 1)),
        rows_own=dma((2,)),
        own_sem=dma((4,)),
        weight_send=dma((2, PIECES + 1, dp_count)),
        weight_recv=dma((2, PIECES + 1, dp_count)),
        grad_send=dma((2, PIECES, dp_count)),
        grad_recv=dma((2, PIECES, dp_count)),
        line_send=dma((2, chunks)),
        line_recv=dma((2, 2, chunks)),
        out_sem=dma((5,)),
        stat_sem=dma((2, bits + 1)),
    )
    outs = dict(
        outputs=((2, rows, model), BF16),
        input_grads=((2, rows, model), F32),
        qkv_sums=((3, part, width), F32),
        out_sums=((width, part), F32),
        up_sums=((part, units), F32),
        down_sums=((units, part), F32),
        row_sums=((6, part // line), F32),
        qv_sums=((2, heads, sizes["head_size"] // dp_count), F32),
        shift_sums=(arrays["up_bias"].shape, F32),
    )
    far = ("block_rows", "upstream_rows", "qkv_own", "out_own", "up_own", "down_own")
    names = list(arrays) + list(outs) + list(scratch)
    return pl.pallas_call(
        functools.partial(layers_kernel, dict(sizes, names=names)),
        out_shape=[jax.ShapeDtypeStruct(shape, kind) for shape, kind in outs.values()],
        in_specs=[ANY_SPEC if name in far else VMEM_SPEC for name in arrays],
        out_specs=[VMEM_SPEC] * len(outs),
        scratch_shapes=list(scratch.values()),
        compiler_params=pltpu.CompilerParams(
            collective_id=1, has_side_effects=True, vmem_limit_bytes=VMEM_LIMIT
        ),
        name="both_layers",
    )(*arrays.values())


def shards(
    block_input,
    seq_ids,
    out_cotangent,
    qkv_weight,
    qv_bias,
    out_weight,
    out_bias,
    norm1_gain,
    norm1_bias,
    up_weight,
    up_bias,
    down_weight,
    down_bias,
    norm2_gain,
    norm2_bias,
):
    dp_count = lax.axis_size("dp")
    line = lax.axis_size("tensor")
    heads, head_part = qv_bias.shape[2], qv_bias.shape[3]
    part = out_bias.shape[1]
    width = qkv_weight.shape[3]
    model = block_input.shape[3]
    units = up_weight.shape[2]
    sizes = dict(
        line=line,
        dp_count=dp_count,
        part=part,
        width=width,
        rows=block_input.shape[2],
        model=model,
        units=units,
        heads=heads,
        head_size=head_part * dp_count,
    )
    arrays = dict(
        block_rows=block_input[:, 0],
        upstream_rows=out_cotangent[:, 0],
        ids=seq_ids,
        qkv_own=qkv_weight[0].reshape(part, 3 * width),
        out_own=out_weight[0],
        up_own=up_weight[0],
        down_own=down_weight[0],
        out_bias=out_bias,
        gain_one=norm1_gain,
        bias_one=norm1_bias,
        down_bias=down_bias,
        gain_two=norm2_gain,
        bias_two=norm2_bias,
        qv_bias=qv_bias[0],
        up_bias=up_bias[0],
    )
    results = both_layers(arrays, sizes)
    outputs, input_grads, qkv_sums, out_sums, up_sums, down_sums, rows, qv_sums, shift_sums = results
    return (
        outputs[None, :, None],
        input_grads[None, :, None],
        jnp.swapaxes(qkv_sums, 0, 1)[None],
        qv_sums[None],
        out_sums[None],
        rows[0][None],
        rows[1][None],
        rows[2][None],
        up_sums[None],
        shift_sums[None],
        down_sums[None],
        rows[3][None],
        rows[4][None],
        rows[5][None],
    )


def solution(mesh):
    return jax.shard_map(
        shards,
        mesh=mesh,
        in_specs=(
            P(None, "dp", "tensor", None),
            P(None, "dp", None),
            P(None, "dp", "tensor", None),
            P("section", "dp", None, "tensor"),
            P("section", None, "tensor", "dp"),
            P("section", "tensor", "dp"),
            P("section", "dp"),
            P("section", "dp"),
            P("section", "dp"),
            P("section", "dp", "tensor"),
            P("section", "tensor", "dp"),
            P("section", "tensor", "dp"),
            P("section", "dp"),
            P("section", "dp"),
            P("section", "dp"),
        ),
        out_specs=(
            P("section", None, "dp", "tensor", None),
            P("section", None, "dp", "tensor", None),
            P("section", "dp", None, "tensor"),
            P("section", None, "tensor", "dp"),
            P("section", "tensor", "dp"),
            P("section", ("dp", "tensor")),
            P("section", ("dp", "tensor")),
            P("section", ("dp", "tensor")),
            P("section", "dp", "tensor"),
            P("section", "tensor", "dp"),
            P("section", "tensor", "dp"),
            P("section", ("dp", "tensor")),
            P("section", ("dp", "tensor")),
            P("section", ("dp", "tensor")),
        ),
        check_vma=False,
    )
```

```python
import functools

import jax
import jax.numpy as jnp
from jax import lax
from jax.experimental import pallas as pl
from jax.experimental.pallas import tpu as pltpu
from jax.sharding import PartitionSpec as P

MESH = pl.DeviceIdType.MESH
F32 = jnp.float32
BF16 = jnp.bfloat16
VMEM_SPEC = pl.BlockSpec(memory_space=pltpu.VMEM)
ANY_SPEC = pl.BlockSpec(memory_space=pl.ANY)
VMEM_LIMIT = 63 * 1024 * 1024
CHUNK = 32
AHEAD = 3
QUARTERS = 4
SLABS = 3
PIECES = SLABS * QUARTERS
STATS = 8
BLOCK = 256
VECTORS = ("out_bias", "gain_one", "bias_one", "down_bias", "gain_two", "bias_two")

ERF_TOP = (
    0.00022905065861350646,
    0.0034082910107109506,
    0.050955695062380861,
    0.18520832239976145,
    1.128379143519084,
)
ERF_BELOW = (
    -1.1791602954361697e-7,
    0.000023547966471313185,
    0.0010179625278914885,
    0.014070470171167667,
    0.11098505178285362,
    0.49746925110067538,
    1.0,
)


def erf(values):
    x = jnp.clip(values, -3.832506856900711, 3.832506856900711)
    square = x * x
    top = jnp.full_like(square, ERF_TOP[0])
    for term in ERF_TOP[1:]:
        top = top * square + term
    below = jnp.full_like(square, ERF_BELOW[0])
    for term in ERF_BELOW[1:]:
        below = below * square + term
    return x * top / below


def nn(a, b):
    return lax.dot_general(a, b, (((1,), (0,)), ((), ())), preferred_element_type=F32)


def nt(a, b):
    return lax.dot_general(a, b, (((1,), (1,)), ((), ())), preferred_element_type=F32)


def tn(a, b):
    return lax.dot_general(a, b, (((0,), (0,)), ((), ())), preferred_element_type=F32)


def loop(count, body):
    def one(index, carry):
        body(index)
        return carry

    lax.fori_loop(0, count, one, 0)


def span(index, size):
    return pl.ds(pl.multiple_of(index * size, size), size)


def mean(values):
    return jnp.mean(values, axis=-1, keepdims=True)


def normalize(summed):
    center = summed - mean(summed)
    scaled = lax.rsqrt(mean(center * center) + 1e-12)
    return center * scaled, scaled


def norm_back(upstream, normed, scaled):
    return scaled * (upstream - mean(upstream) - normed * mean(upstream * normed))


def low_bit(mask):
    return (mask & -mask).bit_length() - 1


class Layers:
    def __init__(self, sizes, refs):
        for name, ref in zip(sizes["names"], refs):
            setattr(self, name, ref)
        self.vectors = [getattr(self, name) for name in VECTORS]
        self.line = sizes["line"]
        self.dp_count = sizes["dp_count"]
        self.bits = self.dp_count.bit_length() - 1
        self.part = sizes["part"]
        self.width = sizes["width"]
        self.rows = sizes["rows"]
        self.tokens = self.line * self.rows
        self.model = sizes["model"]
        self.units = sizes["units"]
        self.heads = sizes["heads"]
        self.head_size = sizes["head_size"]
        self.chunks = self.tokens // CHUNK
        self.quarter = self.part // QUARTERS
        self.section = lax.axis_index("section")
        self.dp = lax.axis_index("dp")
        self.me = lax.axis_index("tensor")
        self.nears = self.me // (self.line // 2)
        self.fars = 1 - self.nears
        self.middle = jnp.logical_and(self.me > 0, self.me < self.line - 1)
        self.own_rows = span(self.me, self.rows)
        self.passes = 0


    def place(self, mask):
        dp = self.dp
        for bit in range(self.bits):
            if mask & (1 << bit):
                dp = dp + (1 << bit) * (1 - 2 * ((self.dp // (1 << bit)) % 2))
        return dp

    def neighbour(self, bit):
        return {"dp": self.place(1 << bit)}

    def across(self):
        return {"section": 1 - self.section}

    def line_peer(self, step):
        return lax.rem(self.me + step, self.line)

    def remote(self, src, dst, send_sem, recv_sem, device):
        return pltpu.make_async_remote_copy(
            src_ref=src,
            dst_ref=dst,
            send_sem=send_sem,
            recv_sem=recv_sem,
            device_id=device,
            device_id_type=MESH,
        )

    def greet(self):
        barrier = pltpu.get_barrier_semaphore()
        targets = [{"tensor": self.line_peer(step)} for step in range(1, self.line)]
        targets += [self.neighbour(bit) for bit in range(self.bits)] + [self.across()]
        for target in targets:
            pl.semaphore_signal(barrier, inc=1, device_id=target, device_id_type=MESH)
        pl.semaphore_wait(barrier, len(targets))


    def rows_copy(self, which, source, target, step):
        return self.remote(
            source.at[self.section],
            target.at[self.own_rows],
            self.rows_send.at[which, step - 1],
            self.rows_recv.at[which, step - 1],
            {"tensor": self.line_peer(step)},
        )

    def rows_local(self, which, source, target):
        return pltpu.make_async_copy(
            source.at[self.section], target.at[self.own_rows], self.rows_own.at[which]
        )

    def rows_start(self, which, source, target):
        for step in range(1, self.line):
            self.rows_copy(which, source, target, step).start()
        self.rows_local(which, source, target).start()

    def rows_wait(self, which, source, target):
        self.rows_local(which, source, target).wait()
        for step in range(1, self.line):
            self.rows_copy(which, source, target, step).wait_recv()


    def weight_slot(self, s, p, mask):
        if p is None:
            return self.small_all.at[s, self.place(mask)]
        return self.weights.at[s, p // QUARTERS, self.piece_rows(p, mask)]

    def piece_rows(self, p, mask):
        at = self.place(mask) * self.part + (p % QUARTERS) * self.quarter
        return pl.ds(pl.multiple_of(at, self.quarter), self.quarter)

    def weight_copy(self, s, p, held, bit):
        number = PIECES if p is None else p
        mask = held | (1 << bit)
        return self.remote(
            self.weight_slot(s, p, held),
            self.weight_slot(s, p, held),
            self.weight_send.at[s, number, mask],
            self.weight_recv.at[s, number, mask],
            self.neighbour(bit),
        )

    def weight_arrival(self, s, p, mask):
        number = PIECES if p is None else p
        return self.remote(
            self.weight_slot(s, p, mask),
            self.weight_slot(s, p, mask),
            self.weight_send.at[s, number, mask],
            self.weight_recv.at[s, number, mask],
            self.neighbour(low_bit(mask)),
        )

    def weight_across(self, s, p):
        number = PIECES if p is None else p
        return self.remote(
            self.weight_slot(s, p, 0),
            self.weight_slot(s, p, 0),
            self.weight_send.at[s, number, 0],
            self.weight_recv.at[s, number, 0],
            self.across(),
        )

    def weight_forward(self, s, p, held):
        top = self.bits if held == 0 else low_bit(held)
        for bit in reversed(range(top)):
            self.weight_copy(s, p, held, bit).start()

    def weight_offer(self, s, p):
        self.weight_across(s, p).start()
        self.weight_forward(s, p, 0)

    def weights_offer(self, s, first, last):
        @pl.when(self.section == s)
        def _():
            loop(last - first, lambda p: self.weight_offer(s, first + p))

    def small_offer(self, s):
        @pl.when(self.section == s)
        def _():
            self.weight_offer(s, None)

    def weights_cross(self, s, p):
        @pl.when(self.section != s)
        def _():
            self.weight_across(s, p).wait_recv()
            self.weight_forward(s, p, 0)

    def weights_relay(self, s, p):
        for bit in reversed(range(1, self.bits)):
            for mask in range(self.dp_count):
                if mask and low_bit(mask) == bit:
                    self.weight_arrival(s, p, mask).wait_recv()
                    self.weight_forward(s, p, mask)

    def weights_land(self, s, p):
        for mask in range(1, self.dp_count, 2):
            self.weight_arrival(s, p, mask).wait_recv()

    def weights_sent(self, s, p):
        for mask in range(1, self.dp_count):
            held = mask & (mask - 1)
            self.weight_copy(s, p, held, low_bit(mask)).wait_send()

        @pl.when(self.section == s)
        def _():
            self.weight_across(s, p).wait_send()


    def grad_slot(self, s, p, mask):
        return self.grads.at[s, p // QUARTERS, self.piece_rows(p, mask)]

    def grad_landed(self, s, p, mask):
        at = mask * self.part + (p % QUARTERS) * self.quarter
        rows = pl.ds(pl.multiple_of(at, self.quarter), self.quarter)
        return self.landed.at[s, p // QUARTERS, rows]

    def grad_copy(self, s, p, mask):
        device = self.neighbour(low_bit(mask)) if mask else self.across()
        return self.remote(
            self.grad_slot(s, p, mask),
            self.grad_landed(s, p, mask),
            self.grad_send.at[s, p, mask],
            self.grad_recv.at[s, p, mask],
            device,
        )

    def grad_total(self, s, p, mask, last=False):
        total = self.grad_slot(s, p, mask)[...].astype(F32)
        for bit in range(low_bit(mask) if mask else self.bits):
            self.grad_copy(s, p, mask | (1 << bit)).wait_recv()
            total = total + self.grad_landed(s, p, mask | (1 << bit))[...].astype(F32)
        return total

    def grads_offer(self, s, p):
        for mask in range(1, self.dp_count, 2):
            self.grad_copy(s, p, mask).start()

    def grads_fold(self, s, p):
        for bit in range(1, self.bits):
            for mask in range(self.dp_count):
                if mask and low_bit(mask) == bit:
                    self.grad_slot(s, p, mask)[...] = self.grad_total(s, p, mask).astype(BF16)
                    self.grad_copy(s, p, mask).start()

    def grads_cross(self, s, p):
        @pl.when(self.section != s)
        def _():
            self.grad_slot(s, p, 0)[...] = self.grad_total(s, p, 0).astype(BF16)
            self.grad_copy(s, p, 0).start()

    def grads_end(self, s, p):
        @pl.when(self.section == s)
        def _():
            total = self.grad_total(s, p, 0)
            self.grad_copy(s, p, 0).wait_recv()
            total = total + self.grad_landed(s, p, 0)[...].astype(F32)
            rows = span(p % QUARTERS, self.quarter)
            slab = p // QUARTERS

            @pl.when(slab == 0)
            def _():
                for which in range(3):
                    at = slice(which * self.width, (which + 1) * self.width)
                    self.qkv_sums[which, rows] = total[:, at]
                self.out_turned[rows] = total[:, 3 * self.width :]

            @pl.when(slab == 1)
            def _():
                self.up_sums[rows] = total

            @pl.when(slab == 2)
            def _():
                self.down_turned[rows] = total

    def grads_sent(self, s, p):
        for mask in range(1, self.dp_count):
            self.grad_copy(s, p, mask).wait_send()

        @pl.when(self.section != s)
        def _():
            self.grad_copy(s, p, 0).wait_send()


    def line_copy(self, half, side, chunk, target):
        rows = span(chunk, CHUNK)
        return self.remote(
            self.staged.at[side, rows],
            self.sums.at[half, side, rows],
            self.line_send.at[side, chunk],
            self.line_recv.at[half, side, chunk],
            {"tensor": target},
        )

    def line_sum(self, finish, tick):
        number = self.passes
        half = number % 2
        self.passes += 1
        near_target = self.me + 1 - 2 * self.nears
        far_target = self.me - 1 + 2 * self.nears

        def send(side, chunk, target):
            rows = span(chunk, CHUNK)
            if number > 0:
                self.line_copy(half, side, chunk, target).wait_send()
            total = self.partial[rows] + self.sums[half, side, rows].astype(F32)
            self.staged[side, rows] = total.astype(BF16)
            self.line_copy(half, side, chunk, target).start()

        def near(chunk):
            @pl.when(self.middle)
            def _():
                self.line_copy(half, self.nears, chunk, near_target).wait_recv()

            send(self.nears, chunk, near_target)

        ahead = jnp.where(self.middle, AHEAD, self.chunks)
        loop(ahead, near)

        def body(chunk):
            @pl.when(chunk + ahead < self.chunks)
            def _():
                near(chunk + ahead)

            self.line_copy(half, self.fars, chunk, near_target).wait_recv()

            @pl.when(self.middle)
            def _():
                send(self.fars, chunk, far_target)

            rows = span(chunk, CHUNK)
            total = (
                self.partial[rows]
                + self.sums[half, 0, rows].astype(F32)
                + self.sums[half, 1, rows].astype(F32)
            )
            finish(rows, total)
            tick(chunk)

        loop(self.chunks, body)

    def line_sent(self):
        def one(chunk):
            self.line_copy(0, self.nears, chunk, self.me + 1 - 2 * self.nears).wait_send()

            @pl.when(self.middle)
            def _():
                self.line_copy(0, self.fars, chunk, self.me - 1 + 2 * self.nears).wait_send()

        loop(self.chunks, one)

    def clear(self):
        for half in range(2):
            for side, end in ((0, 0), (1, self.line - 1)):

                @pl.when(self.me == end)
                def _():
                    self.sums[half, side] = jnp.zeros(self.sums.shape[2:], BF16)

        self.stats[...] = jnp.zeros(self.stats.shape, F32)
        row = jnp.broadcast_to(self.ids[self.section], (self.tokens, self.tokens))
        self.hidden_pairs[...] = jnp.where(row == row.T, 0.0, -1e30)


    def param(self, s, row):
        return self.params[s, row : row + 1]

    def count_stat(self, s, row, values):
        folded = values.reshape(values.shape[0] // 8, 8, values.shape[1])
        self.stats[s, row] += jnp.sum(folded, axis=0)

    def attention(self, s):
        width = self.width
        for block in range(3):
            at = slice(block * width, (block + 1) * width)
            made = nn(self.inputs[s], self.weights[s, 0, :, at])
            if block != 1:
                low = 0 if block == 0 else width
                made = made + self.params[s, 6:7, low : low + width]
            self.qkv[s, :, at] = made.astype(BF16)
        contexts = []
        for head in range(self.heads):
            query, key, value = self.head_parts(s, head)
            scores = nt(query, key) * self.head_size ** (-0.5) + self.hidden_pairs[...]
            shifted = jnp.exp(scores - jnp.max(scores, axis=-1, keepdims=True))
            prob = shifted / jnp.sum(shifted, axis=-1, keepdims=True)
            prob = prob.astype(BF16)
            self.probs[s, head] = prob
            contexts.append(nn(prob, value).astype(BF16))
        self.context[s] = jnp.concatenate(contexts, axis=1)

        def project(block):
            at = span(block, BLOCK)
            self.partial[:, at] = nt(self.context[s], self.weights[s, 0, at, 3 * width :])

        loop(self.model // BLOCK, project)

    def head_parts(self, s, head):
        size = self.head_size
        low = head * size
        return [
            self.qkv[s, :, which * self.width + low : which * self.width + low + size]
            for which in range(3)
        ]

    def feed_up(self, s):
        def block_of(block):
            at = span(block, BLOCK)
            self.partial[:, at] = nn(self.hidden[s], self.weights[s, 1, :, at])

        loop(self.units // BLOCK, block_of)

        def gelu(step):
            rows = span(step, 16)
            pre = self.partial[rows] + self.param(s, 7)
            half = 0.5 * (1.0 + erf(pre * 0.7071067811865476))
            self.active[s, rows] = (pre * half).astype(BF16)
            bell = pre * jnp.exp(-0.5 * pre * pre) * 0.3989422804014327
            self.slope[s, rows] = (half + bell).astype(BF16)

        loop(self.tokens // 16, gelu)

    def feed_down(self, s):
        def block_of(block):
            at = span(block, BLOCK)
            self.partial[:, at] = nt(self.active[s], self.weights[s, 2, at])

        loop(self.model // BLOCK, block_of)

    def after_attention(self, s):
        def finish(rows, total):
            summed = self.inputs[s, rows].astype(F32) + total + self.param(s, 0)
            normed, scaled = normalize(summed)
            self.normed_one[s, rows] = normed.astype(BF16)
            self.scaled_one[s, rows] = jnp.broadcast_to(scaled, (CHUNK, 128))
            hidden = normed * self.param(s, 1) + self.param(s, 2)
            self.wide[rows] = hidden
            self.hidden[s, rows] = hidden.astype(BF16)

        return finish

    def after_feed(self, s):
        def finish(rows, total):
            summed = self.wide[rows] + total + self.param(s, 3)
            normed, scaled = normalize(summed)
            out = normed * self.param(s, 4) + self.param(s, 5)
            self.inputs[s + 1, rows] = out.astype(BF16)
            if s == 0:
                self.normed_two[rows] = normed.astype(BF16)
                self.scaled_two[rows] = jnp.broadcast_to(scaled, (CHUNK, 128))
            else:
                self.start_back(s, rows, self.grad_one_held[rows].astype(F32), normed, scaled)

        return finish

    def start_back(self, s, rows, upstream, normed, scaled):
        grad_two = norm_back(upstream * self.param(s, 4), normed, scaled)
        self.wide[rows] = grad_two
        self.grad_two_held[rows] = grad_two.astype(BF16)
        self.count_stat(s, 3, grad_two)
        self.count_stat(s, 4, upstream * normed)
        self.count_stat(s, 5, upstream)

    def feed_back(self, s):
        def block_of(block):
            at = span(block, BLOCK)
            self.partial[:, at] = nn(self.grad_two_held[...], self.weights[s, 2, :, at])

        loop(self.units // BLOCK, block_of)

        def slopes(step):
            rows = span(step, 16)
            grad_pre = self.partial[rows] * self.slope[s, rows].astype(F32)
            self.grad_pre[rows] = grad_pre.astype(BF16)
            self.count_stat(s, 7, grad_pre)

        loop(self.tokens // 16, slopes)

        def up_of(block):
            at = span(block, BLOCK)
            self.partial[:, at] = nt(self.grad_pre[...], self.weights[s, 1, at])

        loop(self.model // BLOCK, up_of)

    def after_feed_back(self, s):
        def finish(rows, total):
            grad_hidden = self.wide[rows] + total
            normed = self.normed_one[s, rows].astype(F32)
            scaled = self.scaled_one[s, rows][:, :1]
            grad_one = norm_back(grad_hidden * self.param(s, 1), normed, scaled)
            self.grad_wide[rows] = grad_one
            self.grad_one_held[rows] = grad_one.astype(BF16)
            self.count_stat(s, 0, grad_one)
            self.count_stat(s, 1, grad_hidden * normed)
            self.count_stat(s, 2, grad_hidden)

        return finish

    def feed_grads(self, s, step):
        cuts = self.chunks // 2
        block = step // 2
        size = self.model // cuts
        at = span(block, size)

        @pl.when(step % 2 == 0)
        def _():
            made = tn(self.grad_two_held[:, at], self.active[s])
            self.grads[s, 2, at] = made.astype(BF16)

        @pl.when(step % 2 == 1)
        def _():
            made = tn(self.hidden[s, :, at], self.grad_pre[...])
            self.grads[s, 1, at] = made.astype(BF16)

    def attention_grads(self, s, step):
        cuts = self.chunks // 2
        block = step // 2
        size = self.model // cuts
        at = span(block, size)

        @pl.when(step % 2 == 0)
        def _():
            made = tn(self.inputs[s, :, at], self.grad_qkv[...])
            self.grads[s, 0, at, : 3 * self.width] = made.astype(BF16)

        @pl.when(step % 2 == 1)
        def _():
            made = tn(self.grad_one_held[:, at], self.context[s])
            self.grads[s, 0, at, 3 * self.width :] = made.astype(BF16)

    def attention_back(self, s):
        width, size = self.width, self.head_size
        grad_context = nn(self.grad_one_held[...], self.weights[s, 0, :, 3 * width :])
        self.grad_context[...] = grad_context.astype(BF16)
        parts = [[], [], []]
        for head in range(self.heads):
            query, key, value = self.head_parts(s, head)
            above = self.grad_context[:, head * size : (head + 1) * size]
            held = self.probs[s, head]
            prob = held.astype(F32)
            grad_prob = nt(above, value)
            dots = jnp.sum(prob * grad_prob, axis=-1, keepdims=True)
            grad_scores = (prob * (grad_prob - dots) * size ** (-0.5)).astype(BF16)
            parts[0].append(nn(grad_scores, key))
            parts[1].append(tn(grad_scores, query))
            parts[2].append(tn(held, above))
        for which in range(3):
            made = jnp.concatenate(parts[which], axis=1)
            self.grad_qkv[:, which * width : (which + 1) * width] = made.astype(BF16)
            if which != 1:
                folded = jnp.sum(made.reshape(self.tokens // 8, 8, width), axis=0)
                low = 0 if which == 0 else width
                self.stats[s, 6, :, low : low + width] = folded

        def block_of(block):
            at = span(block, BLOCK)
            self.partial[:, at] = nt(self.grad_qkv[...], self.weights[s, 0, at, : 3 * width])

        loop(self.model // BLOCK, block_of)

    def after_attention_back(self, s):
        def finish(rows, total):
            upstream = self.grad_wide[rows] + total
            self.grad_wide[rows] = upstream
            if s == 1:
                normed = self.normed_two[rows].astype(F32)
                self.start_back(0, rows, upstream, normed, self.scaled_two[rows][:, :1])

        return finish


    def output_copy(self, s, local):
        source = self.inputs.at[s + 1, self.own_rows]
        target = self.outputs.at[self.section]
        if local:
            return pltpu.make_async_copy(source, target, self.out_sem.at[0])
        return self.remote(source, target, self.out_sem.at[1], self.out_sem.at[2], self.across())

    def output_start(self, s):
        for local in (True, False):

            @pl.when((self.section == s) if local else (self.section != s))
            def _():
                self.output_copy(s, local).start()

    def input_grad_copy(self):
        return self.remote(
            self.input_grad_staged,
            self.input_grad_landed,
            self.out_sem.at[3],
            self.out_sem.at[4],
            self.across(),
        )

    def input_grad_start(self, s):
        @pl.when(self.section == s)
        def _():
            self.input_grads[self.section] = self.grad_wide[self.own_rows]

        @pl.when(self.section != s)
        def _():
            self.input_grad_staged[...] = self.grad_wide[self.own_rows].astype(BF16)
            self.input_grad_copy().start()

    def outputs_end(self):
        self.output_copy(0, True).wait()
        self.output_copy(0, False).wait()
        self.input_grad_copy().wait()
        self.input_grads[1 - self.section] = self.input_grad_landed[...].astype(F32)


    def stat_copy(self, step):
        return self.remote(
            self.stat_sums.at[step],
            self.stat_landed.at[step],
            self.stat_sem.at[0, step],
            self.stat_sem.at[1, step],
            self.neighbour(step) if step < self.bits else self.across(),
        )

    def stat_step(self, step):
        self.stat_copy(step).wait_recv()
        self.stat_sums[step + 1] = self.stat_sums[step] + self.stat_landed[step]
        if step < self.bits:
            self.stat_copy(step + 1).start()


    def spread_small(self):
        model, dp_count = self.model, self.dp_count
        place = lax.broadcasted_iota(jnp.int32, (1, model), 1) // self.part
        rows = []
        for ref in self.vectors:
            tiled = jnp.concatenate([ref[...].astype(F32)] * dp_count, axis=1)
            rows.append(jnp.where(place == self.dp, tiled, 0.0))

        def spread(values):
            size = values.shape[1]
            shape = (size, size * dp_count)
            low = lax.broadcasted_iota(jnp.int32, shape, 0) + self.dp * size
            chosen = jnp.where(lax.broadcasted_iota(jnp.int32, shape, 1) == low, 1.0, 0.0)
            return nn(values.astype(BF16), chosen.astype(BF16))

        query, value = spread(self.qv_bias[0]), spread(self.qv_bias[1])
        pieces = [query[head : head + 1] for head in range(self.heads)]
        pieces += [value[head : head + 1] for head in range(self.heads)]
        pieces.append(jnp.zeros((1, model - 2 * self.width), F32))
        rows.append(jnp.concatenate(pieces, axis=1))
        above = spread(self.up_bias[...])
        rows.append(
            jnp.concatenate([above[group : group + 1] for group in range(above.shape[0])], axis=1)
        )
        self.small_all[self.section, self.dp] = jnp.concatenate(rows, axis=0)

    def small_outputs(self):
        total = self.stat_sums[self.bits + 1, self.section]
        model = self.model

        def turned(offset):
            return pltpu.roll(total, lax.rem(model - offset, model), 1)

        share = self.part // self.line
        self.row_sums[...] = turned(self.dp * self.part + self.me * share)[:6, :share]
        size = self.head_size // self.dp_count
        moved = turned(self.dp * size)
        for which in range(2):
            for head in range(self.heads):
                low = which * self.width + head * self.head_size
                self.qv_sums[which, head : head + 1] = moved[6:7, low : low + size]
        groups, size = self.shift_sums.shape
        moved = turned(self.dp * size)
        for group in range(groups):
            low = group * size * self.dp_count
            self.shift_sums[group : group + 1] = moved[7:8, low : low + size]

    def own_copies(self):
        mine = pl.ds(pl.multiple_of(self.dp * self.part, self.part), self.part)
        here = self.weights.at[self.section]
        pairs = [
            (self.qkv_own, here.at[0, mine, pl.ds(0, 3 * self.width)]),
            (self.out_own, self.out_raw),
            (self.up_own, here.at[1, mine]),
            (self.down_own, self.down_raw),
        ]
        return [
            pltpu.make_async_copy(source, target, self.own_sem.at[number])
            for number, (source, target) in enumerate(pairs)
        ]

    def run(self):
        def nothing(step):
            pass

        copies = self.own_copies()
        for copy in copies:
            copy.start()
        self.greet()
        self.rows_start(0, self.block_rows, self.inputs.at[0])
        mine = pl.ds(pl.multiple_of(self.dp * self.part, self.part), self.part)
        copies[0].wait()
        copies[1].wait()
        self.weights[self.section, 0, mine, 3 * self.width :] = self.out_raw[...].T
        self.weights_offer(0, 0, QUARTERS)
        self.spread_small()
        self.small_offer(0)
        copies[2].wait()
        copies[3].wait()
        self.weights[self.section, 2, mine] = self.down_raw[...].T
        self.weights_offer(0, QUARTERS, PIECES)
        self.clear()
        for p in range(QUARTERS + 1):
            if p < QUARTERS:
                self.weights_cross(0, p)
            if p == 1:
                self.weights_cross(0, None)
            if p == 2:
                self.weights_relay(0, None)
            if p > 0:
                self.weights_relay(0, p - 1)
        self.weights_land(0, None)
        loop(QUARTERS, functools.partial(self.weights_land, 0))
        self.params[0] = jnp.sum(self.small_all[0], axis=0)
        self.rows_wait(0, self.block_rows, self.inputs.at[0])
        self.rows_start(1, self.upstream_rows, self.grad_one_held)

        self.attention(0)

        def first_tick(step):
            self.weights_cross(0, QUARTERS + step)

            @pl.when(step > 0)
            def _():
                self.weights_relay(0, QUARTERS + step - 1)

        self.line_sum(self.after_attention(0), first_tick)
        self.weights_relay(0, PIECES - 1)
        self.small_offer(1)
        self.weights_offer(1, 0, PIECES)
        loop(QUARTERS, lambda p: self.weights_land(0, QUARTERS + p))
        self.feed_up(0)
        loop(QUARTERS, lambda p: self.weights_land(0, 2 * QUARTERS + p))
        self.feed_down(0)

        def second_tick(step):
            @pl.when(step == 0)
            def _():
                self.weights_cross(1, None)

            @pl.when(step == 1)
            def _():
                self.weights_relay(1, None)

            self.weights_cross(1, step)

            @pl.when(step > 0)
            def _():
                self.weights_relay(1, step - 1)

        self.line_sum(self.after_feed(0), second_tick)
        self.output_start(0)
        self.weights_land(1, None)
        loop(QUARTERS, functools.partial(self.weights_land, 1))
        self.params[1] = jnp.sum(self.small_all[1], axis=0)

        self.attention(1)

        def third_tick(step):
            @pl.when(step < QUARTERS)
            def _():
                self.weights_cross(1, 2 * QUARTERS + step)

            @pl.when(step <= QUARTERS)
            def _():
                self.weights_relay(1, 2 * QUARTERS + step - 1)

        self.line_sum(self.after_attention(1), third_tick)
        loop(QUARTERS, lambda p: self.weights_land(1, QUARTERS + p))
        self.feed_up(1)
        loop(QUARTERS, lambda p: self.weights_land(1, 2 * QUARTERS + p))
        self.feed_down(1)
        self.rows_wait(1, self.upstream_rows, self.grad_one_held)
        self.line_sum(self.after_feed(1), nothing)
        self.output_start(1)

        def turn(order):
            return (SLABS - 1 - order // QUARTERS) * QUARTERS + order % QUARTERS

        def service(s, action, order):
            @pl.when(jnp.logical_and(order >= 0, order < PIECES))
            def _():
                action(s, turn(order))

        self.feed_back(1)
        self.line_sum(self.after_feed_back(1), functools.partial(self.feed_grads, 1))
        loop(2 * QUARTERS, lambda order: self.grads_offer(1, turn(order)))
        self.attention_back(1)

        def fourth_tick(step):
            self.attention_grads(1, step)
            service(1, self.grads_fold, step)
            service(1, self.grads_cross, step - 2)
            service(1, self.grads_end, step - 4)

        self.line_sum(self.after_attention_back(1), fourth_tick)
        loop(QUARTERS, lambda q: self.grads_offer(1, q))
        self.input_grad_start(1)
        self.feed_back(0)

        def fifth_tick(step):
            self.feed_grads(0, step)
            service(1, self.grads_fold, step + 8)
            service(1, self.grads_cross, step + 6)
            service(1, self.grads_end, step + 4)

        self.line_sum(self.after_feed_back(0), fifth_tick)
        loop(2 * QUARTERS, lambda order: self.grads_offer(0, turn(order)))
        self.attention_back(0)

        def sixth_tick(step):
            self.attention_grads(0, step)
            service(0, self.grads_fold, step)
            service(0, self.grads_cross, step - 2)
            service(0, self.grads_end, step - 4)

        self.line_sum(self.after_attention_back(0), sixth_tick)
        loop(QUARTERS, lambda q: self.grads_offer(0, q))
        self.input_grad_start(0)
        self.stat_sums[0] = jnp.sum(self.stats[...], axis=2)
        self.stat_copy(0).start()

        def last_tick(step):
            service(0, self.grads_fold, step + 8)
            service(0, self.grads_cross, step + 6)
            service(0, self.grads_end, step + 4)

        loop(8, last_tick)
        for step in range(self.bits + 1):
            self.stat_step(step)
        self.small_outputs()
        self.out_sums[...] = self.out_turned[...].T
        self.down_sums[...] = self.down_turned[...].T
        self.outputs_end()

        for which, source, target in (
            (0, self.block_rows, self.inputs.at[0]),
            (1, self.upstream_rows, self.grad_one_held),
        ):
            for step in range(1, self.line):
                self.rows_copy(which, source, target, step).wait_send()
        self.line_sent()
        for s in range(2):
            self.weights_sent(s, None)
            loop(PIECES, functools.partial(self.weights_sent, s))
            loop(PIECES, functools.partial(self.grads_sent, s))
        for step in range(self.bits + 1):
            self.stat_copy(step).wait_send()


def layers_kernel(sizes, *refs):
    Layers(sizes, refs).run()


def both_layers(arrays, sizes):
    line, dp_count, part = sizes["line"], sizes["dp_count"], sizes["part"]
    rows, width, model, units = sizes["rows"], sizes["width"], sizes["model"], sizes["units"]
    heads = sizes["heads"]
    tokens = line * rows
    chunks = tokens // CHUNK
    bits = dp_count.bit_length() - 1
    dma = pltpu.SemaphoreType.DMA
    vmem = pltpu.VMEM
    scratch = dict(
        inputs=vmem((3, tokens, model), BF16),
        weights=vmem((2, SLABS, model, units), BF16),
        grads=vmem((2, SLABS, model, units), BF16),
        landed=vmem((2, SLABS, model, units), BF16),
        small_all=vmem((2, dp_count, STATS, model), F32),
        params=vmem((2, STATS, model), F32),
        sums=vmem((2, 2, tokens, model), BF16),
        staged=vmem((2, tokens, model), BF16),
        partial=vmem((tokens, model), F32),
        wide=vmem((tokens, model), F32),
        grad_wide=vmem((tokens, model), F32),
        normed_one=vmem((2, tokens, model), BF16),
        normed_two=vmem((tokens, model), BF16),
        scaled_one=vmem((2, tokens, 128), F32),
        scaled_two=vmem((tokens, 128), F32),
        hidden=vmem((2, tokens, model), BF16),
        active=vmem((2, tokens, units), BF16),
        slope=vmem((2, tokens, units), BF16),
        qkv=vmem((2, tokens, 3 * width), BF16),
        probs=vmem((2, heads, tokens, tokens), BF16),
        context=vmem((2, tokens, width), BF16),
        grad_two_held=vmem((tokens, model), BF16),
        grad_one_held=vmem((tokens, model), BF16),
        grad_pre=vmem((tokens, units), BF16),
        grad_context=vmem((tokens, width), BF16),
        grad_qkv=vmem((tokens, 3 * width), BF16),
        hidden_pairs=vmem((tokens, tokens), F32),
        stats=vmem((2, STATS, 8, model), F32),
        stat_sums=vmem((bits + 2, 2, STATS, model), F32),
        stat_landed=vmem((bits + 1, 2, STATS, model), F32),
        input_grad_staged=vmem((rows, model), BF16),
        input_grad_landed=vmem((rows, model), BF16),
        out_raw=vmem((width, part), BF16),
        down_raw=vmem((units, part), BF16),
        out_turned=vmem((part, width), F32),
        down_turned=vmem((part, units), F32),
        rows_send=dma((2, line - 1)),
        rows_recv=dma((2, line - 1)),
        rows_own=dma((2,)),
        own_sem=dma((4,)),
        weight_send=dma((2, PIECES + 1, dp_count)),
        weight_recv=dma((2, PIECES + 1, dp_count)),
        grad_send=dma((2, PIECES, dp_count)),
        grad_recv=dma((2, PIECES, dp_count)),
        line_send=dma((2, chunks)),
        line_recv=dma((2, 2, chunks)),
        out_sem=dma((5,)),
        stat_sem=dma((2, bits + 1)),
    )
    outs = dict(
        outputs=((2, rows, model), BF16),
        input_grads=((2, rows, model), F32),
        qkv_sums=((3, part, width), F32),
        out_sums=((width, part), F32),
        up_sums=((part, units), F32),
        down_sums=((units, part), F32),
        row_sums=((6, part // line), F32),
        qv_sums=((2, heads, sizes["head_size"] // dp_count), F32),
        shift_sums=(arrays["up_bias"].shape, F32),
    )
    far = ("block_rows", "upstream_rows", "qkv_own", "out_own", "up_own", "down_own")
    names = list(arrays) + list(outs) + list(scratch)
    return pl.pallas_call(
        functools.partial(layers_kernel, dict(sizes, names=names)),
        out_shape=[jax.ShapeDtypeStruct(shape, kind) for shape, kind in outs.values()],
        in_specs=[ANY_SPEC if name in far else VMEM_SPEC for name in arrays],
        out_specs=[VMEM_SPEC] * len(outs),
        scratch_shapes=list(scratch.values()),
        compiler_params=pltpu.CompilerParams(
            collective_id=1, has_side_effects=True, vmem_limit_bytes=VMEM_LIMIT
        ),
        name="both_layers",
    )(*arrays.values())


def shards(
    block_input,
    seq_ids,
    out_cotangent,
    qkv_weight,
    qv_bias,
    out_weight,
    out_bias,
    norm1_gain,
    norm1_bias,
    up_weight,
    up_bias,
    down_weight,
    down_bias,
    norm2_gain,
    norm2_bias,
):
    dp_count = lax.axis_size("dp")
    line = lax.axis_size("tensor")
    heads, head_part = qv_bias.shape[2], qv_bias.shape[3]
    part = out_bias.shape[1]
    width = qkv_weight.shape[3]
    model = block_input.shape[3]
    units = up_weight.shape[2]
    sizes = dict(
        line=line,
        dp_count=dp_count,
        part=part,
        width=width,
        rows=block_input.shape[2],
        model=model,
        units=units,
        heads=heads,
        head_size=head_part * dp_count,
    )
    arrays = dict(
        block_rows=block_input[:, 0],
        upstream_rows=out_cotangent[:, 0],
        ids=seq_ids,
        qkv_own=qkv_weight[0].reshape(part, 3 * width),
        out_own=out_weight[0],
        up_own=up_weight[0],
        down_own=down_weight[0],
        out_bias=out_bias,
        gain_one=norm1_gain,
        bias_one=norm1_bias,
        down_bias=down_bias,
        gain_two=norm2_gain,
        bias_two=norm2_bias,
        qv_bias=qv_bias[0],
        up_bias=up_bias[0],
    )
    results = both_layers(arrays, sizes)
    outputs, input_grads, qkv_sums, out_sums, up_sums, down_sums, rows, qv_sums, shift_sums = results
    return (
        outputs[None, :, None],
        input_grads[None, :, None],
        jnp.swapaxes(qkv_sums, 0, 1)[None],
        qv_sums[None],
        out_sums[None],
        rows[0][None],
        rows[1][None],
        rows[2][None],
        up_sums[None],
        shift_sums[None],
        down_sums[None],
        rows[3][None],
        rows[4][None],
        rows[5][None],
    )


def solution(mesh):
    return jax.shard_map(
        shards,
        mesh=mesh,
        in_specs=(
            P(None, "dp", "tensor", None),
            P(None, "dp", None),
            P(None, "dp", "tensor", None),
            P("section", "dp", None, "tensor"),
            P("section", None, "tensor", "dp"),
            P("section", "tensor", "dp"),
            P("section", "dp"),
            P("section", "dp"),
            P("section", "dp"),
            P("section", "dp", "tensor"),
            P("section", "tensor", "dp"),
            P("section", "tensor", "dp"),
            P("section", "dp"),
            P("section", "dp"),
            P("section", "dp"),
        ),
        out_specs=(
            P("section", None, "dp", "tensor", None),
            P("section", None, "dp", "tensor", None),
            P("section", "dp", None, "tensor"),
            P("section", None, "tensor", "dp"),
            P("section", "tensor", "dp"),
            P("section", ("dp", "tensor")),
            P("section", ("dp", "tensor")),
            P("section", ("dp", "tensor")),
            P("section", "dp", "tensor"),
            P("section", "tensor", "dp"),
            P("section", "tensor", "dp"),
            P("section", ("dp", "tensor")),
            P("section", ("dp", "tensor")),
            P("section", ("dp", "tensor")),
        ),
        check_vma=False,
    )
```

```python
import functools

import jax
import jax.numpy as jnp
from jax import lax
from jax.experimental import pallas as pl
from jax.experimental.pallas import tpu as pltpu
from jax.sharding import PartitionSpec as P

MESH = pl.DeviceIdType.MESH
F32 = jnp.float32
BF16 = jnp.bfloat16
VMEM_SPEC = pl.BlockSpec(memory_space=pltpu.VMEM)
ANY_SPEC = pl.BlockSpec(memory_space=pl.ANY)
VMEM_LIMIT = 63 * 1024 * 1024
CHUNK = 32
AHEAD = 3
QUARTERS = 4
SLABS = 3
PIECES = SLABS * QUARTERS
STATS = 8
BLOCK = 256
VECTORS = ("out_bias", "gain_one", "bias_one", "down_bias", "gain_two", "bias_two")

ERF_TOP = (
    0.00022905065861350646,
    0.0034082910107109506,
    0.050955695062380861,
    0.18520832239976145,
    1.128379143519084,
)
ERF_BELOW = (
    -1.1791602954361697e-7,
    0.000023547966471313185,
    0.0010179625278914885,
    0.014070470171167667,
    0.11098505178285362,
    0.49746925110067538,
    1.0,
)


def erf(values):
    x = jnp.clip(values, -3.832506856900711, 3.832506856900711)
    square = x * x
    top = jnp.full_like(square, ERF_TOP[0])
    for term in ERF_TOP[1:]:
        top = top * square + term
    below = jnp.full_like(square, ERF_BELOW[0])
    for term in ERF_BELOW[1:]:
        below = below * square + term
    return x * top / below


def nn(a, b):
    return lax.dot_general(a, b, (((1,), (0,)), ((), ())), preferred_element_type=F32)


def nt(a, b):
    return lax.dot_general(a, b, (((1,), (1,)), ((), ())), preferred_element_type=F32)


def tn(a, b):
    return lax.dot_general(a, b, (((0,), (0,)), ((), ())), preferred_element_type=F32)


def loop(count, body):
    def one(index, carry):
        body(index)
        return carry

    lax.fori_loop(0, count, one, 0)


def span(index, size):
    return pl.ds(pl.multiple_of(index * size, size), size)


def mean(values):
    return jnp.mean(values, axis=-1, keepdims=True)


def normalize(summed):
    center = summed - mean(summed)
    scaled = lax.rsqrt(mean(center * center) + 1e-12)
    return center * scaled, scaled


def norm_back(upstream, normed, scaled):
    return scaled * (upstream - mean(upstream) - normed * mean(upstream * normed))


def low_bit(mask):
    return (mask & -mask).bit_length() - 1


class Layers:
    def __init__(self, sizes, refs):
        for name, ref in zip(sizes["names"], refs):
            setattr(self, name, ref)
        self.vectors = [getattr(self, name) for name in VECTORS]
        self.line = sizes["line"]
        self.dp_count = sizes["dp_count"]
        self.bits = self.dp_count.bit_length() - 1
        self.part = sizes["part"]
        self.width = sizes["width"]
        self.rows = sizes["rows"]
        self.tokens = self.line * self.rows
        self.model = sizes["model"]
        self.units = sizes["units"]
        self.heads = sizes["heads"]
        self.head_size = sizes["head_size"]
        self.chunks = self.tokens // CHUNK
        self.quarter = self.part // QUARTERS
        self.section = lax.axis_index("section")
        self.dp = lax.axis_index("dp")
        self.me = lax.axis_index("tensor")
        self.nears = self.me // (self.line // 2)
        self.fars = 1 - self.nears
        self.middle = jnp.logical_and(self.me > 0, self.me < self.line - 1)
        self.own_rows = span(self.me, self.rows)
        self.passes = 0


    def place(self, mask):
        dp = self.dp
        for bit in range(self.bits):
            if mask & (1 << bit):
                dp = dp + (1 << bit) * (1 - 2 * ((self.dp // (1 << bit)) % 2))
        return dp

    def neighbour(self, bit):
        return {"dp": self.place(1 << bit)}

    def across(self):
        return {"section": 1 - self.section}

    def line_peer(self, step):
        return lax.rem(self.me + step, self.line)

    def remote(self, src, dst, send_sem, recv_sem, device):
        return pltpu.make_async_remote_copy(
            src_ref=src,
            dst_ref=dst,
            send_sem=send_sem,
            recv_sem=recv_sem,
            device_id=device,
            device_id_type=MESH,
        )

    def greet(self):
        barrier = pltpu.get_barrier_semaphore()
        targets = [{"tensor": self.line_peer(step)} for step in range(1, self.line)]
        targets += [self.neighbour(bit) for bit in range(self.bits)] + [self.across()]
        for target in targets:
            pl.semaphore_signal(barrier, inc=1, device_id=target, device_id_type=MESH)
        pl.semaphore_wait(barrier, len(targets))


    def rows_copy(self, which, source, target, step):
        return self.remote(
            source.at[self.section],
            target.at[self.own_rows],
            self.rows_send.at[which, step - 1],
            self.rows_recv.at[which, step - 1],
            {"tensor": self.line_peer(step)},
        )

    def rows_local(self, which, source, target):
        return pltpu.make_async_copy(
            source.at[self.section], target.at[self.own_rows], self.rows_own.at[which]
        )

    def rows_start(self, which, source, target):
        for step in range(1, self.line):
            self.rows_copy(which, source, target, step).start()
        self.rows_local(which, source, target).start()

    def rows_wait(self, which, source, target):
        self.rows_local(which, source, target).wait()
        for step in range(1, self.line):
            self.rows_copy(which, source, target, step).wait_recv()


    def weight_slot(self, s, p, mask):
        if p is None:
            return self.small_all.at[s, self.place(mask)]
        return self.weights.at[s, p // QUARTERS, self.piece_rows(p, mask)]

    def piece_rows(self, p, mask):
        at = self.place(mask) * self.part + (p % QUARTERS) * self.quarter
        return pl.ds(pl.multiple_of(at, self.quarter), self.quarter)

    def weight_copy(self, s, p, held, bit):
        number = PIECES if p is None else p
        mask = held | (1 << bit)
        return self.remote(
            self.weight_slot(s, p, held),
            self.weight_slot(s, p, held),
            self.weight_send.at[s, number, mask],
            self.weight_recv.at[s, number, mask],
            self.neighbour(bit),
        )

    def weight_arrival(self, s, p, mask):
        number = PIECES if p is None else p
        return self.remote(
            self.weight_slot(s, p, mask),
            self.weight_slot(s, p, mask),
            self.weight_send.at[s, number, mask],
            self.weight_recv.at[s, number, mask],
            self.neighbour(low_bit(mask)),
        )

    def weight_across(self, s, p):
        number = PIECES if p is None else p
        return self.remote(
            self.weight_slot(s, p, 0),
            self.weight_slot(s, p, 0),
            self.weight_send.at[s, number, 0],
            self.weight_recv.at[s, number, 0],
            self.across(),
        )

    def weight_forward(self, s, p, held):
        top = self.bits if held == 0 else low_bit(held)
        for bit in reversed(range(top)):
            self.weight_copy(s, p, held, bit).start()

    def weight_offer(self, s, p):
        self.weight_across(s, p).start()
        self.weight_forward(s, p, 0)

    def weights_offer(self, s, first, last):
        @pl.when(self.section == s)
        def _():
            loop(last - first, lambda p: self.weight_offer(s, first + p))

    def small_offer(self, s):
        @pl.when(self.section == s)
        def _():
            self.weight_offer(s, None)

    def weights_cross(self, s, p):
        @pl.when(self.section != s)
        def _():
            self.weight_across(s, p).wait_recv()
            self.weight_forward(s, p, 0)

    def weights_relay(self, s, p):
        for bit in reversed(range(1, self.bits)):
            for mask in range(self.dp_count):
                if mask and low_bit(mask) == bit:
                    self.weight_arrival(s, p, mask).wait_recv()
                    self.weight_forward(s, p, mask)

    def weights_land(self, s, p):
        for mask in range(1, self.dp_count, 2):
            self.weight_arrival(s, p, mask).wait_recv()

    def weights_sent(self, s, p):
        for mask in range(1, self.dp_count):
            held = mask & (mask - 1)
            self.weight_copy(s, p, held, low_bit(mask)).wait_send()

        @pl.when(self.section == s)
        def _():
            self.weight_across(s, p).wait_send()


    def grad_slot(self, s, p, mask):
        return self.grads.at[s, p // QUARTERS, self.piece_rows(p, mask)]

    def grad_landed(self, s, p, mask):
        at = mask * self.part + (p % QUARTERS) * self.quarter
        rows = pl.ds(pl.multiple_of(at, self.quarter), self.quarter)
        return self.landed.at[s, p // QUARTERS, rows]

    def grad_copy(self, s, p, mask):
        device = self.neighbour(low_bit(mask)) if mask else self.across()
        return self.remote(
            self.grad_slot(s, p, mask),
            self.grad_landed(s, p, mask),
            self.grad_send.at[s, p, mask],
            self.grad_recv.at[s, p, mask],
            device,
        )

    def grad_total(self, s, p, mask, last=False):
        total = self.grad_slot(s, p, mask)[...].astype(F32)
        for bit in range(low_bit(mask) if mask else self.bits):
            self.grad_copy(s, p, mask | (1 << bit)).wait_recv()
            total = total + self.grad_landed(s, p, mask | (1 << bit))[...].astype(F32)
        return total

    def grads_offer(self, s, p):
        for mask in range(1, self.dp_count, 2):
            self.grad_copy(s, p, mask).start()

    def grads_fold(self, s, p):
        for bit in range(1, self.bits):
            for mask in range(self.dp_count):
                if mask and low_bit(mask) == bit:
                    self.grad_slot(s, p, mask)[...] = self.grad_total(s, p, mask).astype(BF16)
                    self.grad_copy(s, p, mask).start()

    def grads_cross(self, s, p):
        @pl.when(self.section != s)
        def _():
            self.grad_slot(s, p, 0)[...] = self.grad_total(s, p, 0).astype(BF16)
            self.grad_copy(s, p, 0).start()

    def grads_end(self, s, p):
        @pl.when(self.section == s)
        def _():
            total = self.grad_total(s, p, 0)
            self.grad_copy(s, p, 0).wait_recv()
            total = total + self.grad_landed(s, p, 0)[...].astype(F32)
            rows = span(p % QUARTERS, self.quarter)
            slab = p // QUARTERS

            @pl.when(slab == 0)
            def _():
                for which in range(3):
                    at = slice(which * self.width, (which + 1) * self.width)
                    self.qkv_sums[which, rows] = total[:, at]
                self.out_turned[rows] = total[:, 3 * self.width :]

            @pl.when(slab == 1)
            def _():
                self.up_sums[rows] = total

            @pl.when(slab == 2)
            def _():
                self.down_turned[rows] = total

    def grads_sent(self, s, p):
        for mask in range(1, self.dp_count):
            self.grad_copy(s, p, mask).wait_send()

        @pl.when(self.section != s)
        def _():
            self.grad_copy(s, p, 0).wait_send()


    def line_copy(self, half, side, chunk, target):
        rows = span(chunk, CHUNK)
        return self.remote(
            self.staged.at[side, rows],
            self.sums.at[half, side, rows],
            self.line_send.at[side, chunk],
            self.line_recv.at[half, side, chunk],
            {"tensor": target},
        )

    def line_sum(self, finish, tick):
        number = self.passes
        half = number % 2
        self.passes += 1
        near_target = self.me + 1 - 2 * self.nears
        far_target = self.me - 1 + 2 * self.nears

        def send(side, chunk, target):
            rows = span(chunk, CHUNK)
            if number > 0:
                self.line_copy(half, side, chunk, target).wait_send()
            total = self.partial[rows] + self.sums[half, side, rows].astype(F32)
            self.staged[side, rows] = total.astype(BF16)
            self.line_copy(half, side, chunk, target).start()

        def near(chunk):
            @pl.when(self.middle)
            def _():
                self.line_copy(half, self.nears, chunk, near_target).wait_recv()

            send(self.nears, chunk, near_target)

        ahead = jnp.where(self.middle, AHEAD, self.chunks)
        loop(ahead, near)

        def body(chunk):
            @pl.when(chunk + ahead < self.chunks)
            def _():
                near(chunk + ahead)

            self.line_copy(half, self.fars, chunk, near_target).wait_recv()

            @pl.when(self.middle)
            def _():
                send(self.fars, chunk, far_target)

            rows = span(chunk, CHUNK)
            total = (
                self.partial[rows]
                + self.sums[half, 0, rows].astype(F32)
                + self.sums[half, 1, rows].astype(F32)
            )
            finish(rows, total)
            tick(chunk)

        loop(self.chunks, body)

    def line_sent(self):
        def one(chunk):
            self.line_copy(0, self.nears, chunk, self.me + 1 - 2 * self.nears).wait_send()

            @pl.when(self.middle)
            def _():
                self.line_copy(0, self.fars, chunk, self.me - 1 + 2 * self.nears).wait_send()

        loop(self.chunks, one)

    def clear(self):
        for half in range(2):
            for side, end in ((0, 0), (1, self.line - 1)):

                @pl.when(self.me == end)
                def _():
                    self.sums[half, side] = jnp.zeros(self.sums.shape[2:], BF16)

        self.stats[...] = jnp.zeros(self.stats.shape, F32)
        row = jnp.broadcast_to(self.ids[self.section], (self.tokens, self.tokens))
        self.hidden_pairs[...] = jnp.where(row == row.T, 0.0, -1e30)


    def param(self, s, row):
        return self.params[s, row : row + 1]

    def count_stat(self, s, row, values):
        folded = values.reshape(values.shape[0] // 8, 8, values.shape[1])
        self.stats[s, row] += jnp.sum(folded, axis=0)

    def attention(self, s):
        width = self.width
        for block in range(3):
            at = slice(block * width, (block + 1) * width)
            made = nn(self.inputs[s], self.weights[s, 0, :, at])
            if block != 1:
                low = 0 if block == 0 else width
                made = made + self.params[s, 6:7, low : low + width]
            self.qkv[s, :, at] = made.astype(BF16)
        contexts = []
        for head in range(self.heads):
            query, key, value = self.head_parts(s, head)
            scores = nt(query, key) * self.head_size ** (-0.5) + self.hidden_pairs[...]
            shifted = jnp.exp(scores - jnp.max(scores, axis=-1, keepdims=True))
            prob = shifted / jnp.sum(shifted, axis=-1, keepdims=True)
            prob = prob.astype(BF16)
            self.probs[s, head] = prob
            contexts.append(nn(prob, value).astype(BF16))
        self.context[s] = jnp.concatenate(contexts, axis=1)

        def project(block):
            at = span(block, BLOCK)
            self.partial[:, at] = nt(self.context[s], self.weights[s, 0, at, 3 * width :])

        loop(self.model // BLOCK, project)

    def head_parts(self, s, head):
        size = self.head_size
        low = head * size
        return [
            self.qkv[s, :, which * self.width + low : which * self.width + low + size]
            for which in range(3)
        ]

    def feed_up(self, s):
        def block_of(block):
            at = span(block, BLOCK)
            self.partial[:, at] = nn(self.hidden[s], self.weights[s, 1, :, at])

        loop(self.units // BLOCK, block_of)

        def gelu(step):
            rows = span(step, 16)
            pre = self.partial[rows] + self.param(s, 7)
            half = 0.5 * (1.0 + erf(pre * 0.7071067811865476))
            self.active[s, rows] = (pre * half).astype(BF16)
            bell = pre * jnp.exp(-0.5 * pre * pre) * 0.3989422804014327
            self.slope[s, rows] = (half + bell).astype(BF16)

        loop(self.tokens // 16, gelu)

    def feed_down(self, s):
        def block_of(block):
            at = span(block, BLOCK)
            self.partial[:, at] = nt(self.active[s], self.weights[s, 2, at])

        loop(self.model // BLOCK, block_of)

    def after_attention(self, s):
        def finish(rows, total):
            summed = self.inputs[s, rows].astype(F32) + total + self.param(s, 0)
            normed, scaled = normalize(summed)
            self.normed_one[s, rows] = normed.astype(BF16)
            self.scaled_one[s, rows] = jnp.broadcast_to(scaled, (CHUNK, 128))
            hidden = normed * self.param(s, 1) + self.param(s, 2)
            self.wide[rows] = hidden
            self.hidden[s, rows] = hidden.astype(BF16)

        return finish

    def after_feed(self, s):
        def finish(rows, total):
            summed = self.wide[rows] + total + self.param(s, 3)
            normed, scaled = normalize(summed)
            out = normed * self.param(s, 4) + self.param(s, 5)
            self.inputs[s + 1, rows] = out.astype(BF16)
            if s == 0:
                self.normed_two[rows] = normed.astype(BF16)
                self.scaled_two[rows] = jnp.broadcast_to(scaled, (CHUNK, 128))
            else:
                self.start_back(s, rows, self.grad_one_held[rows].astype(F32), normed, scaled)

        return finish

    def start_back(self, s, rows, upstream, normed, scaled):
        grad_two = norm_back(upstream * self.param(s, 4), normed, scaled)
        self.wide[rows] = grad_two
        self.grad_two_held[rows] = grad_two.astype(BF16)
        self.count_stat(s, 3, grad_two)
        self.count_stat(s, 4, upstream * normed)
        self.count_stat(s, 5, upstream)

    def feed_back(self, s):
        def block_of(block):
            at = span(block, BLOCK)
            self.partial[:, at] = nn(self.grad_two_held[...], self.weights[s, 2, :, at])

        loop(self.units // BLOCK, block_of)

        def slopes(step):
            rows = span(step, 16)
            grad_pre = self.partial[rows] * self.slope[s, rows].astype(F32)
            self.grad_pre[rows] = grad_pre.astype(BF16)
            self.count_stat(s, 7, grad_pre)

        loop(self.tokens // 16, slopes)

        def up_of(block):
            at = span(block, BLOCK)
            self.partial[:, at] = nt(self.grad_pre[...], self.weights[s, 1, at])

        loop(self.model // BLOCK, up_of)

    def after_feed_back(self, s):
        def finish(rows, total):
            grad_hidden = self.wide[rows] + total
            normed = self.normed_one[s, rows].astype(F32)
            scaled = self.scaled_one[s, rows][:, :1]
            grad_one = norm_back(grad_hidden * self.param(s, 1), normed, scaled)
            self.grad_wide[rows] = grad_one
            self.grad_one_held[rows] = grad_one.astype(BF16)
            self.count_stat(s, 0, grad_one)
            self.count_stat(s, 1, grad_hidden * normed)
            self.count_stat(s, 2, grad_hidden)

        return finish

    def feed_grads(self, s, step):
        cuts = self.chunks // 2
        block = step // 2
        size = self.model // cuts
        at = span(block, size)

        @pl.when(step % 2 == 0)
        def _():
            made = tn(self.grad_two_held[:, at], self.active[s])
            self.grads[s, 2, at] = made.astype(BF16)

        @pl.when(step % 2 == 1)
        def _():
            made = tn(self.hidden[s, :, at], self.grad_pre[...])
            self.grads[s, 1, at] = made.astype(BF16)

    def attention_grads(self, s, step):
        cuts = self.chunks // 2
        block = step // 2
        size = self.model // cuts
        at = span(block, size)

        @pl.when(step % 2 == 0)
        def _():
            made = tn(self.inputs[s, :, at], self.grad_qkv[...])
            self.grads[s, 0, at, : 3 * self.width] = made.astype(BF16)

        @pl.when(step % 2 == 1)
        def _():
            made = tn(self.grad_one_held[:, at], self.context[s])
            self.grads[s, 0, at, 3 * self.width :] = made.astype(BF16)

    def attention_back(self, s):
        width, size = self.width, self.head_size
        grad_context = nn(self.grad_one_held[...], self.weights[s, 0, :, 3 * width :])
        self.grad_context[...] = grad_context.astype(BF16)
        parts = [[], [], []]
        for head in range(self.heads):
            query, key, value = self.head_parts(s, head)
            above = self.grad_context[:, head * size : (head + 1) * size]
            held = self.probs[s, head]
            prob = held.astype(F32)
            grad_prob = nt(above, value)
            dots = jnp.sum(prob * grad_prob, axis=-1, keepdims=True)
            grad_scores = (prob * (grad_prob - dots) * size ** (-0.5)).astype(BF16)
            parts[0].append(nn(grad_scores, key))
            parts[1].append(tn(grad_scores, query))
            parts[2].append(tn(held, above))
        for which in range(3):
            made = jnp.concatenate(parts[which], axis=1)
            self.grad_qkv[:, which * width : (which + 1) * width] = made.astype(BF16)
            if which != 1:
                folded = jnp.sum(made.reshape(self.tokens // 8, 8, width), axis=0)
                low = 0 if which == 0 else width
                self.stats[s, 6, :, low : low + width] = folded

        def block_of(block):
            at = span(block, BLOCK)
            self.partial[:, at] = nt(self.grad_qkv[...], self.weights[s, 0, at, : 3 * width])

        loop(self.model // BLOCK, block_of)

    def after_attention_back(self, s):
        def finish(rows, total):
            upstream = self.grad_wide[rows] + total
            self.grad_wide[rows] = upstream
            if s == 1:
                normed = self.normed_two[rows].astype(F32)
                self.start_back(0, rows, upstream, normed, self.scaled_two[rows][:, :1])

        return finish


    def output_copy(self, s, local):
        source = self.inputs.at[s + 1, self.own_rows]
        target = self.outputs.at[self.section]
        if local:
            return pltpu.make_async_copy(source, target, self.out_sem.at[0])
        return self.remote(source, target, self.out_sem.at[1], self.out_sem.at[2], self.across())

    def output_start(self, s):
        for local in (True, False):

            @pl.when((self.section == s) if local else (self.section != s))
            def _():
                self.output_copy(s, local).start()

    def input_grad_copy(self):
        return self.remote(
            self.input_grad_staged,
            self.input_grad_landed,
            self.out_sem.at[3],
            self.out_sem.at[4],
            self.across(),
        )

    def input_grad_start(self, s):
        @pl.when(self.section == s)
        def _():
            self.input_grads[self.section] = self.grad_wide[self.own_rows]

        @pl.when(self.section != s)
        def _():
            self.input_grad_staged[...] = self.grad_wide[self.own_rows].astype(BF16)
            self.input_grad_copy().start()

    def outputs_end(self):
        self.output_copy(0, True).wait()
        self.output_copy(0, False).wait()
        self.input_grad_copy().wait()
        self.input_grads[1 - self.section] = self.input_grad_landed[...].astype(F32)


    def stat_copy(self, step):
        return self.remote(
            self.stat_sums.at[step],
            self.stat_landed.at[step],
            self.stat_sem.at[0, step],
            self.stat_sem.at[1, step],
            self.neighbour(step) if step < self.bits else self.across(),
        )

    def stat_step(self, step):
        self.stat_copy(step).wait_recv()
        self.stat_sums[step + 1] = self.stat_sums[step] + self.stat_landed[step]
        if step < self.bits:
            self.stat_copy(step + 1).start()


    def spread_small(self):
        model, dp_count = self.model, self.dp_count
        place = lax.broadcasted_iota(jnp.int32, (1, model), 1) // self.part
        rows = []
        for ref in self.vectors:
            tiled = jnp.concatenate([ref[...].astype(F32)] * dp_count, axis=1)
            rows.append(jnp.where(place == self.dp, tiled, 0.0))

        def spread(values):
            size = values.shape[1]
            shape = (size, size * dp_count)
            low = lax.broadcasted_iota(jnp.int32, shape, 0) + self.dp * size
            chosen = jnp.where(lax.broadcasted_iota(jnp.int32, shape, 1) == low, 1.0, 0.0)
            return nn(values.astype(BF16), chosen.astype(BF16))

        query, value = spread(self.qv_bias[0]), spread(self.qv_bias[1])
        pieces = [query[head : head + 1] for head in range(self.heads)]
        pieces += [value[head : head + 1] for head in range(self.heads)]
        pieces.append(jnp.zeros((1, model - 2 * self.width), F32))
        rows.append(jnp.concatenate(pieces, axis=1))
        above = spread(self.up_bias[...])
        rows.append(
            jnp.concatenate([above[group : group + 1] for group in range(above.shape[0])], axis=1)
        )
        self.small_all[self.section, self.dp] = jnp.concatenate(rows, axis=0)

    def small_outputs(self):
        total = self.stat_sums[self.bits + 1, self.section]
        model = self.model

        def turned(offset):
            return pltpu.roll(total, lax.rem(model - offset, model), 1)

        share = self.part // self.line
        self.row_sums[...] = turned(self.dp * self.part + self.me * share)[:6, :share]
        size = self.head_size // self.dp_count
        moved = turned(self.dp * size)
        for which in range(2):
            for head in range(self.heads):
                low = which * self.width + head * self.head_size
                self.qv_sums[which, head : head + 1] = moved[6:7, low : low + size]
        groups, size = self.shift_sums.shape
        moved = turned(self.dp * size)
        for group in range(groups):
            low = group * size * self.dp_count
            self.shift_sums[group : group + 1] = moved[7:8, low : low + size]

    def own_copies(self):
        mine = pl.ds(pl.multiple_of(self.dp * self.part, self.part), self.part)
        here = self.weights.at[self.section]
        pairs = [
            (self.qkv_own, here.at[0, mine, pl.ds(0, 3 * self.width)]),
            (self.out_own, self.out_raw),
            (self.up_own, here.at[1, mine]),
            (self.down_own, self.down_raw),
        ]
        return [
            pltpu.make_async_copy(source, target, self.own_sem.at[number])
            for number, (source, target) in enumerate(pairs)
        ]

    def run(self):
        def nothing(step):
            pass

        copies = self.own_copies()
        for copy in copies:
            copy.start()
        self.greet()
        self.rows_start(0, self.block_rows, self.inputs.at[0])
        mine = pl.ds(pl.multiple_of(self.dp * self.part, self.part), self.part)
        copies[0].wait()
        copies[1].wait()
        self.weights[self.section, 0, mine, 3 * self.width :] = self.out_raw[...].T
        self.weights_offer(0, 0, QUARTERS)
        self.spread_small()
        self.small_offer(0)
        copies[2].wait()
        copies[3].wait()
        self.weights[self.section, 2, mine] = self.down_raw[...].T
        self.weights_offer(0, QUARTERS, PIECES)
        self.clear()
        for p in range(QUARTERS + 1):
            if p < QUARTERS:
                self.weights_cross(0, p)
            if p == 1:
                self.weights_cross(0, None)
            if p == 2:
                self.weights_relay(0, None)
            if p > 0:
                self.weights_relay(0, p - 1)
        self.weights_land(0, None)
        loop(QUARTERS, functools.partial(self.weights_land, 0))
        self.params[0] = jnp.sum(self.small_all[0], axis=0)
        self.rows_wait(0, self.block_rows, self.inputs.at[0])
        self.rows_start(1, self.upstream_rows, self.grad_one_held)

        self.attention(0)

        def first_tick(step):
            self.weights_cross(0, QUARTERS + step)

            @pl.when(step > 0)
            def _():
                self.weights_relay(0, QUARTERS + step - 1)

        self.line_sum(self.after_attention(0), first_tick)
        self.weights_relay(0, PIECES - 1)
        self.small_offer(1)
        self.weights_offer(1, 0, PIECES)
        loop(QUARTERS, lambda p: self.weights_land(0, QUARTERS + p))
        self.feed_up(0)
        loop(QUARTERS, lambda p: self.weights_land(0, 2 * QUARTERS + p))
        self.feed_down(0)

        def second_tick(step):
            @pl.when(step == 0)
            def _():
                self.weights_cross(1, None)

            @pl.when(step == 1)
            def _():
                self.weights_relay(1, None)

            self.weights_cross(1, step)

            @pl.when(step > 0)
            def _():
                self.weights_relay(1, step - 1)

        self.line_sum(self.after_feed(0), second_tick)
        self.output_start(0)
        self.weights_land(1, None)
        loop(QUARTERS, functools.partial(self.weights_land, 1))
        self.params[1] = jnp.sum(self.small_all[1], axis=0)

        self.attention(1)

        def third_tick(step):
            @pl.when(step < QUARTERS)
            def _():
                self.weights_cross(1, 2 * QUARTERS + step)

            @pl.when(step <= QUARTERS)
            def _():
                self.weights_relay(1, 2 * QUARTERS + step - 1)

        self.line_sum(self.after_attention(1), third_tick)
        loop(QUARTERS, lambda p: self.weights_land(1, QUARTERS + p))
        self.feed_up(1)
        loop(QUARTERS, lambda p: self.weights_land(1, 2 * QUARTERS + p))
        self.feed_down(1)
        self.rows_wait(1, self.upstream_rows, self.grad_one_held)
        self.line_sum(self.after_feed(1), nothing)
        self.output_start(1)

        def turn(order):
            return (SLABS - 1 - order // QUARTERS) * QUARTERS + order % QUARTERS

        def service(s, action, order):
            @pl.when(jnp.logical_and(order >= 0, order < PIECES))
            def _():
                action(s, turn(order))

        self.feed_back(1)
        self.line_sum(self.after_feed_back(1), functools.partial(self.feed_grads, 1))
        loop(2 * QUARTERS, lambda order: self.grads_offer(1, turn(order)))
        self.attention_back(1)

        def fourth_tick(step):
            self.attention_grads(1, step)
            service(1, self.grads_fold, step)
            service(1, self.grads_cross, step - 2)
            service(1, self.grads_end, step - 4)

        self.line_sum(self.after_attention_back(1), fourth_tick)
        loop(QUARTERS, lambda q: self.grads_offer(1, q))
        self.input_grad_start(1)
        self.feed_back(0)

        def fifth_tick(step):
            self.feed_grads(0, step)
            service(1, self.grads_fold, step + 8)
            service(1, self.grads_cross, step + 6)
            service(1, self.grads_end, step + 4)

        self.line_sum(self.after_feed_back(0), fifth_tick)
        loop(2 * QUARTERS, lambda order: self.grads_offer(0, turn(order)))
        self.attention_back(0)
        self.stat_sums[0] = jnp.sum(self.stats[...], axis=2)
        self.stat_copy(0).start()

        def sixth_tick(step):
            self.attention_grads(0, step)
            for number in range(self.bits + 1):

                @pl.when(step == min(2 * number + 2, self.chunks - 1))
                def _():
                    self.stat_step(number)

            service(0, self.grads_fold, step)
            service(0, self.grads_cross, step - 2)
            service(0, self.grads_end, step - 4)

        self.line_sum(self.after_attention_back(0), sixth_tick)
        loop(QUARTERS, lambda q: self.grads_offer(0, q))
        self.input_grad_start(0)

        def last_tick(step):
            service(0, self.grads_fold, step + 8)
            service(0, self.grads_cross, step + 6)
            service(0, self.grads_end, step + 4)

        loop(8, last_tick)
        self.small_outputs()
        self.out_sums[...] = self.out_turned[...].T
        self.down_sums[...] = self.down_turned[...].T
        self.outputs_end()

        for which, source, target in (
            (0, self.block_rows, self.inputs.at[0]),
            (1, self.upstream_rows, self.grad_one_held),
        ):
            for step in range(1, self.line):
                self.rows_copy(which, source, target, step).wait_send()
        self.line_sent()
        for s in range(2):
            self.weights_sent(s, None)
            loop(PIECES, functools.partial(self.weights_sent, s))
            loop(PIECES, functools.partial(self.grads_sent, s))
        for step in range(self.bits + 1):
            self.stat_copy(step).wait_send()


def layers_kernel(sizes, *refs):
    Layers(sizes, refs).run()


def both_layers(arrays, sizes):
    line, dp_count, part = sizes["line"], sizes["dp_count"], sizes["part"]
    rows, width, model, units = sizes["rows"], sizes["width"], sizes["model"], sizes["units"]
    heads = sizes["heads"]
    tokens = line * rows
    chunks = tokens // CHUNK
    bits = dp_count.bit_length() - 1
    dma = pltpu.SemaphoreType.DMA
    vmem = pltpu.VMEM
    scratch = dict(
        inputs=vmem((3, tokens, model), BF16),
        weights=vmem((2, SLABS, model, units), BF16),
        grads=vmem((2, SLABS, model, units), BF16),
        landed=vmem((2, SLABS, model, units), BF16),
        small_all=vmem((2, dp_count, STATS, model), F32),
        params=vmem((2, STATS, model), F32),
        sums=vmem((2, 2, tokens, model), BF16),
        staged=vmem((2, tokens, model), BF16),
        partial=vmem((tokens, model), F32),
        wide=vmem((tokens, model), F32),
        grad_wide=vmem((tokens, model), F32),
        normed_one=vmem((2, tokens, model), BF16),
        normed_two=vmem((tokens, model), BF16),
        scaled_one=vmem((2, tokens, 128), F32),
        scaled_two=vmem((tokens, 128), F32),
        hidden=vmem((2, tokens, model), BF16),
        active=vmem((2, tokens, units), BF16),
        slope=vmem((2, tokens, units), BF16),
        qkv=vmem((2, tokens, 3 * width), BF16),
        probs=vmem((2, heads, tokens, tokens), BF16),
        context=vmem((2, tokens, width), BF16),
        grad_two_held=vmem((tokens, model), BF16),
        grad_one_held=vmem((tokens, model), BF16),
        grad_pre=vmem((tokens, units), BF16),
        grad_context=vmem((tokens, width), BF16),
        grad_qkv=vmem((tokens, 3 * width), BF16),
        hidden_pairs=vmem((tokens, tokens), F32),
        stats=vmem((2, STATS, 8, model), F32),
        stat_sums=vmem((bits + 2, 2, STATS, model), F32),
        stat_landed=vmem((bits + 1, 2, STATS, model), F32),
        input_grad_staged=vmem((rows, model), BF16),
        input_grad_landed=vmem((rows, model), BF16),
        out_raw=vmem((width, part), BF16),
        down_raw=vmem((units, part), BF16),
        out_turned=vmem((part, width), F32),
        down_turned=vmem((part, units), F32),
        rows_send=dma((2, line - 1)),
        rows_recv=dma((2, line - 1)),
        rows_own=dma((2,)),
        own_sem=dma((4,)),
        weight_send=dma((2, PIECES + 1, dp_count)),
        weight_recv=dma((2, PIECES + 1, dp_count)),
        grad_send=dma((2, PIECES, dp_count)),
        grad_recv=dma((2, PIECES, dp_count)),
        line_send=dma((2, chunks)),
        line_recv=dma((2, 2, chunks)),
        out_sem=dma((5,)),
        stat_sem=dma((2, bits + 1)),
    )
    outs = dict(
        outputs=((2, rows, model), BF16),
        input_grads=((2, rows, model), F32),
        qkv_sums=((3, part, width), F32),
        out_sums=((width, part), F32),
        up_sums=((part, units), F32),
        down_sums=((units, part), F32),
        row_sums=((6, part // line), F32),
        qv_sums=((2, heads, sizes["head_size"] // dp_count), F32),
        shift_sums=(arrays["up_bias"].shape, F32),
    )
    far = ("block_rows", "upstream_rows", "qkv_own", "out_own", "up_own", "down_own")
    names = list(arrays) + list(outs) + list(scratch)
    return pl.pallas_call(
        functools.partial(layers_kernel, dict(sizes, names=names)),
        out_shape=[jax.ShapeDtypeStruct(shape, kind) for shape, kind in outs.values()],
        in_specs=[ANY_SPEC if name in far else VMEM_SPEC for name in arrays],
        out_specs=[VMEM_SPEC] * len(outs),
        scratch_shapes=list(scratch.values()),
        compiler_params=pltpu.CompilerParams(
            collective_id=1, has_side_effects=True, vmem_limit_bytes=VMEM_LIMIT
        ),
        name="both_layers",
    )(*arrays.values())


def shards(
    block_input,
    seq_ids,
    out_cotangent,
    qkv_weight,
    qv_bias,
    out_weight,
    out_bias,
    norm1_gain,
    norm1_bias,
    up_weight,
    up_bias,
    down_weight,
    down_bias,
    norm2_gain,
    norm2_bias,
):
    dp_count = lax.axis_size("dp")
    line = lax.axis_size("tensor")
    heads, head_part = qv_bias.shape[2], qv_bias.shape[3]
    part = out_bias.shape[1]
    width = qkv_weight.shape[3]
    model = block_input.shape[3]
    units = up_weight.shape[2]
    sizes = dict(
        line=line,
        dp_count=dp_count,
        part=part,
        width=width,
        rows=block_input.shape[2],
        model=model,
        units=units,
        heads=heads,
        head_size=head_part * dp_count,
    )
    arrays = dict(
        block_rows=block_input[:, 0],
        upstream_rows=out_cotangent[:, 0],
        ids=seq_ids,
        qkv_own=qkv_weight[0].reshape(part, 3 * width),
        out_own=out_weight[0],
        up_own=up_weight[0],
        down_own=down_weight[0],
        out_bias=out_bias,
        gain_one=norm1_gain,
        bias_one=norm1_bias,
        down_bias=down_bias,
        gain_two=norm2_gain,
        bias_two=norm2_bias,
        qv_bias=qv_bias[0],
        up_bias=up_bias[0],
    )
    results = both_layers(arrays, sizes)
    outputs, input_grads, qkv_sums, out_sums, up_sums, down_sums, rows, qv_sums, shift_sums = results
    return (
        outputs[None, :, None],
        input_grads[None, :, None],
        jnp.swapaxes(qkv_sums, 0, 1)[None],
        qv_sums[None],
        out_sums[None],
        rows[0][None],
        rows[1][None],
        rows[2][None],
        up_sums[None],
        shift_sums[None],
        down_sums[None],
        rows[3][None],
        rows[4][None],
        rows[5][None],
    )


def solution(mesh):
    return jax.shard_map(
        shards,
        mesh=mesh,
        in_specs=(
            P(None, "dp", "tensor", None),
            P(None, "dp", None),
            P(None, "dp", "tensor", None),
            P("section", "dp", None, "tensor"),
            P("section", None, "tensor", "dp"),
            P("section", "tensor", "dp"),
            P("section", "dp"),
            P("section", "dp"),
            P("section", "dp"),
            P("section", "dp", "tensor"),
            P("section", "tensor", "dp"),
            P("section", "tensor", "dp"),
            P("section", "dp"),
            P("section", "dp"),
            P("section", "dp"),
        ),
        out_specs=(
            P("section", None, "dp", "tensor", None),
            P("section", None, "dp", "tensor", None),
            P("section", "dp", None, "tensor"),
            P("section", None, "tensor", "dp"),
            P("section", "tensor", "dp"),
            P("section", ("dp", "tensor")),
            P("section", ("dp", "tensor")),
            P("section", ("dp", "tensor")),
            P("section", "dp", "tensor"),
            P("section", "tensor", "dp"),
            P("section", "tensor", "dp"),
            P("section", ("dp", "tensor")),
            P("section", ("dp", "tensor")),
            P("section", ("dp", "tensor")),
        ),
        check_vma=False,
    )
```

```python
import functools

import jax
import jax.numpy as jnp
from jax import lax
from jax.experimental import pallas as pl
from jax.experimental.pallas import tpu as pltpu
from jax.sharding import PartitionSpec as P

MESH = pl.DeviceIdType.MESH
F32 = jnp.float32
BF16 = jnp.bfloat16
VMEM_SPEC = pl.BlockSpec(memory_space=pltpu.VMEM)
ANY_SPEC = pl.BlockSpec(memory_space=pl.ANY)
VMEM_LIMIT = 63 * 1024 * 1024
CHUNK = 32
AHEAD = 3
QUARTERS = 4
SLABS = 3
PIECES = SLABS * QUARTERS
STATS = 8
BLOCK = 256
VECTORS = ("out_bias", "gain_one", "bias_one", "down_bias", "gain_two", "bias_two")

ERF_TOP = (
    0.00022905065861350646,
    0.0034082910107109506,
    0.050955695062380861,
    0.18520832239976145,
    1.128379143519084,
)
ERF_BELOW = (
    -1.1791602954361697e-7,
    0.000023547966471313185,
    0.0010179625278914885,
    0.014070470171167667,
    0.11098505178285362,
    0.49746925110067538,
    1.0,
)


def erf(values):
    x = jnp.clip(values, -3.832506856900711, 3.832506856900711)
    square = x * x
    top = jnp.full_like(square, ERF_TOP[0])
    for term in ERF_TOP[1:]:
        top = top * square + term
    below = jnp.full_like(square, ERF_BELOW[0])
    for term in ERF_BELOW[1:]:
        below = below * square + term
    return x * top / below


def nn(a, b):
    return lax.dot_general(a, b, (((1,), (0,)), ((), ())), preferred_element_type=F32)


def nt(a, b):
    return lax.dot_general(a, b, (((1,), (1,)), ((), ())), preferred_element_type=F32)


def tn(a, b):
    return lax.dot_general(a, b, (((0,), (0,)), ((), ())), preferred_element_type=F32)


def loop(count, body):
    def one(index, carry):
        body(index)
        return carry

    lax.fori_loop(0, count, one, 0)


def span(index, size):
    return pl.ds(pl.multiple_of(index * size, size), size)


def mean(values):
    return jnp.mean(values, axis=-1, keepdims=True)


def normalize(summed):
    center = summed - mean(summed)
    scaled = lax.rsqrt(mean(center * center) + 1e-12)
    return center * scaled, scaled


def norm_back(upstream, normed, scaled):
    return scaled * (upstream - mean(upstream) - normed * mean(upstream * normed))


def low_bit(mask):
    return (mask & -mask).bit_length() - 1


class Layers:
    def __init__(self, sizes, refs):
        for name, ref in zip(sizes["names"], refs):
            setattr(self, name, ref)
        self.vectors = [getattr(self, name) for name in VECTORS]
        self.line = sizes["line"]
        self.dp_count = sizes["dp_count"]
        self.bits = self.dp_count.bit_length() - 1
        self.part = sizes["part"]
        self.width = sizes["width"]
        self.rows = sizes["rows"]
        self.tokens = self.line * self.rows
        self.model = sizes["model"]
        self.units = sizes["units"]
        self.heads = sizes["heads"]
        self.head_size = sizes["head_size"]
        self.chunks = self.tokens // CHUNK
        self.quarter = self.part // QUARTERS
        self.section = lax.axis_index("section")
        self.dp = lax.axis_index("dp")
        self.me = lax.axis_index("tensor")
        self.nears = self.me // (self.line // 2)
        self.fars = 1 - self.nears
        self.middle = jnp.logical_and(self.me > 0, self.me < self.line - 1)
        self.own_rows = span(self.me, self.rows)
        self.passes = 0


    def place(self, mask):
        dp = self.dp
        for bit in range(self.bits):
            if mask & (1 << bit):
                dp = dp + (1 << bit) * (1 - 2 * ((self.dp // (1 << bit)) % 2))
        return dp

    def neighbour(self, bit):
        return {"dp": self.place(1 << bit)}

    def across(self):
        return {"section": 1 - self.section}

    def line_peer(self, step):
        return lax.rem(self.me + step, self.line)

    def remote(self, src, dst, send_sem, recv_sem, device):
        return pltpu.make_async_remote_copy(
            src_ref=src,
            dst_ref=dst,
            send_sem=send_sem,
            recv_sem=recv_sem,
            device_id=device,
            device_id_type=MESH,
        )

    def greet(self):
        barrier = pltpu.get_barrier_semaphore()
        targets = [{"tensor": self.line_peer(step)} for step in range(1, self.line)]
        targets += [self.neighbour(bit) for bit in range(self.bits)] + [self.across()]
        for target in targets:
            pl.semaphore_signal(barrier, inc=1, device_id=target, device_id_type=MESH)
        pl.semaphore_wait(barrier, len(targets))


    def rows_copy(self, which, source, target, step):
        return self.remote(
            source.at[self.section],
            target.at[self.own_rows],
            self.rows_send.at[which, step - 1],
            self.rows_recv.at[which, step - 1],
            {"tensor": self.line_peer(step)},
        )

    def rows_local(self, which, source, target):
        return pltpu.make_async_copy(
            source.at[self.section], target.at[self.own_rows], self.rows_own.at[which]
        )

    def rows_start(self, which, source, target):
        for step in range(1, self.line):
            self.rows_copy(which, source, target, step).start()
        self.rows_local(which, source, target).start()

    def rows_wait(self, which, source, target):
        self.rows_local(which, source, target).wait()
        for step in range(1, self.line):
            self.rows_copy(which, source, target, step).wait_recv()


    def weight_slot(self, s, p, mask):
        if p is None:
            return self.small_all.at[s, self.place(mask)]
        return self.weights.at[s, p // QUARTERS, self.piece_rows(p, mask)]

    def piece_rows(self, p, mask):
        at = self.place(mask) * self.part + (p % QUARTERS) * self.quarter
        return pl.ds(pl.multiple_of(at, self.quarter), self.quarter)

    def weight_copy(self, s, p, held, bit):
        number = PIECES if p is None else p
        mask = held | (1 << bit)
        return self.remote(
            self.weight_slot(s, p, held),
            self.weight_slot(s, p, held),
            self.weight_send.at[s, number, mask],
            self.weight_recv.at[s, number, mask],
            self.neighbour(bit),
        )

    def weight_arrival(self, s, p, mask):
        number = PIECES if p is None else p
        return self.remote(
            self.weight_slot(s, p, mask),
            self.weight_slot(s, p, mask),
            self.weight_send.at[s, number, mask],
            self.weight_recv.at[s, number, mask],
            self.neighbour(low_bit(mask)),
        )

    def weight_across(self, s, p):
        number = PIECES if p is None else p
        return self.remote(
            self.weight_slot(s, p, 0),
            self.weight_slot(s, p, 0),
            self.weight_send.at[s, number, 0],
            self.weight_recv.at[s, number, 0],
            self.across(),
        )

    def weight_forward(self, s, p, held):
        top = self.bits if held == 0 else low_bit(held)
        for bit in reversed(range(top)):
            self.weight_copy(s, p, held, bit).start()

    def weights_offer(self, p):
        self.weight_across(self.section, p).start()

        @pl.when(self.section == 0)
        def _():
            self.weight_forward(0, p, 0)

    def weights_offer_late(self, p):
        @pl.when(self.section == 1)
        def _():
            self.weight_forward(1, p, 0)

    def weights_cross(self, s, p):
        @pl.when(self.section != s)
        def _():
            self.weight_across(s, p).wait_recv()
            self.weight_forward(s, p, 0)

    def weights_relay(self, s, p):
        for bit in reversed(range(1, self.bits)):
            for mask in range(self.dp_count):
                if mask and low_bit(mask) == bit:
                    self.weight_arrival(s, p, mask).wait_recv()
                    self.weight_forward(s, p, mask)

    def weights_land(self, s, p):
        for mask in range(1, self.dp_count, 2):
            self.weight_arrival(s, p, mask).wait_recv()

    def weights_sent(self, s, p):
        for mask in range(1, self.dp_count):
            held = mask & (mask - 1)
            self.weight_copy(s, p, held, low_bit(mask)).wait_send()

        @pl.when(self.section == s)
        def _():
            self.weight_across(s, p).wait_send()


    def grad_slot(self, s, p, mask):
        return self.grads.at[s, p // QUARTERS, self.piece_rows(p, mask)]

    def grad_landed(self, s, p, mask):
        at = mask * self.part + (p % QUARTERS) * self.quarter
        rows = pl.ds(pl.multiple_of(at, self.quarter), self.quarter)
        return self.landed.at[s, p // QUARTERS, rows]

    def grad_copy(self, s, p, mask):
        device = self.neighbour(low_bit(mask)) if mask else self.across()
        return self.remote(
            self.grad_slot(s, p, mask),
            self.grad_landed(s, p, mask),
            self.grad_send.at[s, p, mask],
            self.grad_recv.at[s, p, mask],
            device,
        )

    def grad_total(self, s, p, mask, last=False):
        total = self.grad_slot(s, p, mask)[...].astype(F32)
        for bit in range(low_bit(mask) if mask else self.bits):
            self.grad_copy(s, p, mask | (1 << bit)).wait_recv()
            total = total + self.grad_landed(s, p, mask | (1 << bit))[...].astype(F32)
        return total

    def grads_offer(self, s, p):
        for mask in range(1, self.dp_count, 2):
            self.grad_copy(s, p, mask).start()

    def grads_fold(self, s, p):
        for bit in range(1, self.bits):
            for mask in range(self.dp_count):
                if mask and low_bit(mask) == bit:
                    self.grad_slot(s, p, mask)[...] = self.grad_total(s, p, mask).astype(BF16)
                    self.grad_copy(s, p, mask).start()

    def grads_cross(self, s, p):
        @pl.when(self.section != s)
        def _():
            self.grad_slot(s, p, 0)[...] = self.grad_total(s, p, 0).astype(BF16)
            self.grad_copy(s, p, 0).start()

    def grads_end(self, s, p):
        @pl.when(self.section == s)
        def _():
            total = self.grad_total(s, p, 0)
            self.grad_copy(s, p, 0).wait_recv()
            total = total + self.grad_landed(s, p, 0)[...].astype(F32)
            rows = span(p % QUARTERS, self.quarter)
            slab = p // QUARTERS

            @pl.when(slab == 0)
            def _():
                for which in range(3):
                    at = slice(which * self.width, (which + 1) * self.width)
                    self.qkv_sums[which, rows] = total[:, at]
                self.out_turned[rows] = total[:, 3 * self.width :]

            @pl.when(slab == 1)
            def _():
                self.up_sums[rows] = total

            @pl.when(slab == 2)
            def _():
                self.down_turned[rows] = total

    def grads_sent(self, s, p):
        for mask in range(1, self.dp_count):
            self.grad_copy(s, p, mask).wait_send()

        @pl.when(self.section != s)
        def _():
            self.grad_copy(s, p, 0).wait_send()


    def line_copy(self, half, side, chunk, target):
        rows = span(chunk, CHUNK)
        return self.remote(
            self.staged.at[side, rows],
            self.sums.at[half, side, rows],
            self.line_send.at[side, chunk],
            self.line_recv.at[half, side, chunk],
            {"tensor": target},
        )

    def line_sum(self, finish, tick):
        number = self.passes
        half = number % 2
        self.passes += 1
        near_target = self.me + 1 - 2 * self.nears
        far_target = self.me - 1 + 2 * self.nears

        def send(side, chunk, target):
            rows = span(chunk, CHUNK)
            if number > 0:
                self.line_copy(half, side, chunk, target).wait_send()
            total = self.partial[rows] + self.sums[half, side, rows].astype(F32)
            self.staged[side, rows] = total.astype(BF16)
            self.line_copy(half, side, chunk, target).start()

        def near(chunk):
            @pl.when(self.middle)
            def _():
                self.line_copy(half, self.nears, chunk, near_target).wait_recv()

            send(self.nears, chunk, near_target)

        ahead = jnp.where(self.middle, AHEAD, self.chunks)
        loop(ahead, near)

        def body(chunk):
            @pl.when(chunk + ahead < self.chunks)
            def _():
                near(chunk + ahead)

            self.line_copy(half, self.fars, chunk, near_target).wait_recv()

            @pl.when(self.middle)
            def _():
                send(self.fars, chunk, far_target)

            rows = span(chunk, CHUNK)
            total = (
                self.partial[rows]
                + self.sums[half, 0, rows].astype(F32)
                + self.sums[half, 1, rows].astype(F32)
            )
            finish(rows, total)
            tick(chunk)

        loop(self.chunks, body)

    def line_sent(self):
        def one(chunk):
            self.line_copy(0, self.nears, chunk, self.me + 1 - 2 * self.nears).wait_send()

            @pl.when(self.middle)
            def _():
                self.line_copy(0, self.fars, chunk, self.me - 1 + 2 * self.nears).wait_send()

        loop(self.chunks, one)

    def clear(self):
        for half in range(2):
            for side, end in ((0, 0), (1, self.line - 1)):

                @pl.when(self.me == end)
                def _():
                    self.sums[half, side] = jnp.zeros(self.sums.shape[2:], BF16)

        self.stats[...] = jnp.zeros(self.stats.shape, F32)
        row = jnp.broadcast_to(self.ids[self.section], (self.tokens, self.tokens))
        self.hidden_pairs[...] = jnp.where(row == row.T, 0.0, -1e30)


    def param(self, s, row):
        return self.params[s, row : row + 1]

    def count_stat(self, s, row, values):
        folded = values.reshape(values.shape[0] // 8, 8, values.shape[1])
        self.stats[s, row] += jnp.sum(folded, axis=0)

    def attention(self, s):
        width = self.width
        for block in range(3):
            at = slice(block * width, (block + 1) * width)
            made = nn(self.inputs[s], self.weights[s, 0, :, at])
            if block != 1:
                low = 0 if block == 0 else width
                made = made + self.params[s, 6:7, low : low + width]
            self.qkv[s, :, at] = made.astype(BF16)
        contexts = []
        for head in range(self.heads):
            query, key, value = self.head_parts(s, head)
            scores = nt(query, key) * self.head_size ** (-0.5) + self.hidden_pairs[...]
            shifted = jnp.exp(scores - jnp.max(scores, axis=-1, keepdims=True))
            prob = shifted / jnp.sum(shifted, axis=-1, keepdims=True)
            prob = prob.astype(BF16)
            self.probs[s, head] = prob
            contexts.append(nn(prob, value).astype(BF16))
        self.context[s] = jnp.concatenate(contexts, axis=1)

        def project(block):
            at = span(block, BLOCK)
            self.partial[:, at] = nt(self.context[s], self.weights[s, 0, at, 3 * width :])

        loop(self.model // BLOCK, project)

    def head_parts(self, s, head):
        size = self.head_size
        low = head * size
        return [
            self.qkv[s, :, which * self.width + low : which * self.width + low + size]
            for which in range(3)
        ]

    def feed_up(self, s):
        def block_of(block):
            at = span(block, BLOCK)
            self.partial[:, at] = nn(self.hidden[s], self.weights[s, 1, :, at])

        loop(self.units // BLOCK, block_of)

        def gelu(step):
            rows = span(step, 16)
            pre = self.partial[rows] + self.param(s, 7)
            half = 0.5 * (1.0 + erf(pre * 0.7071067811865476))
            self.active[s, rows] = (pre * half).astype(BF16)
            bell = pre * jnp.exp(-0.5 * pre * pre) * 0.3989422804014327
            self.slope[s, rows] = (half + bell).astype(BF16)

        loop(self.tokens // 16, gelu)

    def feed_down(self, s):
        def block_of(block):
            at = span(block, BLOCK)
            self.partial[:, at] = nt(self.active[s], self.weights[s, 2, at])

        loop(self.model // BLOCK, block_of)

    def after_attention(self, s):
        def finish(rows, total):
            summed = self.inputs[s, rows].astype(F32) + total + self.param(s, 0)
            normed, scaled = normalize(summed)
            self.normed_one[s, rows] = normed.astype(BF16)
            self.scaled_one[s, rows] = jnp.broadcast_to(scaled, (CHUNK, 128))
            hidden = normed * self.param(s, 1) + self.param(s, 2)
            self.wide[rows] = hidden
            self.hidden[s, rows] = hidden.astype(BF16)

        return finish

    def after_feed(self, s):
        def finish(rows, total):
            summed = self.wide[rows] + total + self.param(s, 3)
            normed, scaled = normalize(summed)
            out = normed * self.param(s, 4) + self.param(s, 5)
            self.inputs[s + 1, rows] = out.astype(BF16)
            if s == 0:
                self.normed_two[rows] = normed.astype(BF16)
                self.scaled_two[rows] = jnp.broadcast_to(scaled, (CHUNK, 128))
            else:
                self.start_back(s, rows, self.grad_one_held[rows].astype(F32), normed, scaled)

        return finish

    def start_back(self, s, rows, upstream, normed, scaled):
        grad_two = norm_back(upstream * self.param(s, 4), normed, scaled)
        self.wide[rows] = grad_two
        self.grad_two_held[rows] = grad_two.astype(BF16)
        self.count_stat(s, 3, grad_two)
        self.count_stat(s, 4, upstream * normed)
        self.count_stat(s, 5, upstream)

    def feed_back(self, s):
        def block_of(block):
            at = span(block, BLOCK)
            self.partial[:, at] = nn(self.grad_two_held[...], self.weights[s, 2, :, at])

        loop(self.units // BLOCK, block_of)

        def slopes(step):
            rows = span(step, 16)
            grad_pre = self.partial[rows] * self.slope[s, rows].astype(F32)
            self.grad_pre[rows] = grad_pre.astype(BF16)
            self.count_stat(s, 7, grad_pre)

        loop(self.tokens // 16, slopes)

        def up_of(block):
            at = span(block, BLOCK)
            self.partial[:, at] = nt(self.grad_pre[...], self.weights[s, 1, at])

        loop(self.model // BLOCK, up_of)

    def after_feed_back(self, s):
        def finish(rows, total):
            grad_hidden = self.wide[rows] + total
            normed = self.normed_one[s, rows].astype(F32)
            scaled = self.scaled_one[s, rows][:, :1]
            grad_one = norm_back(grad_hidden * self.param(s, 1), normed, scaled)
            self.grad_wide[rows] = grad_one
            self.grad_one_held[rows] = grad_one.astype(BF16)
            self.count_stat(s, 0, grad_one)
            self.count_stat(s, 1, grad_hidden * normed)
            self.count_stat(s, 2, grad_hidden)

        return finish

    def feed_grads(self, s, step):
        cuts = self.chunks // 2
        block = step // 2
        size = self.model // cuts
        at = span(block, size)

        @pl.when(step % 2 == 0)
        def _():
            made = tn(self.grad_two_held[:, at], self.active[s])
            self.grads[s, 2, at] = made.astype(BF16)

        @pl.when(step % 2 == 1)
        def _():
            made = tn(self.hidden[s, :, at], self.grad_pre[...])
            self.grads[s, 1, at] = made.astype(BF16)

    def attention_grads(self, s, step):
        cuts = self.chunks // 2
        block = step // 2
        size = self.model // cuts
        at = span(block, size)

        @pl.when(step % 2 == 0)
        def _():
            made = tn(self.inputs[s, :, at], self.grad_qkv[...])
            self.grads[s, 0, at, : 3 * self.width] = made.astype(BF16)

        @pl.when(step % 2 == 1)
        def _():
            made = tn(self.grad_one_held[:, at], self.context[s])
            self.grads[s, 0, at, 3 * self.width :] = made.astype(BF16)

    def attention_back(self, s):
        width, size = self.width, self.head_size
        grad_context = nn(self.grad_one_held[...], self.weights[s, 0, :, 3 * width :])
        self.grad_context[...] = grad_context.astype(BF16)
        parts = [[], [], []]
        for head in range(self.heads):
            query, key, value = self.head_parts(s, head)
            above = self.grad_context[:, head * size : (head + 1) * size]
            held = self.probs[s, head]
            prob = held.astype(F32)
            grad_prob = nt(above, value)
            dots = jnp.sum(prob * grad_prob, axis=-1, keepdims=True)
            grad_scores = (prob * (grad_prob - dots) * size ** (-0.5)).astype(BF16)
            parts[0].append(nn(grad_scores, key))
            parts[1].append(tn(grad_scores, query))
            parts[2].append(tn(held, above))
        for which in range(3):
            made = jnp.concatenate(parts[which], axis=1)
            self.grad_qkv[:, which * width : (which + 1) * width] = made.astype(BF16)
            if which != 1:
                folded = jnp.sum(made.reshape(self.tokens // 8, 8, width), axis=0)
                low = 0 if which == 0 else width
                self.stats[s, 6, :, low : low + width] = folded

        def block_of(block):
            at = span(block, BLOCK)
            self.partial[:, at] = nt(self.grad_qkv[...], self.weights[s, 0, at, : 3 * width])

        loop(self.model // BLOCK, block_of)

    def after_attention_back(self, s):
        def finish(rows, total):
            upstream = self.grad_wide[rows] + total
            self.grad_wide[rows] = upstream
            if s == 1:
                normed = self.normed_two[rows].astype(F32)
                self.start_back(0, rows, upstream, normed, self.scaled_two[rows][:, :1])

        return finish


    def output_copy(self, s, local):
        source = self.inputs.at[s + 1, self.own_rows]
        target = self.outputs.at[self.section]
        if local:
            return pltpu.make_async_copy(source, target, self.out_sem.at[0])
        return self.remote(source, target, self.out_sem.at[1], self.out_sem.at[2], self.across())

    def output_start(self, s):
        for local in (True, False):

            @pl.when((self.section == s) if local else (self.section != s))
            def _():
                self.output_copy(s, local).start()

    def input_grad_copy(self):
        return self.remote(
            self.input_grad_staged,
            self.input_grad_landed,
            self.out_sem.at[3],
            self.out_sem.at[4],
            self.across(),
        )

    def input_grad_start(self, s):
        @pl.when(self.section == s)
        def _():
            self.input_grads[self.section] = self.grad_wide[self.own_rows]

        @pl.when(self.section != s)
        def _():
            self.input_grad_staged[...] = self.grad_wide[self.own_rows].astype(BF16)
            self.input_grad_copy().start()

    def outputs_end(self):
        self.output_copy(0, True).wait()
        self.output_copy(0, False).wait()
        self.input_grad_copy().wait()
        self.input_grads[1 - self.section] = self.input_grad_landed[...].astype(F32)


    def stat_copy(self, step):
        return self.remote(
            self.stat_sums.at[step],
            self.stat_landed.at[step],
            self.stat_sem.at[0, step],
            self.stat_sem.at[1, step],
            self.neighbour(step) if step < self.bits else self.across(),
        )

    def stat_step(self, step):
        self.stat_copy(step).wait_recv()
        self.stat_sums[step + 1] = self.stat_sums[step] + self.stat_landed[step]
        if step < self.bits:
            self.stat_copy(step + 1).start()


    def spread_small(self):
        model, dp_count = self.model, self.dp_count
        place = lax.broadcasted_iota(jnp.int32, (1, model), 1) // self.part
        rows = []
        for ref in self.vectors:
            tiled = jnp.concatenate([ref[...].astype(F32)] * dp_count, axis=1)
            rows.append(jnp.where(place == self.dp, tiled, 0.0))

        def spread(values):
            size = values.shape[1]
            shape = (size, size * dp_count)
            low = lax.broadcasted_iota(jnp.int32, shape, 0) + self.dp * size
            chosen = jnp.where(lax.broadcasted_iota(jnp.int32, shape, 1) == low, 1.0, 0.0)
            return nn(values.astype(BF16), chosen.astype(BF16))

        query, value = spread(self.qv_bias[0]), spread(self.qv_bias[1])
        pieces = [query[head : head + 1] for head in range(self.heads)]
        pieces += [value[head : head + 1] for head in range(self.heads)]
        pieces.append(jnp.zeros((1, model - 2 * self.width), F32))
        rows.append(jnp.concatenate(pieces, axis=1))
        above = spread(self.up_bias[...])
        rows.append(
            jnp.concatenate([above[group : group + 1] for group in range(above.shape[0])], axis=1)
        )
        self.small_all[self.section, self.dp] = jnp.concatenate(rows, axis=0)

    def small_outputs(self):
        total = self.stat_sums[self.bits + 1, self.section]
        model = self.model

        def turned(offset):
            return pltpu.roll(total, lax.rem(model - offset, model), 1)

        share = self.part // self.line
        self.row_sums[...] = turned(self.dp * self.part + self.me * share)[:6, :share]
        size = self.head_size // self.dp_count
        moved = turned(self.dp * size)
        for which in range(2):
            for head in range(self.heads):
                low = which * self.width + head * self.head_size
                self.qv_sums[which, head : head + 1] = moved[6:7, low : low + size]
        groups, size = self.shift_sums.shape
        moved = turned(self.dp * size)
        for group in range(groups):
            low = group * size * self.dp_count
            self.shift_sums[group : group + 1] = moved[7:8, low : low + size]

    def own_copies(self):
        mine = pl.ds(pl.multiple_of(self.dp * self.part, self.part), self.part)
        here = self.weights.at[self.section]
        pairs = [
            (self.qkv_own, here.at[0, mine, pl.ds(0, 3 * self.width)]),
            (self.out_own, self.out_raw),
            (self.up_own, here.at[1, mine]),
            (self.down_own, self.down_raw),
        ]
        return [
            pltpu.make_async_copy(source, target, self.own_sem.at[number])
            for number, (source, target) in enumerate(pairs)
        ]

    def run(self):
        def nothing(step):
            pass

        copies = self.own_copies()
        for copy in copies:
            copy.start()
        self.greet()
        self.rows_start(0, self.block_rows, self.inputs.at[0])
        mine = pl.ds(pl.multiple_of(self.dp * self.part, self.part), self.part)
        copies[0].wait()
        copies[1].wait()
        self.weights[self.section, 0, mine, 3 * self.width :] = self.out_raw[...].T
        loop(QUARTERS, self.weights_offer)
        self.spread_small()
        self.weights_offer(None)
        copies[2].wait()
        copies[3].wait()
        self.weights[self.section, 2, mine] = self.down_raw[...].T
        loop(PIECES - QUARTERS, lambda p: self.weights_offer(QUARTERS + p))
        self.clear()
        for p in range(QUARTERS + 1):
            if p < QUARTERS:
                self.weights_cross(0, p)
            if p == 1:
                self.weights_cross(0, None)
            if p == 2:
                self.weights_relay(0, None)
            if p > 0:
                self.weights_relay(0, p - 1)
        self.weights_land(0, None)
        loop(QUARTERS, functools.partial(self.weights_land, 0))
        self.params[0] = jnp.sum(self.small_all[0], axis=0)
        self.rows_wait(0, self.block_rows, self.inputs.at[0])
        self.rows_start(1, self.upstream_rows, self.grad_one_held)

        self.attention(0)

        def first_tick(step):
            self.weights_cross(0, QUARTERS + step)

            @pl.when(step > 0)
            def _():
                self.weights_relay(0, QUARTERS + step - 1)

        self.line_sum(self.after_attention(0), first_tick)
        self.weights_relay(0, PIECES - 1)
        self.weights_offer_late(None)
        loop(PIECES, self.weights_offer_late)
        loop(QUARTERS, lambda p: self.weights_land(0, QUARTERS + p))
        self.feed_up(0)
        loop(QUARTERS, lambda p: self.weights_land(0, 2 * QUARTERS + p))
        self.feed_down(0)

        self.weights_cross(1, None)
        loop(PIECES, functools.partial(self.weights_cross, 1))

        def second_tick(step):
            @pl.when(step == 1)
            def _():
                self.weights_relay(1, None)

            @pl.when(step > 0)
            def _():
                self.weights_relay(1, step - 1)

        self.line_sum(self.after_feed(0), second_tick)
        self.output_start(0)
        self.weights_land(1, None)
        loop(QUARTERS, functools.partial(self.weights_land, 1))
        self.params[1] = jnp.sum(self.small_all[1], axis=0)

        self.attention(1)

        def third_tick(step):
            @pl.when(step <= QUARTERS)
            def _():
                self.weights_relay(1, 2 * QUARTERS + step - 1)

        self.line_sum(self.after_attention(1), third_tick)
        loop(QUARTERS, lambda p: self.weights_land(1, QUARTERS + p))
        self.feed_up(1)
        loop(QUARTERS, lambda p: self.weights_land(1, 2 * QUARTERS + p))
        self.feed_down(1)
        self.rows_wait(1, self.upstream_rows, self.grad_one_held)
        self.line_sum(self.after_feed(1), nothing)
        self.output_start(1)

        def turn(order):
            return (SLABS - 1 - order // QUARTERS) * QUARTERS + order % QUARTERS

        def service(s, action, order):
            @pl.when(jnp.logical_and(order >= 0, order < PIECES))
            def _():
                action(s, turn(order))

        self.feed_back(1)
        self.line_sum(self.after_feed_back(1), functools.partial(self.feed_grads, 1))
        loop(2 * QUARTERS, lambda order: self.grads_offer(1, turn(order)))
        self.attention_back(1)

        def fourth_tick(step):
            self.attention_grads(1, step)
            service(1, self.grads_fold, step)
            service(1, self.grads_cross, step - 2)
            service(1, self.grads_end, step - 4)

        self.line_sum(self.after_attention_back(1), fourth_tick)
        loop(QUARTERS, lambda q: self.grads_offer(1, q))
        self.input_grad_start(1)
        self.feed_back(0)

        def fifth_tick(step):
            self.feed_grads(0, step)
            service(1, self.grads_fold, step + 8)
            service(1, self.grads_cross, step + 6)
            service(1, self.grads_end, step + 4)

        self.line_sum(self.after_feed_back(0), fifth_tick)
        loop(2 * QUARTERS, lambda order: self.grads_offer(0, turn(order)))
        self.attention_back(0)
        self.stat_sums[0] = jnp.sum(self.stats[...], axis=2)
        self.stat_copy(0).start()

        def sixth_tick(step):
            self.attention_grads(0, step)
            for number in range(self.bits + 1):

                @pl.when(step == min(2 * number + 2, self.chunks - 1))
                def _():
                    self.stat_step(number)

            service(0, self.grads_fold, step)
            service(0, self.grads_cross, step - 2)
            service(0, self.grads_end, step - 4)

        self.line_sum(self.after_attention_back(0), sixth_tick)
        loop(QUARTERS, lambda q: self.grads_offer(0, q))
        self.input_grad_start(0)

        def last_tick(step):
            service(0, self.grads_fold, step + 8)
            service(0, self.grads_cross, step + 6)
            service(0, self.grads_end, step + 4)

        loop(8, last_tick)
        self.small_outputs()
        self.out_sums[...] = self.out_turned[...].T
        self.down_sums[...] = self.down_turned[...].T
        self.outputs_end()

        for which, source, target in (
            (0, self.block_rows, self.inputs.at[0]),
            (1, self.upstream_rows, self.grad_one_held),
        ):
            for step in range(1, self.line):
                self.rows_copy(which, source, target, step).wait_send()
        self.line_sent()
        for s in range(2):
            self.weights_sent(s, None)
            loop(PIECES, functools.partial(self.weights_sent, s))
            loop(PIECES, functools.partial(self.grads_sent, s))
        for step in range(self.bits + 1):
            self.stat_copy(step).wait_send()


def layers_kernel(sizes, *refs):
    Layers(sizes, refs).run()


def both_layers(arrays, sizes):
    line, dp_count, part = sizes["line"], sizes["dp_count"], sizes["part"]
    rows, width, model, units = sizes["rows"], sizes["width"], sizes["model"], sizes["units"]
    heads = sizes["heads"]
    tokens = line * rows
    chunks = tokens // CHUNK
    bits = dp_count.bit_length() - 1
    dma = pltpu.SemaphoreType.DMA
    vmem = pltpu.VMEM
    scratch = dict(
        inputs=vmem((3, tokens, model), BF16),
        weights=vmem((2, SLABS, model, units), BF16),
        grads=vmem((2, SLABS, model, units), BF16),
        landed=vmem((2, SLABS, model, units), BF16),
        small_all=vmem((2, dp_count, STATS, model), F32),
        params=vmem((2, STATS, model), F32),
        sums=vmem((2, 2, tokens, model), BF16),
        staged=vmem((2, tokens, model), BF16),
        partial=vmem((tokens, model), F32),
        wide=vmem((tokens, model), F32),
        grad_wide=vmem((tokens, model), F32),
        normed_one=vmem((2, tokens, model), BF16),
        normed_two=vmem((tokens, model), BF16),
        scaled_one=vmem((2, tokens, 128), F32),
        scaled_two=vmem((tokens, 128), F32),
        hidden=vmem((2, tokens, model), BF16),
        active=vmem((2, tokens, units), BF16),
        slope=vmem((2, tokens, units), BF16),
        qkv=vmem((2, tokens, 3 * width), BF16),
        probs=vmem((2, heads, tokens, tokens), BF16),
        context=vmem((2, tokens, width), BF16),
        grad_two_held=vmem((tokens, model), BF16),
        grad_one_held=vmem((tokens, model), BF16),
        grad_pre=vmem((tokens, units), BF16),
        grad_context=vmem((tokens, width), BF16),
        grad_qkv=vmem((tokens, 3 * width), BF16),
        hidden_pairs=vmem((tokens, tokens), F32),
        stats=vmem((2, STATS, 8, model), F32),
        stat_sums=vmem((bits + 2, 2, STATS, model), F32),
        stat_landed=vmem((bits + 1, 2, STATS, model), F32),
        input_grad_staged=vmem((rows, model), BF16),
        input_grad_landed=vmem((rows, model), BF16),
        out_raw=vmem((width, part), BF16),
        down_raw=vmem((units, part), BF16),
        out_turned=vmem((part, width), F32),
        down_turned=vmem((part, units), F32),
        rows_send=dma((2, line - 1)),
        rows_recv=dma((2, line - 1)),
        rows_own=dma((2,)),
        own_sem=dma((4,)),
        weight_send=dma((2, PIECES + 1, dp_count)),
        weight_recv=dma((2, PIECES + 1, dp_count)),
        grad_send=dma((2, PIECES, dp_count)),
        grad_recv=dma((2, PIECES, dp_count)),
        line_send=dma((2, chunks)),
        line_recv=dma((2, 2, chunks)),
        out_sem=dma((5,)),
        stat_sem=dma((2, bits + 1)),
    )
    outs = dict(
        outputs=((2, rows, model), BF16),
        input_grads=((2, rows, model), F32),
        qkv_sums=((3, part, width), F32),
        out_sums=((width, part), F32),
        up_sums=((part, units), F32),
        down_sums=((units, part), F32),
        row_sums=((6, part // line), F32),
        qv_sums=((2, heads, sizes["head_size"] // dp_count), F32),
        shift_sums=(arrays["up_bias"].shape, F32),
    )
    far = ("block_rows", "upstream_rows", "qkv_own", "out_own", "up_own", "down_own")
    names = list(arrays) + list(outs) + list(scratch)
    return pl.pallas_call(
        functools.partial(layers_kernel, dict(sizes, names=names)),
        out_shape=[jax.ShapeDtypeStruct(shape, kind) for shape, kind in outs.values()],
        in_specs=[ANY_SPEC if name in far else VMEM_SPEC for name in arrays],
        out_specs=[VMEM_SPEC] * len(outs),
        scratch_shapes=list(scratch.values()),
        compiler_params=pltpu.CompilerParams(
            collective_id=1, has_side_effects=True, vmem_limit_bytes=VMEM_LIMIT
        ),
        name="both_layers",
    )(*arrays.values())


def shards(
    block_input,
    seq_ids,
    out_cotangent,
    qkv_weight,
    qv_bias,
    out_weight,
    out_bias,
    norm1_gain,
    norm1_bias,
    up_weight,
    up_bias,
    down_weight,
    down_bias,
    norm2_gain,
    norm2_bias,
):
    dp_count = lax.axis_size("dp")
    line = lax.axis_size("tensor")
    heads, head_part = qv_bias.shape[2], qv_bias.shape[3]
    part = out_bias.shape[1]
    width = qkv_weight.shape[3]
    model = block_input.shape[3]
    units = up_weight.shape[2]
    sizes = dict(
        line=line,
        dp_count=dp_count,
        part=part,
        width=width,
        rows=block_input.shape[2],
        model=model,
        units=units,
        heads=heads,
        head_size=head_part * dp_count,
    )
    arrays = dict(
        block_rows=block_input[:, 0],
        upstream_rows=out_cotangent[:, 0],
        ids=seq_ids,
        qkv_own=qkv_weight[0].reshape(part, 3 * width),
        out_own=out_weight[0],
        up_own=up_weight[0],
        down_own=down_weight[0],
        out_bias=out_bias,
        gain_one=norm1_gain,
        bias_one=norm1_bias,
        down_bias=down_bias,
        gain_two=norm2_gain,
        bias_two=norm2_bias,
        qv_bias=qv_bias[0],
        up_bias=up_bias[0],
    )
    results = both_layers(arrays, sizes)
    outputs, input_grads, qkv_sums, out_sums, up_sums, down_sums, rows, qv_sums, shift_sums = results
    return (
        outputs[None, :, None],
        input_grads[None, :, None],
        jnp.swapaxes(qkv_sums, 0, 1)[None],
        qv_sums[None],
        out_sums[None],
        rows[0][None],
        rows[1][None],
        rows[2][None],
        up_sums[None],
        shift_sums[None],
        down_sums[None],
        rows[3][None],
        rows[4][None],
        rows[5][None],
    )


def solution(mesh):
    return jax.shard_map(
        shards,
        mesh=mesh,
        in_specs=(
            P(None, "dp", "tensor", None),
            P(None, "dp", None),
            P(None, "dp", "tensor", None),
            P("section", "dp", None, "tensor"),
            P("section", None, "tensor", "dp"),
            P("section", "tensor", "dp"),
            P("section", "dp"),
            P("section", "dp"),
            P("section", "dp"),
            P("section", "dp", "tensor"),
            P("section", "tensor", "dp"),
            P("section", "tensor", "dp"),
            P("section", "dp"),
            P("section", "dp"),
            P("section", "dp"),
        ),
        out_specs=(
            P("section", None, "dp", "tensor", None),
            P("section", None, "dp", "tensor", None),
            P("section", "dp", None, "tensor"),
            P("section", None, "tensor", "dp"),
            P("section", "tensor", "dp"),
            P("section", ("dp", "tensor")),
            P("section", ("dp", "tensor")),
            P("section", ("dp", "tensor")),
            P("section", "dp", "tensor"),
            P("section", "tensor", "dp"),
            P("section", "tensor", "dp"),
            P("section", ("dp", "tensor")),
            P("section", ("dp", "tensor")),
            P("section", ("dp", "tensor")),
        ),
        check_vma=False,
    )
```

```python
import functools

import jax
import jax.numpy as jnp
from jax import lax
from jax.experimental import pallas as pl
from jax.experimental.pallas import tpu as pltpu
from jax.sharding import PartitionSpec as P

MESH = pl.DeviceIdType.MESH
F32 = jnp.float32
BF16 = jnp.bfloat16
VMEM_SPEC = pl.BlockSpec(memory_space=pltpu.VMEM)
ANY_SPEC = pl.BlockSpec(memory_space=pl.ANY)
VMEM_LIMIT = 63 * 1024 * 1024
CHUNK = 32
AHEAD = 2
QUARTERS = 4
SLABS = 3
PIECES = SLABS * QUARTERS
STATS = 8
BLOCK = 256
VECTORS = ("out_bias", "gain_one", "bias_one", "down_bias", "gain_two", "bias_two")

ERF_TOP = (
    0.00022905065861350646,
    0.0034082910107109506,
    0.050955695062380861,
    0.18520832239976145,
    1.128379143519084,
)
ERF_BELOW = (
    -1.1791602954361697e-7,
    0.000023547966471313185,
    0.0010179625278914885,
    0.014070470171167667,
    0.11098505178285362,
    0.49746925110067538,
    1.0,
)


def erf(values):
    x = jnp.clip(values, -3.832506856900711, 3.832506856900711)
    square = x * x
    top = jnp.full_like(square, ERF_TOP[0])
    for term in ERF_TOP[1:]:
        top = top * square + term
    below = jnp.full_like(square, ERF_BELOW[0])
    for term in ERF_BELOW[1:]:
        below = below * square + term
    return x * top / below


def nn(a, b):
    return lax.dot_general(a, b, (((1,), (0,)), ((), ())), preferred_element_type=F32)


def nt(a, b):
    return lax.dot_general(a, b, (((1,), (1,)), ((), ())), preferred_element_type=F32)


def tn(a, b):
    return lax.dot_general(a, b, (((0,), (0,)), ((), ())), preferred_element_type=F32)


def loop(count, body):
    def one(index, carry):
        body(index)
        return carry

    lax.fori_loop(0, count, one, 0)


def span(index, size):
    return pl.ds(pl.multiple_of(index * size, size), size)


def mean(values):
    return jnp.mean(values, axis=-1, keepdims=True)


def normalize(summed):
    center = summed - mean(summed)
    scaled = lax.rsqrt(mean(center * center) + 1e-12)
    return center * scaled, scaled


def norm_back(upstream, normed, scaled):
    return scaled * (upstream - mean(upstream) - normed * mean(upstream * normed))


def low_bit(mask):
    return (mask & -mask).bit_length() - 1


class Layers:
    def __init__(self, sizes, refs):
        for name, ref in zip(sizes["names"], refs):
            setattr(self, name, ref)
        self.vectors = [getattr(self, name) for name in VECTORS]
        self.line = sizes["line"]
        self.dp_count = sizes["dp_count"]
        self.bits = self.dp_count.bit_length() - 1
        self.part = sizes["part"]
        self.width = sizes["width"]
        self.rows = sizes["rows"]
        self.tokens = self.line * self.rows
        self.model = sizes["model"]
        self.units = sizes["units"]
        self.heads = sizes["heads"]
        self.head_size = sizes["head_size"]
        self.chunks = self.tokens // CHUNK
        self.quarter = self.part // QUARTERS
        self.section = lax.axis_index("section")
        self.dp = lax.axis_index("dp")
        self.me = lax.axis_index("tensor")
        self.nears = self.me // (self.line // 2)
        self.fars = 1 - self.nears
        self.middle = jnp.logical_and(self.me > 0, self.me < self.line - 1)
        self.own_rows = span(self.me, self.rows)
        self.passes = 0


    def place(self, mask):
        dp = self.dp
        for bit in range(self.bits):
            if mask & (1 << bit):
                dp = dp + (1 << bit) * (1 - 2 * ((self.dp // (1 << bit)) % 2))
        return dp

    def neighbour(self, bit):
        return {"dp": self.place(1 << bit)}

    def across(self):
        return {"section": 1 - self.section}

    def line_peer(self, step):
        return lax.rem(self.me + step, self.line)

    def remote(self, src, dst, send_sem, recv_sem, device):
        return pltpu.make_async_remote_copy(
            src_ref=src,
            dst_ref=dst,
            send_sem=send_sem,
            recv_sem=recv_sem,
            device_id=device,
            device_id_type=MESH,
        )

    def greet(self):
        barrier = pltpu.get_barrier_semaphore()
        targets = [{"tensor": self.line_peer(step)} for step in range(1, self.line)]
        targets += [self.neighbour(bit) for bit in range(self.bits)] + [self.across()]
        for target in targets:
            pl.semaphore_signal(barrier, inc=1, device_id=target, device_id_type=MESH)
        pl.semaphore_wait(barrier, len(targets))


    def rows_copy(self, which, source, target, step):
        return self.remote(
            source.at[self.section],
            target.at[self.own_rows],
            self.rows_send.at[which, step - 1],
            self.rows_recv.at[which, step - 1],
            {"tensor": self.line_peer(step)},
        )

    def rows_local(self, which, source, target):
        return pltpu.make_async_copy(
            source.at[self.section], target.at[self.own_rows], self.rows_own.at[which]
        )

    def rows_start(self, which, source, target):
        for step in range(1, self.line):
            self.rows_copy(which, source, target, step).start()
        self.rows_local(which, source, target).start()

    def rows_wait(self, which, source, target):
        self.rows_local(which, source, target).wait()
        for step in range(1, self.line):
            self.rows_copy(which, source, target, step).wait_recv()


    def weight_slot(self, s, p, mask):
        if p is None:
            return self.small_all.at[s, self.place(mask)]
        return self.weights.at[s, p // QUARTERS, self.piece_rows(p, mask)]

    def piece_rows(self, p, mask):
        at = self.place(mask) * self.part + (p % QUARTERS) * self.quarter
        return pl.ds(pl.multiple_of(at, self.quarter), self.quarter)

    def weight_copy(self, s, p, held, bit):
        number = PIECES if p is None else p
        mask = held | (1 << bit)
        return self.remote(
            self.weight_slot(s, p, held),
            self.weight_slot(s, p, held),
            self.weight_send.at[s, number, mask],
            self.weight_recv.at[s, number, mask],
            self.neighbour(bit),
        )

    def weight_arrival(self, s, p, mask):
        number = PIECES if p is None else p
        return self.remote(
            self.weight_slot(s, p, mask),
            self.weight_slot(s, p, mask),
            self.weight_send.at[s, number, mask],
            self.weight_recv.at[s, number, mask],
            self.neighbour(low_bit(mask)),
        )

    def weight_across(self, s, p):
        number = PIECES if p is None else p
        return self.remote(
            self.weight_slot(s, p, 0),
            self.weight_slot(s, p, 0),
            self.weight_send.at[s, number, 0],
            self.weight_recv.at[s, number, 0],
            self.across(),
        )

    def weight_forward(self, s, p, held):
        top = self.bits if held == 0 else low_bit(held)
        for bit in reversed(range(top)):
            self.weight_copy(s, p, held, bit).start()

    def weights_offer(self, p):
        self.weight_across(self.section, p).start()

        @pl.when(self.section == 0)
        def _():
            self.weight_forward(0, p, 0)

    def weights_offer_late(self, p):
        @pl.when(self.section == 1)
        def _():
            self.weight_forward(1, p, 0)

    def weights_cross(self, s, p):
        @pl.when(self.section != s)
        def _():
            self.weight_across(s, p).wait_recv()
            self.weight_forward(s, p, 0)

    def weights_relay(self, s, p):
        for bit in reversed(range(1, self.bits)):
            for mask in range(self.dp_count):
                if mask and low_bit(mask) == bit:
                    self.weight_arrival(s, p, mask).wait_recv()
                    self.weight_forward(s, p, mask)

    def weights_land(self, s, p):
        for mask in range(1, self.dp_count, 2):
            self.weight_arrival(s, p, mask).wait_recv()

    def weights_sent(self, s, p):
        for mask in range(1, self.dp_count):
            held = mask & (mask - 1)
            self.weight_copy(s, p, held, low_bit(mask)).wait_send()

        @pl.when(self.section == s)
        def _():
            self.weight_across(s, p).wait_send()


    def grad_slot(self, s, p, mask):
        return self.grads.at[s, p // QUARTERS, self.piece_rows(p, mask)]

    def grad_landed(self, s, p, mask):
        at = mask * self.part + (p % QUARTERS) * self.quarter
        rows = pl.ds(pl.multiple_of(at, self.quarter), self.quarter)
        return self.landed.at[s, p // QUARTERS, rows]

    def grad_copy(self, s, p, mask):
        device = self.neighbour(low_bit(mask)) if mask else self.across()
        return self.remote(
            self.grad_slot(s, p, mask),
            self.grad_landed(s, p, mask),
            self.grad_send.at[s, p, mask],
            self.grad_recv.at[s, p, mask],
            device,
        )

    def grad_total(self, s, p, mask, last=False):
        total = self.grad_slot(s, p, mask)[...].astype(F32)
        for bit in range(low_bit(mask) if mask else self.bits):
            self.grad_copy(s, p, mask | (1 << bit)).wait_recv()
            total = total + self.grad_landed(s, p, mask | (1 << bit))[...].astype(F32)
        return total

    def grads_offer(self, s, p):
        for mask in range(1, self.dp_count, 2):
            self.grad_copy(s, p, mask).start()

    def grads_fold(self, s, p):
        for bit in range(1, self.bits):
            for mask in range(self.dp_count):
                if mask and low_bit(mask) == bit:
                    self.grad_slot(s, p, mask)[...] = self.grad_total(s, p, mask).astype(BF16)
                    self.grad_copy(s, p, mask).start()

    def grads_cross(self, s, p):
        @pl.when(self.section != s)
        def _():
            self.grad_slot(s, p, 0)[...] = self.grad_total(s, p, 0).astype(BF16)
            self.grad_copy(s, p, 0).start()

    def grads_end(self, s, p):
        @pl.when(self.section == s)
        def _():
            total = self.grad_total(s, p, 0)
            self.grad_copy(s, p, 0).wait_recv()
            total = total + self.grad_landed(s, p, 0)[...].astype(F32)
            rows = span(p % QUARTERS, self.quarter)
            slab = p // QUARTERS

            @pl.when(slab == 0)
            def _():
                for which in range(3):
                    at = slice(which * self.width, (which + 1) * self.width)
                    self.qkv_sums[which, rows] = total[:, at]
                self.out_turned[rows] = total[:, 3 * self.width :]

            @pl.when(slab == 1)
            def _():
                self.up_sums[rows] = total

            @pl.when(slab == 2)
            def _():
                self.down_turned[rows] = total

    def grads_sent(self, s, p):
        for mask in range(1, self.dp_count):
            self.grad_copy(s, p, mask).wait_send()

        @pl.when(self.section != s)
        def _():
            self.grad_copy(s, p, 0).wait_send()


    def line_copy(self, half, side, chunk, target):
        rows = span(chunk, CHUNK)
        return self.remote(
            self.staged.at[side, rows],
            self.sums.at[half, side, rows],
            self.line_send.at[side, chunk],
            self.line_recv.at[half, side, chunk],
            {"tensor": target},
        )

    def line_sum(self, finish, tick):
        number = self.passes
        half = number % 2
        self.passes += 1
        near_target = self.me + 1 - 2 * self.nears
        far_target = self.me - 1 + 2 * self.nears

        def send(side, chunk, target):
            rows = span(chunk, CHUNK)
            if number > 0:
                self.line_copy(half, side, chunk, target).wait_send()
            total = self.partial[rows] + self.sums[half, side, rows].astype(F32)
            self.staged[side, rows] = total.astype(BF16)
            self.line_copy(half, side, chunk, target).start()

        def near(chunk):
            @pl.when(self.middle)
            def _():
                self.line_copy(half, self.nears, chunk, near_target).wait_recv()

            send(self.nears, chunk, near_target)

        ahead = jnp.where(self.middle, AHEAD, self.chunks)
        loop(ahead, near)

        def body(chunk):
            @pl.when(chunk + ahead < self.chunks)
            def _():
                near(chunk + ahead)

            self.line_copy(half, self.fars, chunk, near_target).wait_recv()

            @pl.when(self.middle)
            def _():
                send(self.fars, chunk, far_target)

            rows = span(chunk, CHUNK)
            total = (
                self.partial[rows]
                + self.sums[half, 0, rows].astype(F32)
                + self.sums[half, 1, rows].astype(F32)
            )
            finish(rows, total)
            tick(chunk)

        loop(self.chunks, body)

    def line_sent(self):
        def one(chunk):
            self.line_copy(0, self.nears, chunk, self.me + 1 - 2 * self.nears).wait_send()

            @pl.when(self.middle)
            def _():
                self.line_copy(0, self.fars, chunk, self.me - 1 + 2 * self.nears).wait_send()

        loop(self.chunks, one)

    def clear(self):
        for half in range(2):
            for side, end in ((0, 0), (1, self.line - 1)):

                @pl.when(self.me == end)
                def _():
                    self.sums[half, side] = jnp.zeros(self.sums.shape[2:], BF16)

        self.stats[...] = jnp.zeros(self.stats.shape, F32)
        row = jnp.broadcast_to(self.ids[self.section], (self.tokens, self.tokens))
        self.hidden_pairs[...] = jnp.where(row == row.T, 0.0, -1e30)


    def param(self, s, row):
        return self.params[s, row : row + 1]

    def count_stat(self, s, row, values):
        folded = values.reshape(values.shape[0] // 8, 8, values.shape[1])
        self.stats[s, row] += jnp.sum(folded, axis=0)

    def attention(self, s):
        width = self.width
        for block in range(3):
            at = slice(block * width, (block + 1) * width)
            made = nn(self.inputs[s], self.weights[s, 0, :, at])
            if block != 1:
                low = 0 if block == 0 else width
                made = made + self.params[s, 6:7, low : low + width]
            self.qkv[s, :, at] = made.astype(BF16)
        contexts = []
        for head in range(self.heads):
            query, key, value = self.head_parts(s, head)
            scores = nt(query, key) * self.head_size ** (-0.5) + self.hidden_pairs[...]
            shifted = jnp.exp(scores - jnp.max(scores, axis=-1, keepdims=True))
            prob = shifted / jnp.sum(shifted, axis=-1, keepdims=True)
            prob = prob.astype(BF16)
            self.probs[s, head] = prob
            contexts.append(nn(prob, value).astype(BF16))
        self.context[s] = jnp.concatenate(contexts, axis=1)

        def project(block):
            at = span(block, BLOCK)
            self.partial[:, at] = nt(self.context[s], self.weights[s, 0, at, 3 * width :])

        loop(self.model // BLOCK, project)

    def head_parts(self, s, head):
        size = self.head_size
        low = head * size
        return [
            self.qkv[s, :, which * self.width + low : which * self.width + low + size]
            for which in range(3)
        ]

    def feed_up(self, s):
        def block_of(block):
            at = span(block, BLOCK)
            self.partial[:, at] = nn(self.hidden[s], self.weights[s, 1, :, at])

        loop(self.units // BLOCK, block_of)

        def gelu(step):
            rows = span(step, 16)
            pre = self.partial[rows] + self.param(s, 7)
            half = 0.5 * (1.0 + erf(pre * 0.7071067811865476))
            self.active[s, rows] = (pre * half).astype(BF16)
            bell = pre * jnp.exp(-0.5 * pre * pre) * 0.3989422804014327
            self.slope[s, rows] = (half + bell).astype(BF16)

        loop(self.tokens // 16, gelu)

    def feed_down(self, s):
        def block_of(block):
            at = span(block, BLOCK)
            self.partial[:, at] = nt(self.active[s], self.weights[s, 2, at])

        loop(self.model // BLOCK, block_of)

    def after_attention(self, s):
        def finish(rows, total):
            summed = self.inputs[s, rows].astype(F32) + total + self.param(s, 0)
            normed, scaled = normalize(summed)
            self.normed_one[s, rows] = normed.astype(BF16)
            self.scaled_one[s, rows] = jnp.broadcast_to(scaled, (CHUNK, 128))
            hidden = normed * self.param(s, 1) + self.param(s, 2)
            self.wide[rows] = hidden
            self.hidden[s, rows] = hidden.astype(BF16)

        return finish

    def after_feed(self, s):
        def finish(rows, total):
            summed = self.wide[rows] + total + self.param(s, 3)
            normed, scaled = normalize(summed)
            out = normed * self.param(s, 4) + self.param(s, 5)
            self.inputs[s + 1, rows] = out.astype(BF16)
            if s == 0:
                self.normed_two[rows] = normed.astype(BF16)
                self.scaled_two[rows] = jnp.broadcast_to(scaled, (CHUNK, 128))
            else:
                self.start_back(s, rows, self.grad_one_held[rows].astype(F32), normed, scaled)

        return finish

    def start_back(self, s, rows, upstream, normed, scaled):
        grad_two = norm_back(upstream * self.param(s, 4), normed, scaled)
        self.wide[rows] = grad_two
        self.grad_two_held[rows] = grad_two.astype(BF16)
        self.count_stat(s, 3, grad_two)
        self.count_stat(s, 4, upstream * normed)
        self.count_stat(s, 5, upstream)

    def feed_back(self, s):
        def block_of(block):
            at = span(block, BLOCK)
            self.partial[:, at] = nn(self.grad_two_held[...], self.weights[s, 2, :, at])

        loop(self.units // BLOCK, block_of)

        def slopes(step):
            rows = span(step, 16)
            grad_pre = self.partial[rows] * self.slope[s, rows].astype(F32)
            self.grad_pre[rows] = grad_pre.astype(BF16)
            self.count_stat(s, 7, grad_pre)

        loop(self.tokens // 16, slopes)

        def up_of(block):
            at = span(block, BLOCK)
            self.partial[:, at] = nt(self.grad_pre[...], self.weights[s, 1, at])

        loop(self.model // BLOCK, up_of)

    def after_feed_back(self, s):
        def finish(rows, total):
            grad_hidden = self.wide[rows] + total
            normed = self.normed_one[s, rows].astype(F32)
            scaled = self.scaled_one[s, rows][:, :1]
            grad_one = norm_back(grad_hidden * self.param(s, 1), normed, scaled)
            self.grad_wide[rows] = grad_one
            self.grad_one_held[rows] = grad_one.astype(BF16)
            self.count_stat(s, 0, grad_one)
            self.count_stat(s, 1, grad_hidden * normed)
            self.count_stat(s, 2, grad_hidden)

        return finish

    def feed_grads(self, s, step):
        cuts = self.chunks // 2
        block = step // 2
        size = self.model // cuts
        at = span(block, size)

        @pl.when(step % 2 == 0)
        def _():
            made = tn(self.grad_two_held[:, at], self.active[s])
            self.grads[s, 2, at] = made.astype(BF16)

        @pl.when(step % 2 == 1)
        def _():
            made = tn(self.hidden[s, :, at], self.grad_pre[...])
            self.grads[s, 1, at] = made.astype(BF16)

    def attention_grads(self, s, step):
        cuts = self.chunks // 2
        block = step // 2
        size = self.model // cuts
        at = span(block, size)

        @pl.when(step % 2 == 0)
        def _():
            made = tn(self.inputs[s, :, at], self.grad_qkv[...])
            self.grads[s, 0, at, : 3 * self.width] = made.astype(BF16)

        @pl.when(step % 2 == 1)
        def _():
            made = tn(self.grad_one_held[:, at], self.context[s])
            self.grads[s, 0, at, 3 * self.width :] = made.astype(BF16)

    def attention_back(self, s):
        width, size = self.width, self.head_size
        grad_context = nn(self.grad_one_held[...], self.weights[s, 0, :, 3 * width :])
        self.grad_context[...] = grad_context.astype(BF16)
        parts = [[], [], []]
        for head in range(self.heads):
            query, key, value = self.head_parts(s, head)
            above = self.grad_context[:, head * size : (head + 1) * size]
            held = self.probs[s, head]
            prob = held.astype(F32)
            grad_prob = nt(above, value)
            dots = jnp.sum(prob * grad_prob, axis=-1, keepdims=True)
            grad_scores = (prob * (grad_prob - dots) * size ** (-0.5)).astype(BF16)
            parts[0].append(nn(grad_scores, key))
            parts[1].append(tn(grad_scores, query))
            parts[2].append(tn(held, above))
        for which in range(3):
            made = jnp.concatenate(parts[which], axis=1)
            self.grad_qkv[:, which * width : (which + 1) * width] = made.astype(BF16)
            if which != 1:
                folded = jnp.sum(made.reshape(self.tokens // 8, 8, width), axis=0)
                low = 0 if which == 0 else width
                self.stats[s, 6, :, low : low + width] = folded

        def block_of(block):
            at = span(block, BLOCK)
            self.partial[:, at] = nt(self.grad_qkv[...], self.weights[s, 0, at, : 3 * width])

        loop(self.model // BLOCK, block_of)

    def after_attention_back(self, s):
        def finish(rows, total):
            upstream = self.grad_wide[rows] + total
            self.grad_wide[rows] = upstream
            if s == 1:
                normed = self.normed_two[rows].astype(F32)
                self.start_back(0, rows, upstream, normed, self.scaled_two[rows][:, :1])

        return finish


    def output_copy(self, s, local):
        source = self.inputs.at[s + 1, self.own_rows]
        target = self.outputs.at[self.section]
        if local:
            return pltpu.make_async_copy(source, target, self.out_sem.at[0])
        return self.remote(source, target, self.out_sem.at[1], self.out_sem.at[2], self.across())

    def output_start(self, s):
        for local in (True, False):

            @pl.when((self.section == s) if local else (self.section != s))
            def _():
                self.output_copy(s, local).start()

    def input_grad_copy(self):
        return self.remote(
            self.input_grad_staged,
            self.input_grad_landed,
            self.out_sem.at[3],
            self.out_sem.at[4],
            self.across(),
        )

    def input_grad_start(self, s):
        @pl.when(self.section == s)
        def _():
            self.input_grads[self.section] = self.grad_wide[self.own_rows]

        @pl.when(self.section != s)
        def _():
            self.input_grad_staged[...] = self.grad_wide[self.own_rows].astype(BF16)
            self.input_grad_copy().start()

    def outputs_end(self):
        self.output_copy(0, True).wait()
        self.output_copy(0, False).wait()
        self.input_grad_copy().wait()
        self.input_grads[1 - self.section] = self.input_grad_landed[...].astype(F32)


    def stat_copy(self, step):
        return self.remote(
            self.stat_sums.at[step],
            self.stat_landed.at[step],
            self.stat_sem.at[0, step],
            self.stat_sem.at[1, step],
            self.neighbour(step) if step < self.bits else self.across(),
        )

    def stat_step(self, step):
        self.stat_copy(step).wait_recv()
        self.stat_sums[step + 1] = self.stat_sums[step] + self.stat_landed[step]
        if step < self.bits:
            self.stat_copy(step + 1).start()


    def spread_small(self):
        model, dp_count = self.model, self.dp_count
        place = lax.broadcasted_iota(jnp.int32, (1, model), 1) // self.part
        rows = []
        for ref in self.vectors:
            tiled = jnp.concatenate([ref[...].astype(F32)] * dp_count, axis=1)
            rows.append(jnp.where(place == self.dp, tiled, 0.0))

        def spread(values):
            size = values.shape[1]
            shape = (size, size * dp_count)
            low = lax.broadcasted_iota(jnp.int32, shape, 0) + self.dp * size
            chosen = jnp.where(lax.broadcasted_iota(jnp.int32, shape, 1) == low, 1.0, 0.0)
            return nn(values.astype(BF16), chosen.astype(BF16))

        query, value = spread(self.qv_bias[0]), spread(self.qv_bias[1])
        pieces = [query[head : head + 1] for head in range(self.heads)]
        pieces += [value[head : head + 1] for head in range(self.heads)]
        pieces.append(jnp.zeros((1, model - 2 * self.width), F32))
        rows.append(jnp.concatenate(pieces, axis=1))
        above = spread(self.up_bias[...])
        rows.append(
            jnp.concatenate([above[group : group + 1] for group in range(above.shape[0])], axis=1)
        )
        self.small_all[self.section, self.dp] = jnp.concatenate(rows, axis=0)

    def small_outputs(self):
        total = self.stat_sums[self.bits + 1, self.section]
        model = self.model

        def turned(offset):
            return pltpu.roll(total, lax.rem(model - offset, model), 1)

        share = self.part // self.line
        self.row_sums[...] = turned(self.dp * self.part + self.me * share)[:6, :share]
        size = self.head_size // self.dp_count
        moved = turned(self.dp * size)
        for which in range(2):
            for head in range(self.heads):
                low = which * self.width + head * self.head_size
                self.qv_sums[which, head : head + 1] = moved[6:7, low : low + size]
        groups, size = self.shift_sums.shape
        moved = turned(self.dp * size)
        for group in range(groups):
            low = group * size * self.dp_count
            self.shift_sums[group : group + 1] = moved[7:8, low : low + size]

    def own_copies(self):
        mine = pl.ds(pl.multiple_of(self.dp * self.part, self.part), self.part)
        here = self.weights.at[self.section]
        pairs = [
            (self.qkv_own, here.at[0, mine, pl.ds(0, 3 * self.width)]),
            (self.out_own, self.out_raw),
            (self.up_own, here.at[1, mine]),
            (self.down_own, self.down_raw),
        ]
        return [
            pltpu.make_async_copy(source, target, self.own_sem.at[number])
            for number, (source, target) in enumerate(pairs)
        ]

    def run(self):
        def nothing(step):
            pass

        copies = self.own_copies()
        for copy in copies:
            copy.start()
        self.greet()
        self.rows_start(0, self.block_rows, self.inputs.at[0])
        mine = pl.ds(pl.multiple_of(self.dp * self.part, self.part), self.part)
        copies[0].wait()
        copies[1].wait()
        self.weights[self.section, 0, mine, 3 * self.width :] = self.out_raw[...].T
        loop(QUARTERS, self.weights_offer)
        self.spread_small()
        self.weights_offer(None)
        copies[2].wait()
        copies[3].wait()
        self.weights[self.section, 2, mine] = self.down_raw[...].T
        loop(PIECES - QUARTERS, lambda p: self.weights_offer(QUARTERS + p))
        self.clear()
        for p in range(QUARTERS + 1):
            if p < QUARTERS:
                self.weights_cross(0, p)
            if p == 1:
                self.weights_cross(0, None)
            if p == 2:
                self.weights_relay(0, None)
            if p > 0:
                self.weights_relay(0, p - 1)
        self.weights_land(0, None)
        loop(QUARTERS, functools.partial(self.weights_land, 0))
        self.params[0] = jnp.sum(self.small_all[0], axis=0)
        self.rows_wait(0, self.block_rows, self.inputs.at[0])
        self.rows_start(1, self.upstream_rows, self.grad_one_held)

        self.attention(0)

        def first_tick(step):
            self.weights_cross(0, QUARTERS + step)

            @pl.when(step > 0)
            def _():
                self.weights_relay(0, QUARTERS + step - 1)

        self.line_sum(self.after_attention(0), first_tick)
        self.weights_relay(0, PIECES - 1)
        self.weights_offer_late(None)
        loop(PIECES, self.weights_offer_late)
        loop(QUARTERS, lambda p: self.weights_land(0, QUARTERS + p))
        self.feed_up(0)
        loop(QUARTERS, lambda p: self.weights_land(0, 2 * QUARTERS + p))
        self.feed_down(0)

        self.weights_cross(1, None)
        loop(PIECES, functools.partial(self.weights_cross, 1))

        def second_tick(step):
            @pl.when(step == 1)
            def _():
                self.weights_relay(1, None)

            @pl.when(step > 0)
            def _():
                self.weights_relay(1, step - 1)

        self.line_sum(self.after_feed(0), second_tick)
        self.output_start(0)
        self.weights_land(1, None)
        loop(QUARTERS, functools.partial(self.weights_land, 1))
        self.params[1] = jnp.sum(self.small_all[1], axis=0)

        self.attention(1)

        def third_tick(step):
            @pl.when(step <= QUARTERS)
            def _():
                self.weights_relay(1, 2 * QUARTERS + step - 1)

        self.line_sum(self.after_attention(1), third_tick)
        loop(QUARTERS, lambda p: self.weights_land(1, QUARTERS + p))
        self.feed_up(1)
        loop(QUARTERS, lambda p: self.weights_land(1, 2 * QUARTERS + p))
        self.feed_down(1)
        self.rows_wait(1, self.upstream_rows, self.grad_one_held)
        self.line_sum(self.after_feed(1), nothing)
        self.output_start(1)

        def turn(order):
            return (SLABS - 1 - order // QUARTERS) * QUARTERS + order % QUARTERS

        def service(s, action, order):
            @pl.when(jnp.logical_and(order >= 0, order < PIECES))
            def _():
                action(s, turn(order))

        self.feed_back(1)
        self.line_sum(self.after_feed_back(1), functools.partial(self.feed_grads, 1))
        loop(2 * QUARTERS, lambda order: self.grads_offer(1, turn(order)))
        self.attention_back(1)

        def fourth_tick(step):
            self.attention_grads(1, step)
            service(1, self.grads_fold, step)
            service(1, self.grads_cross, step - 2)
            service(1, self.grads_end, step - 4)

        self.line_sum(self.after_attention_back(1), fourth_tick)
        loop(QUARTERS, lambda q: self.grads_offer(1, q))
        self.input_grad_start(1)
        self.feed_back(0)

        def fifth_tick(step):
            self.feed_grads(0, step)
            service(1, self.grads_fold, step + 8)
            service(1, self.grads_cross, step + 6)
            service(1, self.grads_end, step + 4)

        self.line_sum(self.after_feed_back(0), fifth_tick)
        loop(2 * QUARTERS, lambda order: self.grads_offer(0, turn(order)))
        self.attention_back(0)
        self.stat_sums[0] = jnp.sum(self.stats[...], axis=2)
        self.stat_copy(0).start()

        def sixth_tick(step):
            self.attention_grads(0, step)
            for number in range(self.bits + 1):

                @pl.when(step == min(2 * number + 2, self.chunks - 1))
                def _():
                    self.stat_step(number)

            service(0, self.grads_fold, step)
            service(0, self.grads_cross, step - 2)
            service(0, self.grads_end, step - 4)

        self.line_sum(self.after_attention_back(0), sixth_tick)
        loop(QUARTERS, lambda q: self.grads_offer(0, q))
        self.input_grad_start(0)

        self.small_outputs()
        self.down_sums[...] = self.down_turned[...].T

        def last_tick(step):
            service(0, self.grads_fold, step + 8)
            service(0, self.grads_cross, step + 6)
            service(0, self.grads_end, step + 4)

        loop(8, last_tick)
        self.out_sums[...] = self.out_turned[...].T
        self.outputs_end()

        for which, source, target in (
            (0, self.block_rows, self.inputs.at[0]),
            (1, self.upstream_rows, self.grad_one_held),
        ):
            for step in range(1, self.line):
                self.rows_copy(which, source, target, step).wait_send()
        self.line_sent()
        for s in range(2):
            self.weights_sent(s, None)
            loop(PIECES, functools.partial(self.weights_sent, s))
            loop(PIECES, functools.partial(self.grads_sent, s))
        for step in range(self.bits + 1):
            self.stat_copy(step).wait_send()


def layers_kernel(sizes, *refs):
    Layers(sizes, refs).run()


def both_layers(arrays, sizes):
    line, dp_count, part = sizes["line"], sizes["dp_count"], sizes["part"]
    rows, width, model, units = sizes["rows"], sizes["width"], sizes["model"], sizes["units"]
    heads = sizes["heads"]
    tokens = line * rows
    chunks = tokens // CHUNK
    bits = dp_count.bit_length() - 1
    dma = pltpu.SemaphoreType.DMA
    vmem = pltpu.VMEM
    scratch = dict(
        inputs=vmem((3, tokens, model), BF16),
        weights=vmem((2, SLABS, model, units), BF16),
        grads=vmem((2, SLABS, model, units), BF16),
        landed=vmem((2, SLABS, model, units), BF16),
        small_all=vmem((2, dp_count, STATS, model), F32),
        params=vmem((2, STATS, model), F32),
        sums=vmem((2, 2, tokens, model), BF16),
        staged=vmem((2, tokens, model), BF16),
        partial=vmem((tokens, model), F32),
        wide=vmem((tokens, model), F32),
        grad_wide=vmem((tokens, model), F32),
        normed_one=vmem((2, tokens, model), BF16),
        normed_two=vmem((tokens, model), BF16),
        scaled_one=vmem((2, tokens, 128), F32),
        scaled_two=vmem((tokens, 128), F32),
        hidden=vmem((2, tokens, model), BF16),
        active=vmem((2, tokens, units), BF16),
        slope=vmem((2, tokens, units), BF16),
        qkv=vmem((2, tokens, 3 * width), BF16),
        probs=vmem((2, heads, tokens, tokens), BF16),
        context=vmem((2, tokens, width), BF16),
        grad_two_held=vmem((tokens, model), BF16),
        grad_one_held=vmem((tokens, model), BF16),
        grad_pre=vmem((tokens, units), BF16),
        grad_context=vmem((tokens, width), BF16),
        grad_qkv=vmem((tokens, 3 * width), BF16),
        hidden_pairs=vmem((tokens, tokens), F32),
        stats=vmem((2, STATS, 8, model), F32),
        stat_sums=vmem((bits + 2, 2, STATS, model), F32),
        stat_landed=vmem((bits + 1, 2, STATS, model), F32),
        input_grad_staged=vmem((rows, model), BF16),
        input_grad_landed=vmem((rows, model), BF16),
        out_raw=vmem((width, part), BF16),
        down_raw=vmem((units, part), BF16),
        out_turned=vmem((part, width), F32),
        down_turned=vmem((part, units), F32),
        rows_send=dma((2, line - 1)),
        rows_recv=dma((2, line - 1)),
        rows_own=dma((2,)),
        own_sem=dma((4,)),
        weight_send=dma((2, PIECES + 1, dp_count)),
        weight_recv=dma((2, PIECES + 1, dp_count)),
        grad_send=dma((2, PIECES, dp_count)),
        grad_recv=dma((2, PIECES, dp_count)),
        line_send=dma((2, chunks)),
        line_recv=dma((2, 2, chunks)),
        out_sem=dma((5,)),
        stat_sem=dma((2, bits + 1)),
    )
    outs = dict(
        outputs=((2, rows, model), BF16),
        input_grads=((2, rows, model), F32),
        qkv_sums=((3, part, width), F32),
        out_sums=((width, part), F32),
        up_sums=((part, units), F32),
        down_sums=((units, part), F32),
        row_sums=((6, part // line), F32),
        qv_sums=((2, heads, sizes["head_size"] // dp_count), F32),
        shift_sums=(arrays["up_bias"].shape, F32),
    )
    far = ("block_rows", "upstream_rows", "qkv_own", "out_own", "up_own", "down_own")
    names = list(arrays) + list(outs) + list(scratch)
    return pl.pallas_call(
        functools.partial(layers_kernel, dict(sizes, names=names)),
        out_shape=[jax.ShapeDtypeStruct(shape, kind) for shape, kind in outs.values()],
        in_specs=[ANY_SPEC if name in far else VMEM_SPEC for name in arrays],
        out_specs=[VMEM_SPEC] * len(outs),
        scratch_shapes=list(scratch.values()),
        compiler_params=pltpu.CompilerParams(
            collective_id=1, has_side_effects=True, vmem_limit_bytes=VMEM_LIMIT
        ),
        name="both_layers",
    )(*arrays.values())


def shards(
    block_input,
    seq_ids,
    out_cotangent,
    qkv_weight,
    qv_bias,
    out_weight,
    out_bias,
    norm1_gain,
    norm1_bias,
    up_weight,
    up_bias,
    down_weight,
    down_bias,
    norm2_gain,
    norm2_bias,
):
    dp_count = lax.axis_size("dp")
    line = lax.axis_size("tensor")
    heads, head_part = qv_bias.shape[2], qv_bias.shape[3]
    part = out_bias.shape[1]
    width = qkv_weight.shape[3]
    model = block_input.shape[3]
    units = up_weight.shape[2]
    sizes = dict(
        line=line,
        dp_count=dp_count,
        part=part,
        width=width,
        rows=block_input.shape[2],
        model=model,
        units=units,
        heads=heads,
        head_size=head_part * dp_count,
    )
    arrays = dict(
        block_rows=block_input[:, 0],
        upstream_rows=out_cotangent[:, 0],
        ids=seq_ids,
        qkv_own=qkv_weight[0].reshape(part, 3 * width),
        out_own=out_weight[0],
        up_own=up_weight[0],
        down_own=down_weight[0],
        out_bias=out_bias,
        gain_one=norm1_gain,
        bias_one=norm1_bias,
        down_bias=down_bias,
        gain_two=norm2_gain,
        bias_two=norm2_bias,
        qv_bias=qv_bias[0],
        up_bias=up_bias[0],
    )
    results = both_layers(arrays, sizes)
    outputs, input_grads, qkv_sums, out_sums, up_sums, down_sums, rows, qv_sums, shift_sums = results
    return (
        outputs[None, :, None],
        input_grads[None, :, None],
        jnp.swapaxes(qkv_sums, 0, 1)[None],
        qv_sums[None],
        out_sums[None],
        rows[0][None],
        rows[1][None],
        rows[2][None],
        up_sums[None],
        shift_sums[None],
        down_sums[None],
        rows[3][None],
        rows[4][None],
        rows[5][None],
    )


def solution(mesh):
    return jax.shard_map(
        shards,
        mesh=mesh,
        in_specs=(
            P(None, "dp", "tensor", None),
            P(None, "dp", None),
            P(None, "dp", "tensor", None),
            P("section", "dp", None, "tensor"),
            P("section", None, "tensor", "dp"),
            P("section", "tensor", "dp"),
            P("section", "dp"),
            P("section", "dp"),
            P("section", "dp"),
            P("section", "dp", "tensor"),
            P("section", "tensor", "dp"),
            P("section", "tensor", "dp"),
            P("section", "dp"),
            P("section", "dp"),
            P("section", "dp"),
        ),
        out_specs=(
            P("section", None, "dp", "tensor", None),
            P("section", None, "dp", "tensor", None),
            P("section", "dp", None, "tensor"),
            P("section", None, "tensor", "dp"),
            P("section", "tensor", "dp"),
            P("section", ("dp", "tensor")),
            P("section", ("dp", "tensor")),
            P("section", ("dp", "tensor")),
            P("section", "dp", "tensor"),
            P("section", "tensor", "dp"),
            P("section", "tensor", "dp"),
            P("section", ("dp", "tensor")),
            P("section", ("dp", "tensor")),
            P("section", ("dp", "tensor")),
        ),
        check_vma=False,
    )
```
